256 devices in a mesh: dp: 16 (over z, core), fsdp: 16 (over y, x).
Axes of the slice: x: 4, y: 4, z: 8, core: 2. Of those that a mesh axis runs over, the one named last changes fastest.
Arguments:
- features: bfloat16 [16, 16, 32, 32, 512], P('fsdp', None, 'dp'), may hold values from -6 to 6
- conv_weight: bfloat16 [3, 3, 512, 8], replicated, may hold values from -0.046875 to 0.046875
- vae_noise: float32 [16, 16, 4096], P('dp', 'fsdp'), may hold values from -6 to 6
- flips: int32 [16, 16, 4], P('dp', 'fsdp'), may hold values from 0 to 1
- crops: int32 [16, 16, 4, 2], P('dp', 'fsdp'), may hold values from 0 to 4
- tsteps: int32 [16, 16, 4], P('dp', 'fsdp'), may hold values from 0 to 999
- diffusion_noise: float32 [16, 16, 4, 4096], P('dp', 'fsdp'), may hold values from -6 to 6
- selected: int32 [16, 16], P('dp', 'fsdp'), may hold values from 0 to 1, as said below
- w_patch: bfloat16 [16, 384], replicated, may hold values from -1.5 to 1.5
- w_time: bfloat16 [256, 384], replicated, may hold values from -0.375 to 0.375
- w_ada: bfloat16 [384, 1152], replicated, may hold values from -0.3125 to 0.3125
- w_fc1: bfloat16 [384, 1536], P(None, 'fsdp'), may hold values from -1 to 1
- w_fc2: bfloat16 [384, 1536], P(None, 'fsdp'), may hold values from -1 to 1
- w_final: bfloat16 [384, 16], replicated, may hold values from -0.3125 to 0.3125
- noise_fc1: float32 [384, 1536], P(None, 'fsdp'), may hold values from -6 to 6
- noise_fc2: float32 [384, 1536], P(None, 'fsdp'), may hold values from -6 to 6
Outputs:
- update_fc1: float32 [384, 1536], P(None, 'fsdp')
- update_fc2: float32 [384, 1536], P(None, 'fsdp')
- mean_loss: float32 [], replicated
- latent_moments: float32 [16, 16, 8192], P('dp', 'fsdp')
The draws below stay inside these ranges and needn't reach their ends.
Inputs may be any that keep to these rules, and one draw needn't show every extreme that they name: `selected`: exactly 128 slots are 1.
All inputs are finite; a program needn't handle non-finite values.
Results may differ from the reference program's by a relative error of at most 0.00091.
Values may be sent and summed in bfloat16 or wider, within the bound.
A program may use at most 64 MiB of HBM per device.

```python
import math
from functools import partial
import jax
import jax.numpy as jnp
from jax import lax

D = 384
FF = 1536
FCH = 512
FREQ = 256
LAT = 32
LC = 4
AUG = 4
TSTEPS = 1000
SLOTS = 16
SELECTED = 128
N_FSDP = 16


def scaled_columns(key, row_count, col_count, fan_in):
    base_values = jnp.clip(jax.random.normal(key, (row_count, col_count), jnp.float32), -6.0, 6.0)
    spread = jnp.exp(jax.random.uniform(jax.random.fold_in(key, 7), (col_count,), jnp.float32, -1.15, 1.15))
    return jnp.clip(base_values * spread[None, :] / math.sqrt(fan_in), -1.0, 1.0)


def draw_w_fc1(key, part):
    return scaled_columns(key, D, FF, D).astype(jnp.bfloat16)


def draw_w_fc2(key, part):
    return scaled_columns(key, D, FF, FF).astype(jnp.bfloat16)


def draw_diffusion_noise(key, part):
    full_shape = (SLOTS, N_FSDP, AUG, LAT * LAT * LC)
    return jnp.clip(jax.random.normal(key, full_shape, jnp.float32), -6.0, 6.0)


def draw_selected(key, part):
    shuffled = jax.random.permutation(key, SLOTS * N_FSDP)
    return (shuffled < SELECTED).astype(jnp.int32).reshape(SLOTS, N_FSDP)


def set_ends(drawn, stream_key, low, top_value):
    longest = drawn.shape.index(max(drawn.shape))
    spots = []
    for shift in (0, 1):
        where = [jax.random.randint(jax.random.fold_in(stream_key, axis), (), 0, length) for axis, length in enumerate(drawn.shape)]
        where[longest] = (where[longest] + shift) % drawn.shape[longest]
        spots.append(tuple(where))
    return drawn.at[spots[0]].set(low).at[spots[1]].set(top_value)


def steps_of(own_key, shape, cuts, least, largest):
    def one(position, blocks):
        draws = jax.random.uniform(jax.random.fold_in(jax.random.fold_in(own_key, 6), position), (blocks,), jnp.float32, least / len(cuts), largest / len(cuts))
        return jnp.repeat(jnp.exp(draws), shape[position] // blocks).reshape((-1,) + (1,) * (len(shape) - position - 1))

    loudness = one(*cuts[0])
    for cut in cuts[1:]:
        loudness = loudness * one(*cut)
    return loudness


def scatter_about(key, dims, deviation, reach, cuts=(), kind=jnp.bfloat16):
    array = jax.random.normal(key, dims, jnp.float32) * deviation
    if len(cuts) > 0:
        array = steps_of(key, dims, cuts, -0.22, 0.18) * array
    return jnp.clip(array, min=-reach, max=reach).astype(kind)


def setup_inputs(seed: int = 0) -> dict:
    keys = jax.random.split(jax.random.key(seed), 17)
    features = scatter_about(keys[0], (N_FSDP, SLOTS, LAT, LAT, FCH), 1.0, 6.0, ((0, 16), (2, 16)))
    conv_weight = scatter_about(keys[1], (3, 3, FCH, 2 * LC), (36 * FCH) ** -0.5, 0.046875)
    vae_noise = scatter_about(keys[2], (SLOTS, N_FSDP, LAT * LAT * LC), 1.0, 6.0, ((0, 16), (1, 16)), jnp.float32)
    flips = set_ends(jax.random.randint(keys[3], (SLOTS, N_FSDP, AUG), 0, 2), jax.random.fold_in(keys[3], 1), 0, 1).astype(jnp.int32)
    crops = set_ends(jax.random.randint(keys[4], (SLOTS, N_FSDP, AUG, 2), 0, 5), jax.random.fold_in(keys[4], 1), 0, 4).astype(jnp.int32)
    tsteps = set_ends(jax.random.randint(keys[5], (SLOTS, N_FSDP, AUG), 0, TSTEPS), jax.random.fold_in(keys[5], 1), 0, TSTEPS - 1).astype(jnp.int32)
    diffusion_noise = draw_diffusion_noise(jax.random.fold_in(keys[16], 71), 0)
    selected = draw_selected(jax.random.fold_in(keys[16], 71), 0)
    w_patch = scatter_about(keys[8], (4 * LC, D), (4 * LC) ** -0.5, 1.5)
    w_time = scatter_about(keys[9], (FREQ, D), FREQ ** -0.5, 0.375)
    w_ada = scatter_about(keys[10], (D, 3 * D), D ** -0.5, 0.3125)
    w_fc1 = draw_w_fc1(jax.random.fold_in(keys[16], 71), 0)
    w_fc2 = draw_w_fc2(jax.random.fold_in(keys[16], 71), 0)
    w_final = scatter_about(keys[13], (D, 4 * LC), D ** -0.5, 0.3125)
    noise_fc1 = scatter_about(keys[14], (D, FF), 1.0, 6.0, ((1, 16),), jnp.float32)
    noise_fc2 = scatter_about(keys[15], (D, FF), 1.0, 6.0, ((1, 16),), jnp.float32)
    return dict(features=features, conv_weight=conv_weight, vae_noise=vae_noise, flips=flips, crops=crops, tsteps=tsteps, diffusion_noise=diffusion_noise, selected=selected, w_patch=w_patch, w_time=w_time, w_ada=w_ada, w_fc1=w_fc1, w_fc2=w_fc2, w_final=w_final, noise_fc1=noise_fc1, noise_fc2=noise_fc2)


clip_offset = 1e-05
noise_weight = 16.0
norm_epsilon = 1e-06

def layer_norm(values):
    center = values - lax.optimization_barrier(jnp.mean(values, axis=-1, keepdims=True))
    variance = lax.optimization_barrier(jnp.mean(center * center, axis=-1, keepdims=True))
    return center * lax.rsqrt(variance + norm_epsilon)

def position_table(side_cells, width):
    quarter = width // 4
    frequency = 1.0 / 10000.0 ** (jnp.arange(quarter, dtype=jnp.float32) / quarter)
    positions = jnp.arange(side_cells, dtype=jnp.float32)
    angles = positions[:, None] * frequency[None, :]
    line_table = jnp.concatenate([jnp.sin(angles), jnp.cos(angles)], axis=1)
    row_part = jnp.repeat(line_table, side_cells, axis=0)
    col_part = jnp.tile(line_table, (side_cells, 1))
    return jnp.concatenate([row_part, col_part], axis=1)

def time_features(steps_in, width):
    half_width = width // 2
    rates = jnp.exp(-math.log(10000.0) * jnp.arange(half_width, dtype=jnp.float32) / half_width)
    phases = steps_in.astype(jnp.float32)[:, None] * rates[None, :]
    return jnp.concatenate([jnp.cos(phases), jnp.sin(phases)], axis=1)

def alpha_bars(steps_in, horizon):
    beta_table = jnp.linspace(0.0001, 0.02, horizon, dtype=jnp.float32)
    alpha_bar = jnp.cumprod(1.0 - beta_table)
    matches = jnp.arange(horizon, dtype=jnp.int32)[None, :] == steps_in.astype(jnp.int32)[:, None]
    return lax.optimization_barrier(jnp.sum(jnp.where(matches, alpha_bar[None, :], 0.0), axis=1))

def augment(latent, mirror, crop_at):
    side_cells = latent.shape[0]
    mirrored = jnp.where(mirror == 1, latent[:, ::-1, :], latent)
    padded = jnp.pad(mirrored, ((2, 2), (2, 2), (0, 0)))
    starts = (crop_at[0].astype(jnp.int32), crop_at[1].astype(jnp.int32), jnp.int32(0))
    return lax.dynamic_slice(padded, starts, (side_cells, side_cells, latent.shape[2]))

def patchify(grid):
    views_count = grid.shape[0]
    half_side = grid.shape[1] // 2
    channels = grid.shape[3]
    blocks = grid.reshape(views_count, half_side, 2, half_side, 2, channels)
    blocks = blocks.transpose(0, 1, 3, 2, 4, 5)
    return blocks.reshape(views_count * half_side * half_side, 4 * channels)

def conv_moments(padded, kernel):
    image_count, padded_rows, side_cells, channels = padded.shape
    out_width = kernel.shape[3]
    tap_matrix = kernel.transpose(2, 0, 1, 3).reshape(channels, 9 * out_width)
    tap_values = jnp.dot(padded.reshape(-1, channels), tap_matrix, preferred_element_type=jnp.float32)
    tap_values = tap_values.reshape(image_count, padded_rows, side_cells, 3, 3, out_width)
    tap_values = jnp.pad(tap_values, ((0, 0), (0, 0), (1, 1), (0, 0), (0, 0), (0, 0)))
    out_rows = padded_rows - 2
    summed = jnp.zeros((image_count, out_rows, side_cells, out_width), jnp.float32)
    for row_tap in range(3):
        for col_tap in range(3):
            summed = summed + tap_values[:, row_tap:row_tap + out_rows, col_tap:col_tap + side_cells, row_tap, col_tap, :]
    return summed

def example_terms(mean_part, logvar, vae_eps, mirror, crop_at, steps_in, noise, weights):
    w_patch, w_time, w_ada, w_fc1, w_fc2, w_final = weights
    side_cells = mean_part.shape[0]
    channels = mean_part.shape[2]
    views_count = mirror.shape[0]
    width = w_fc1.shape[0]
    latent = mean_part + jnp.exp(0.5 * logvar) * vae_eps.reshape(mean_part.shape)
    augmented = jax.vmap(augment, in_axes=(None, 0, 0))(latent, mirror, crop_at)
    alpha_bar = alpha_bars(steps_in, TSTEPS)
    noise_grid = noise.reshape(views_count, side_cells, side_cells, channels)
    keep_part = jnp.sqrt(alpha_bar)[:, None, None, None]
    blend_part = jnp.sqrt(1.0 - alpha_bar)[:, None, None, None]
    noised = keep_part * augmented + blend_part * noise_grid
    patches = patchify(noised).astype(jnp.bfloat16)
    target = patchify(noise_grid)
    half_side = side_cells // 2
    per_view = half_side * half_side
    tokens = jnp.dot(patches, w_patch, preferred_element_type=jnp.float32)
    tokens = tokens + jnp.tile(position_table(half_side, width), (views_count, 1))
    stamp = time_features(steps_in, w_time.shape[0]).astype(jnp.bfloat16)
    conditioning = jax.nn.silu(jnp.dot(stamp, w_time, preferred_element_type=jnp.float32))
    modulation = jnp.dot(conditioning.astype(jnp.bfloat16), w_ada, preferred_element_type=jnp.float32)
    offset_rows = jnp.repeat(modulation[:, :width], per_view, axis=0)
    scale_rows = jnp.repeat(modulation[:, width:2 * width], per_view, axis=0)
    gate_rows = jnp.repeat(modulation[:, 2 * width:], per_view, axis=0)
    modulated = (layer_norm(tokens) * (1.0 + scale_rows) + offset_rows).astype(jnp.bfloat16)
    preact = jnp.dot(modulated, w_fc1, preferred_element_type=jnp.float32)
    hidden, gelu_back = jax.vjp(partial(jax.nn.gelu, approximate=True), preact)
    hidden_low = hidden.astype(jnp.bfloat16)
    branch = lax.dot_general(hidden_low, w_fc2, (((1,), (1,)), ((), ())), preferred_element_type=jnp.float32)
    mixed_rows = tokens + gate_rows * branch
    final_norm, norm_back = jax.vjp(layer_norm, mixed_rows)
    final_low = final_norm.astype(jnp.bfloat16)
    predicted = jnp.dot(final_low, w_final, preferred_element_type=jnp.float32)
    residue = predicted - target
    entries = residue.shape[0] * residue.shape[1]
    loss_value = jnp.sum(residue * residue) / entries
    grad_pred = (residue * (2.0 / entries)).astype(jnp.bfloat16)
    grad_final = lax.dot_general(grad_pred, w_final, (((1,), (1,)), ((), ())), preferred_element_type=jnp.float32)
    grad_mixed = norm_back(grad_final)[0]
    grad_branch = (gate_rows * grad_mixed).astype(jnp.bfloat16)
    grad_fc2 = lax.dot_general(grad_branch, hidden_low, (((0,), (0,)), ((), ())), preferred_element_type=jnp.float32)
    grad_hidden = jnp.dot(grad_branch, w_fc2, preferred_element_type=jnp.float32)
    grad_pre = gelu_back(grad_hidden)[0].astype(jnp.bfloat16)
    grad_fc1 = lax.dot_general(modulated, grad_pre, (((0,), (0,)), ((), ())), preferred_element_type=jnp.float32)
    return (loss_value, grad_fc1, grad_fc2)

def clip_pair(grad_fc1, grad_fc2):
    squares = jnp.sum(grad_fc1 * grad_fc1) + jnp.sum(grad_fc2 * grad_fc2)
    root_mean = jnp.sqrt(squares / (grad_fc1.size + grad_fc2.size))
    factor = 1.0 / (root_mean + clip_offset)
    return (grad_fc1 * factor, grad_fc2 * factor)

def selected_terms(chosen, mean_part, logvar, vae_eps, mirror, crop_at, steps_in, noise, weights):

    def compute():
        loss_value, grad_fc1, grad_fc2 = example_terms(mean_part, logvar, vae_eps, mirror, crop_at, steps_in, noise, weights)
        clipped_fc1, clipped_fc2 = clip_pair(grad_fc1, grad_fc2)
        return (loss_value, clipped_fc1, clipped_fc2)

    def skipped():
        zeros = jnp.zeros((weights[3].shape[0], weights[3].shape[1]), jnp.float32)
        return (jnp.zeros((), jnp.float32), zeros, zeros)
    return lax.cond(chosen == 1, compute, skipped)

def reference(features, conv_weight, vae_noise, flips, crops, tsteps, diffusion_noise, selected, w_patch, w_time, w_ada, w_fc1, w_fc2, w_final, noise_fc1, noise_fc2):
    group_count = features.shape[0]
    slot_count = features.shape[1]
    side_cells = features.shape[2]
    images = features.reshape(group_count * slot_count, side_cells, side_cells, features.shape[4])

    def one_image(image):
        padded = jnp.pad(image, ((1, 1), (0, 0), (0, 0)))[None]
        return conv_moments(padded, conv_weight)[0]
    moments = lax.map(one_image, images)
    latent_moments = jnp.swapaxes(moments.reshape(group_count, slot_count, -1), 0, 1)

    def reorder(values):
        return jnp.swapaxes(values, 0, 1).reshape((group_count * slot_count,) + values.shape[2:])
    inputs = (moments, reorder(vae_noise), reorder(flips), reorder(crops), reorder(tsteps), reorder(diffusion_noise), reorder(selected))
    weights = (w_patch, w_time, w_ada, w_fc1, w_fc2, w_final)
    channels = conv_weight.shape[3] // 2

    def accumulate(running, item):
        moment, vae_eps, mirror, crop_at, steps_in, noise, chosen = item
        loss_value, clipped_fc1, clipped_fc2 = selected_terms(chosen, moment[..., :channels], moment[..., channels:], vae_eps, mirror, crop_at, steps_in, noise, weights)
        return ((running[0] + loss_value, running[1] + clipped_fc1, running[2] + clipped_fc2), None)
    start_state = (jnp.zeros((), jnp.float32), jnp.zeros(w_fc1.shape, jnp.float32), jnp.zeros(w_fc1.shape, jnp.float32))
    totals, ignored = lax.scan(accumulate, start_state, inputs)
    update_fc1 = (totals[1] + noise_weight * noise_fc1) / SELECTED
    update_fc2 = (totals[2] + noise_weight * noise_fc2) / SELECTED
    return (update_fc1, update_fc2, totals[0] / SELECTED, latent_moments)
```

```python
import math

import jax
import jax.numpy as jnp
import ml_dtypes
import numpy as np
from jax import lax
from jax.experimental import pallas as pl
from jax.experimental.pallas import tpu as pltpu
from jax.sharding import Mesh
from jax.sharding import PartitionSpec as P

MESH = pl.DeviceIdType.MESH
DP = ("dp_0", "dp_1")
FSDP = ("fsdp_0", "fsdp_1")
NZ, NC, NY, NX = 8, 2, 4, 4
NDP = NZ * NC
D, FF, TOK, FCH = 384, 1536, 1024, 512
SHARD = FF // (NY * NX)
HALF = SHARD // 2
SIDE, LC, AUG, TSTEPS = 32, 4, 4, 1000
SELECTED = 128
CHUNK = 384
PIECE = 5
TILES = NZ * PIECE
USED_TILES = (SHARD // 8) * (D // 128)
clip_offset = 1e-05
noise_weight = 16.0
norm_epsilon = 1e-06
VMEM_SPEC = pl.BlockSpec(memory_space=pltpu.VMEM)
SMEM_SPEC = pl.BlockSpec(memory_space=pltpu.SMEM)
F32, BF16 = jnp.float32, jnp.bfloat16


def three_parts(table):
    high = table.astype(np.float32).astype(ml_dtypes.bfloat16)
    rest = table.astype(np.float32) - high.astype(np.float32)
    middle = rest.astype(ml_dtypes.bfloat16)
    low = (rest - middle.astype(np.float32)).astype(ml_dtypes.bfloat16)
    return high, middle, low


def position_rows():
    side, quarter = SIDE // 2, D // 4
    frequency = 1.0 / 10000.0 ** (np.arange(quarter) / quarter)
    angles = np.arange(side)[:, None] * frequency[None, :]
    line = np.concatenate([np.sin(angles), np.cos(angles)], axis=1)
    parts = three_parts(line)
    zero = np.zeros_like(parts[0])
    rows = [np.concatenate([p, zero], axis=1) for p in parts]
    cols = [np.concatenate([zero, p], axis=1) for p in parts]
    return np.concatenate(rows + cols, axis=0)


def blend_tables():
    beta = 0.0001 + np.arange(TSTEPS) * (0.02 - 0.0001) / (TSTEPS - 1)
    alpha_bar = np.cumprod(1.0 - beta)
    return np.stack([np.sqrt(alpha_bar), np.sqrt(1.0 - alpha_bar)]).astype(np.float32)


def time_rates():
    steps = np.arange(128, dtype=np.float32)
    scaled = np.float32(-math.log(10000.0)) * steps / np.float32(128)
    return np.exp(scaled).astype(np.float32).reshape(1, 128)


def conv_kernel(x_ref, w_ref, msg_ref):
    taps = lax.dot_general(
        w_ref[...], x_ref[...], (((1,), (1,)), ((), ())), preferred_element_type=F32
    )
    lane = lax.broadcasted_iota(jnp.int32, (8, 128), 1)
    col = lane % SIDE
    zero = jnp.zeros((8, 128), F32)

    def tap(dy, dx, v):
        at = (dy * 3 + dx) * 8
        return taps[at : at + 8, 128 * v : 128 * v + 128]

    for v in range(8):
        rows = []
        for dy in range(3):
            left = jnp.where(col == 0, zero, pltpu.roll(tap(dy, 0, v), 1, 1))
            right = jnp.where(col == SIDE - 1, zero, pltpu.roll(tap(dy, 2, v), 127, 1))
            rows.append(left + tap(dy, 1, v) + right)
        for odd in range(2):
            parts = [pltpu.roll(r, 64, 1) if odd else r for r in rows]
            parts = [jnp.where(lane < 64, r, zero) for r in parts]
            msg_ref[2 * v + odd] = (
                parts[2] + pltpu.roll(parts[1], 32, 1) + pltpu.roll(parts[0], 64, 1)
            )


def place():
    return tuple(lax.axis_index(a) for a in ("dp_0", "dp_1", "fsdp_0", "fsdp_1"))


def gather_kernel(w1_ref, w2_ref, msg_ref, all_ref, got_ref, *sems):
    s1_send, s1_recv, s2_send, s2_recv, p_send, p_recv, m_send, m_recv = sems
    z, c, y, x = place()
    me = z * NC + c

    def x_at(k):
        return lax.rem(x + k, NX)

    def y_at(k):
        return lax.rem(y + k, NY)

    def dp_at(k):
        return lax.rem(me + k, NDP)

    def dp_device(k):
        other = dp_at(k)
        return {"dp_0": other // NC, "dp_1": lax.rem(other, NC)}

    barrier = pltpu.get_barrier_semaphore()
    for k in range(1, NX):
        pl.semaphore_signal(barrier, 1, device_id={"fsdp_1": x_at(k)}, device_id_type=MESH)
        pl.semaphore_signal(barrier, 1, device_id={"fsdp_0": y_at(k)}, device_id_type=MESH)
    for k in range(1, NDP):
        pl.semaphore_signal(barrier, 1, device_id=dp_device(k), device_id_type=MESH)
    own = jnp.where(c == 0, w1_ref[...], w2_ref[...])
    all_ref[c, y, x, 0] = own[:HALF]
    all_ref[c, y, x, 1] = own[HALF:]
    got_ref[me] = msg_ref[me]
    pl.semaphore_wait(barrier, NX - 1 + NY - 1 + NDP - 1)

    def remote(ref, at, send, recv, device):
        return pltpu.make_async_remote_copy(
            src_ref=ref.at[at],
            dst_ref=ref.at[at],
            send_sem=send,
            recv_sem=recv,
            device_id=device,
            device_id_type=MESH,
        )

    def message(k):
        return pltpu.make_async_remote_copy(
            src_ref=msg_ref.at[dp_at(k)],
            dst_ref=got_ref.at[me],
            send_sem=m_send.at[k],
            recv_sem=m_recv.at[k],
            device_id=dp_device(k),
            device_id_type=MESH,
        )

    def first(half, k):
        device = {"fsdp_1": x_at(k)} if half == 0 else {"fsdp_0": y_at(k)}
        return remote(
            all_ref, (c, y, x, half), s1_send.at[half, k], s1_recv.at[half, k], device
        )

    def line(half, k):
        if half == 0:
            return (c, y_at(NY - k), slice(None), 0)
        return (c, slice(None), x_at(NX - k), 1)

    def second(half, k):
        device = {"fsdp_0": y_at(k)} if half == 0 else {"fsdp_1": x_at(k)}
        return remote(
            all_ref, line(half, 0), s2_send.at[half, k], s2_recv.at[half, k], device
        )

    def across(half, k):
        return remote(
            all_ref, line(half, k), p_send.at[half, k], p_recv.at[half, k], {"dp_1": 1 - c}
        )

    messages = [message(k) for k in range(1, NDP)]
    firsts = [[first(h, k) for k in range(1, 4)] for h in range(2)]
    seconds = [[second(h, k) for k in range(1, 4)] for h in range(2)]
    acrosses = [[across(h, k) for k in range(4)] for h in range(2)]
    for m in messages:
        m.start()
    for k in range(3):
        for h in range(2):
            firsts[h][k].start()
    for h in range(2):
        for f in firsts[h]:
            f.wait_recv()
        for s in seconds[h]:
            s.start()
        acrosses[h][0].start()
    for k in range(3):
        for h in range(2):
            seconds[h][k].wait_recv()
            acrosses[h][k + 1].start()
    for m in messages:
        m.wait_recv()
    for h in range(2):
        for a in acrosses[h]:
            a.wait_recv()
    for group in [messages] + firsts + seconds + acrosses:
        for copy in group:
            copy.wait_send()


def split_three(value):
    high = value.astype(BF16)
    rest = value - high.astype(F32)
    middle = rest.astype(BF16)
    low = (rest - middle.astype(F32)).astype(BF16)
    return jnp.concatenate([high, middle, low], axis=0)


def joined_three(value, rows):
    return (value[2 * rows :] + value[rows : 2 * rows]) + value[:rows]


def compute_kernel(
    flips_ref,
    crops_ref,
    steps_ref,
    selected_ref,
    table_ref,
    got_ref,
    weights_ref,
    vae_ref,
    noise_ref,
    wp_ref,
    pos_ref,
    rates_ref,
    wt_ref,
    wa_ref,
    wf_ref,
    grads_ref,
    loss_ref,
    moments_ref,
    rows_ref,
    pads_ref,
    shift_ref,
    scale_ref,
    gate_ref,
    tok_ref,
    modt_ref,
    mod_ref,
    w2_ref,
    hid_ref,
    slope_ref,
    target_ref,
    gbt_ref,
    gb_ref,
    raw_ref,
    square_ref,
):
    lane = lax.broadcasted_iota(jnp.int32, (8, 128), 1)
    zero = jnp.zeros((8, 128), F32)

    for k in range(8):
        low = pltpu.roll(got_ref[2 * k], 96, 1)
        above = pltpu.roll(got_ref[2 * k + 2], 96, 1) if k < 7 else zero
        high = pltpu.roll(got_ref[2 * k + 1], 32, 1)
        below = pltpu.roll(got_ref[2 * k - 1], 32, 1) if k > 0 else zero
        four = jnp.where(lane < 96, low, above) + jnp.where(lane >= 32, high, below)
        for r in range(4):
            at = (4 * k + r) * 8
            rows_ref[at : at + 8, :] = pltpu.roll(four, 128 - 32 * r, 1) if r else four
    wide = lax.broadcasted_iota(jnp.int32, (SIDE, 128), 1) // SIDE
    halves = []
    for h in range(2):
        value = rows_ref[pl.ds(4 * h, SIDE, stride=8), :]
        for ch in range(1, 4):
            part = rows_ref[pl.ds(4 * h + ch, SIDE, stride=8), :]
            value = jnp.where(wide == ch, pltpu.roll(part, 32 * ch, 1), value)
        halves.append(value)
    by_channel = jnp.concatenate(halves, axis=1)
    source = lax.broadcasted_iota(jnp.int32, (256, 512), 0)
    goal = lax.broadcasted_iota(jnp.int32, (256, 512), 1)
    channel, column = source // SIDE, source % SIDE
    natural = column * 8 + channel
    apart = 256 + (channel // 4) * 128 + column * 4 + channel % 4
    spread = jnp.where((goal == natural) | (goal == apart), 1.0, 0.0).astype(BF16)
    placed = joined_three(
        jnp.dot(split_three(by_channel), spread, preferred_element_type=F32), SIDE
    )
    moments_ref[pl.ds(0, SIDE, stride=2), :] = placed[:, 0:128]
    moments_ref[pl.ds(1, SIDE, stride=2), :] = placed[:, 128:256]

    @pl.when(selected_ref[0, 0] != 1)
    def _():
        grads_ref[...] = jnp.zeros_like(grads_ref)
        loss_ref[...] = jnp.zeros_like(loss_ref)

    @pl.when(selected_ref[0, 0] == 1)
    def _():
        latent = placed[:, 256:384] + jnp.exp(0.5 * placed[:, 384:512]) * vae_ref[...]
        source = lax.broadcasted_iota(jnp.int32, (128, 128), 0)
        goal = lax.broadcasted_iota(jnp.int32, (128, 128), 1)
        maps = []
        for a in range(AUG):
            cell = goal // LC + crops_ref[1, a] - 2
            inside = (cell >= 0) & (cell < SIDE)
            mirror = (flips_ref[0, a] == 1).astype(jnp.int32)
            cell = cell + mirror * (SIDE - 1 - 2 * cell)
            match = inside & (source == cell * LC + goal % LC)
            maps.append(jnp.where(match, 1.0, 0.0).astype(BF16))
        columns = jnp.dot(
            split_three(latent), jnp.concatenate(maps, axis=1), preferred_element_type=F32
        )
        columns = joined_three(columns, SIDE)
        noised, noises = [], []
        for a in range(AUG):
            pads_ref[a] = jnp.zeros((40, 128), F32)
            pads_ref[a, 2 : 2 + SIDE, :] = columns[:, 128 * a : 128 * a + 128]
        for dr in range(2):
            for a in range(AUG):
                view = pads_ref[a, pl.ds(crops_ref[0, a] + dr, 16, stride=2), :]
                noise = noise_ref[pl.ds(dr * 4 + a, 16, stride=8), :]
                step = steps_ref[0, a]
                noised.append(table_ref[0, step] * view + table_ref[1, step] * noise)
                noises.append(noise)

        def patched(pieces):
            turned = jnp.concatenate(pieces, axis=0).T
            first, last = [], []
            for m in range(8):
                even = turned[16 * m : 16 * m + 8]
                odd = turned[16 * m + 8 : 16 * m + 16]
                first.append(jnp.where(lane < 64, even, pltpu.roll(odd, 64, 1)))
                last.append(jnp.where(lane < 64, pltpu.roll(even, 64, 1), odd))
            return jnp.concatenate(
                [jnp.concatenate(first, axis=1), jnp.concatenate(last, axis=1)], axis=0
            )

        patches = patched(noised).astype(BF16)
        target_ref[...] = patched(noises)

        which = lax.broadcasted_iota(jnp.int32, (96, TOK), 0)
        token = lax.broadcasted_iota(jnp.int32, (96, TOK), 1)
        cell = jnp.where(which < 48, token % 16, token // 64)
        marks = jnp.where(which % 16 == cell, 1.0, 0.0).astype(BF16)
        tok_ref[...] = lax.dot_general(
            jnp.concatenate([wp_ref[...], pos_ref[...]], axis=0),
            jnp.concatenate([patches, marks], axis=0),
            (((0,), (0,)), ((), ())),
            preferred_element_type=F32,
        )

        row = lax.broadcasted_iota(jnp.int32, (8, 128), 0)
        steps = jnp.zeros((8, 128), F32)
        for a in range(AUG):
            steps = jnp.where(row == a, steps_ref[0, a].astype(F32), steps)
        phases = steps * rates_ref[...]
        stamp = jnp.concatenate([jnp.cos(phases), jnp.sin(phases)], axis=1).astype(BF16)
        raw = jnp.dot(stamp, wt_ref[...], preferred_element_type=F32)
        conditioning = (raw * (1.0 / (1.0 + jnp.exp(-raw)))).astype(BF16)
        modulation = jnp.dot(conditioning, wa_ref[...], preferred_element_type=F32)
        views = [jnp.broadcast_to(modulation[a : a + 1], (16, 3 * D)) for a in range(AUG)]
        turned = jnp.concatenate(views + views, axis=0).T
        shift_ref[...] = turned[:D]
        scale_ref[...] = 1.0 + turned[D : 2 * D]
        gate_ref[...] = turned[2 * D :]

        @pl.loop(0, TOK // 128)
        def _(m):
            at = pl.ds(pl.multiple_of(m * 128, 128), 128)
            value = tok_ref[:, at]
            center = value - jnp.sum(value, axis=0, keepdims=True) * (1.0 / D)
            variance = jnp.sum(center * center, axis=0, keepdims=True) * (1.0 / D)
            normed = center * lax.rsqrt(variance + norm_epsilon)
            out = normed * scale_ref[...] + shift_ref[...]
            modt_ref[:, at] = out.astype(BF16)
            mod_ref[at, :] = out.T.astype(BF16)

        @pl.loop(0, FF // 128)
        def _(m):
            at = pl.ds(pl.multiple_of(m * 128, 128), 128)
            w2_ref[:, at] = weights_ref[1, at, :].astype(F32).T.astype(BF16)

        root = math.sqrt(2.0 / math.pi)

        @pl.loop(0, FF // CHUNK)
        def _(f):
            at = pl.ds(pl.multiple_of(f * CHUNK, CHUNK), CHUNK)
            pre = jnp.dot(weights_ref[0, at, :], modt_ref[...], preferred_element_type=F32)
            squared = pre * pre
            inner = pre * (squared * (root * 0.044715) + root)
            share = 0.5 * jnp.tanh(inner) + 0.5
            hidden = pre * share
            hid_ref[at, :] = hidden.astype(BF16)
            slope = (1.0 - share) * hidden * (squared * (6.0 * root * 0.044715) + 2.0 * root)
            slope_ref[at, :] = slope + share

        loss_ref[...] = jnp.zeros_like(loss_ref)

        @pl.loop(0, TOK // 256)
        def _(m):
            at = pl.ds(pl.multiple_of(m * 256, 256), 256)
            branch = jnp.dot(w2_ref[...], hid_ref[:, at], preferred_element_type=F32)
            gate = jnp.concatenate([gate_ref[...], gate_ref[...]], axis=1)
            mixed = tok_ref[:, at] + gate * branch
            center = mixed - jnp.sum(mixed, axis=0, keepdims=True) * (1.0 / D)
            variance = jnp.sum(center * center, axis=0, keepdims=True) * (1.0 / D)
            inverse = lax.rsqrt(variance + norm_epsilon)
            normed = center * inverse
            predicted = jnp.dot(wf_ref[...], normed.astype(BF16), preferred_element_type=F32)
            residue = predicted - target_ref[:, at]
            loss_ref[...] += jnp.sum(residue * residue) * (1.0 / (TOK * 16))
            grad_pred = (residue * (2.0 / (TOK * 16))).astype(BF16)
            grad_normed = lax.dot_general(
                wf_ref[...], grad_pred, (((0,), (0,)), ((), ())), preferred_element_type=F32
            )
            mean = jnp.sum(grad_normed, axis=0, keepdims=True) * (1.0 / D)
            along = jnp.sum(grad_normed * normed, axis=0, keepdims=True) * (1.0 / D)
            grad_mixed = inverse * (grad_normed - mean - normed * along)
            grad_branch = gate * grad_mixed
            gbt_ref[:, at] = grad_branch.astype(BF16)
            gb_ref[at, :] = grad_branch.T.astype(BF16)

        square_ref[...] = jnp.zeros_like(square_ref)

        @pl.loop(0, FF // CHUNK)
        def _(f):
            at = pl.ds(pl.multiple_of(f * CHUNK, CHUNK), CHUNK)
            grad_hidden = jnp.dot(
                weights_ref[1, at, :], gbt_ref[...], preferred_element_type=F32
            )
            grad_pre = (slope_ref[at, :] * grad_hidden).astype(BF16)
            grad_1 = jnp.dot(grad_pre, mod_ref[...], preferred_element_type=F32)
            grad_2 = jnp.dot(hid_ref[at, :], gb_ref[...], preferred_element_type=F32)
            raw_ref[0, at, :] = grad_1
            raw_ref[1, at, :] = grad_2
            square_ref[...] += jnp.sum(
                grad_1 * grad_1 + grad_2 * grad_2, axis=0, keepdims=True
            )

        total = jnp.sum(square_ref[...], axis=1, keepdims=True)
        factor = 1.0 / (jnp.sqrt(total * (1.0 / (2 * D * FF))) + clip_offset)

        @pl.loop(0, FF // CHUNK)
        def _(f):
            at = pl.ds(pl.multiple_of(f * CHUNK, CHUNK), CHUNK)
            for w in range(2):
                grads_ref[w, at, :] = (raw_ref[w, at, :] * factor).astype(BF16)


def reduce_kernel(g_ref, loss_ref, sum_ref, total_ref, *scratch):
    (r0, s1, r1, acc, r2, tiles, r3, whole, l0, l1, l2) = scratch[:11]
    (q_send, q_recv, s1_send, s1_recv, s2_send, s2_recv, z_send, z_recv) = scratch[11:19]
    (a_send, a_recv, f_send, f_recv, l_send, l_recv) = scratch[19:]
    z, c, y, x = place()
    partner = {"dp_1": 1 - c}

    def x_at(k):
        return lax.rem(x + k, NX)

    def y_at(k):
        return lax.rem(y + k, NY)

    def z_at(k):
        return lax.rem(z + k, NZ)

    barrier = pltpu.get_barrier_semaphore()
    pl.semaphore_signal(barrier, 1, device_id=partner, device_id_type=MESH)
    for k in range(1, NX):
        pl.semaphore_signal(barrier, 1, device_id={"fsdp_1": x_at(k)}, device_id_type=MESH)
        pl.semaphore_signal(barrier, 1, device_id={"fsdp_0": y_at(k)}, device_id_type=MESH)
    for k in range(1, NZ):
        pl.semaphore_signal(barrier, 1, device_id={"dp_0": z_at(k)}, device_id_type=MESH)
    l0[0] = loss_ref[...]
    pl.semaphore_wait(barrier, 1 + NX - 1 + NY - 1 + NZ - 1)

    def remote(src, dst, send, recv, device):
        return pltpu.make_async_remote_copy(
            src_ref=src,
            dst_ref=dst,
            send_sem=send,
            recv_sem=recv,
            device_id=device,
            device_id_type=MESH,
        )

    def piece(half, k):
        if half == 0:
            return (slice(None), x_at(k), 0)
        return (y_at(k), slice(None), 1)

    def part(half, k, j):
        if half == 0:
            return (j, x_at(k), 0)
        return (y_at(k), j, 1)

    def first_to(half, k):
        return {"fsdp_1": x_at(k)} if half == 0 else {"fsdp_0": y_at(k)}

    def second_to(half, k):
        return {"fsdp_0": y_at(k)} if half == 0 else {"fsdp_1": x_at(k)}

    def second_at(half, k):
        return y_at(k) if half == 0 else x_at(k)

    loss_0 = remote(l0.at[0], l0.at[1], l_send.at[0], l_recv.at[0], partner)
    loss_0.start()
    swaps = {}
    for k in (2, 1, 3, 0):
        for h in range(2):
            at = piece(h, k)
            swaps[h, k] = remote(
                g_ref.at[(1 - c,) + at], r0.at[at], q_send.at[h, k], q_recv.at[h, k], partner
            )
            swaps[h, k].start()
    firsts = {}
    for k in (2, 1, 3, 0):
        for h in range(2):
            swaps[h, k].wait_recv()
            for j in range(4):
                at = part(h, k, j)
                value = g_ref[(c,) + at].astype(F32) + r0[at].astype(F32)
                if k == 0:
                    acc[h, j] = value
                else:
                    s1[h, k - 1, j] = value.astype(BF16)
            if k > 0:
                firsts[h, k] = remote(
                    s1.at[h, k - 1],
                    r1.at[h, k - 1],
                    s1_send.at[h, k],
                    s1_recv.at[h, k],
                    first_to(h, k),
                )
                firsts[h, k].start()
    loss_0.wait_recv()
    l1[x] = l0[0] + l0[1]
    losses = [loss_0]
    for k in range(1, NX):
        copy = remote(l1.at[x], l1.at[x], l_send.at[k], l_recv.at[k], {"fsdp_1": x_at(k)})
        copy.start()
        losses.append(copy)
    seconds = {}
    for h in range(2):
        for k in (1, 3, 2):
            firsts[h, k].wait_recv()
        for k in (2, 1, 3, 0):
            j = second_at(h, k)
            acc[h, j] = (acc[h, j] + r1[h, 0, j].astype(F32)) + (
                r1[h, 1, j].astype(F32) + r1[h, 2, j].astype(F32)
            )
            if k > 0:
                seconds[h, k] = remote(
                    acc.at[h, j],
                    r2.at[h, k - 1],
                    s2_send.at[h, k],
                    s2_recv.at[h, k],
                    second_to(h, k),
                )
                seconds[h, k].start()
    for copy in losses[1:]:
        copy.wait_recv()
    l2[y] = (l1[0] + l1[1]) + (l1[2] + l1[3])
    for k in range(1, NY):
        copy = remote(
            l2.at[y], l2.at[y], l_send.at[3 + k], l_recv.at[3 + k], {"fsdp_0": y_at(k)}
        )
        copy.start()
        losses.append(copy)
    for h in range(2):
        for k in (1, 3, 2):
            seconds[h, k].wait_recv()
        j = second_at(h, 0)
        value = (acc[h, j] + r2[h, 0]) + (r2[h, 1] + r2[h, 2])
        for i in range(HALF // 8):
            for n in range(D // 128):
                t = (h * (HALF // 8) + i) * (D // 128) + n
                tiles[t // PIECE, t % PIECE] = value[8 * i : 8 * i + 8, 128 * n : 128 * n + 128]
    for copy in losses[4:]:
        copy.wait_recv()
    at = USED_TILES
    tiles[at // PIECE, at % PIECE] = (l2[0] + l2[1]) + (l2[2] + l2[3])
    for t in range(USED_TILES + 1, TILES):
        tiles[t // PIECE, t % PIECE] = jnp.zeros((8, 128), F32)

    order = (4, 3, 5, 2, 6, 1, 7)
    thirds = []
    for k in order:
        copy = remote(
            tiles.at[z_at(k)], r3.at[z], z_send.at[k], z_recv.at[k], {"dp_0": z_at(k)}
        )
        copy.start()
        thirds.append(copy)
    r3[z] = tiles[z]
    for copy in thirds:
        copy.wait_recv()
    value = r3[0]
    for k in range(1, NZ):
        value = value + r3[k]
    whole[c, z] = value
    spreads = {}
    for k in order:
        spreads[k] = remote(
            whole.at[c, z], whole.at[c, z], a_send.at[k], a_recv.at[k], {"dp_0": z_at(k)}
        )
        spreads[k].start()
    crossings = []
    for k in (0, 7, 1, 6, 2, 5, 3, 4):
        if k > 0:
            spreads[k].wait_recv()
        at = z_at(NZ - k) if k > 0 else z
        copy = remote(whole.at[c, at], whole.at[c, at], f_send.at[k], f_recv.at[k], partner)
        copy.start()
        crossings.append(copy)
    for copy in crossings:
        copy.wait_recv()
    for w in range(2):
        for t in range(USED_TILES):
            i, n = t // (D // 128), t % (D // 128)
            sum_ref[w, 8 * i : 8 * i + 8, 128 * n : 128 * n + 128] = whole[
                w, t // PIECE, t % PIECE
            ]
    total_ref[...] = whole[0, USED_TILES // PIECE, USED_TILES % PIECE]
    for group in (swaps, firsts, seconds, spreads):
        for copy in group.values():
            copy.wait_send()
    for group in (losses, thirds, crossings):
        for copy in group:
            copy.wait_send()


def per_device(
    features,
    conv_weight,
    vae_noise,
    flips,
    crops,
    tsteps,
    diffusion_noise,
    selected,
    w_patch,
    w_time,
    w_ada,
    w_fc1,
    w_fc2,
    w_final,
    noise_fc1,
    noise_fc2,
):
    dma = pltpu.SemaphoreType.DMA
    pixels = features.reshape(TOK, FCH)
    taps = conv_weight.transpose(0, 1, 3, 2).reshape(72, FCH)
    messages = pl.pallas_call(
        conv_kernel,
        out_shape=jax.ShapeDtypeStruct((NDP, 8, 128), F32),
        in_specs=[VMEM_SPEC] * 2,
        out_specs=VMEM_SPEC,
        name="conv",
    )(pixels, taps)
    gathered, received = pl.pallas_call(
        gather_kernel,
        out_shape=(
            jax.ShapeDtypeStruct((2, NY, NX, 2, HALF, D), BF16),
            jax.ShapeDtypeStruct((NDP, 8, 128), F32),
        ),
        in_specs=[VMEM_SPEC] * 3,
        out_specs=(VMEM_SPEC, VMEM_SPEC),
        scratch_shapes=[dma((2, 4))] * 6 + [dma((NDP,))] * 2,
        compiler_params=pltpu.CompilerParams(collective_id=0, has_side_effects=True),
        name="gather",
    )(w_fc1.T, w_fc2.T, messages)
    weights = gathered.reshape(2, FF, D)
    views = diffusion_noise.reshape(AUG, SIDE, SIDE * LC).transpose(1, 0, 2)
    grads, loss, moments = pl.pallas_call(
        compute_kernel,
        out_shape=(
            jax.ShapeDtypeStruct((2, FF, D), BF16),
            jax.ShapeDtypeStruct((8, 128), F32),
            jax.ShapeDtypeStruct((2 * SIDE, 128), F32),
        ),
        in_specs=[SMEM_SPEC] * 5 + [VMEM_SPEC] * 10,
        out_specs=(VMEM_SPEC,) * 3,
        scratch_shapes=[
            pltpu.VMEM((256, 128), F32),
            pltpu.VMEM((AUG, 40, 128), F32),
            pltpu.VMEM((D, 128), F32),
            pltpu.VMEM((D, 128), F32),
            pltpu.VMEM((D, 128), F32),
            pltpu.VMEM((D, TOK), F32),
            pltpu.VMEM((D, TOK), BF16),
            pltpu.VMEM((TOK, D), BF16),
            pltpu.VMEM((D, FF), BF16),
            pltpu.VMEM((FF, TOK), BF16),
            pltpu.VMEM((FF, TOK), F32),
            pltpu.VMEM((16, TOK), F32),
            pltpu.VMEM((D, TOK), BF16),
            pltpu.VMEM((TOK, D), BF16),
            pltpu.VMEM((2, FF, D), F32),
            pltpu.VMEM((1, D), F32),
        ],
        compiler_params=pltpu.CompilerParams(vmem_limit_bytes=56 << 20),
        name="example",
    )(
        flips.reshape(1, AUG),
        crops.reshape(AUG, 2).T,
        tsteps.reshape(1, AUG),
        selected,
        jnp.asarray(blend_tables()),
        received,
        weights,
        vae_noise.reshape(SIDE, SIDE * LC),
        views.reshape(SIDE * AUG, SIDE * LC),
        w_patch,
        jnp.asarray(position_rows()),
        jnp.asarray(time_rates()),
        w_time,
        w_ada,
        w_final.T,
    )
    quarter = (2, 4, HALF, D)
    sums, total = pl.pallas_call(
        reduce_kernel,
        out_shape=(
            jax.ShapeDtypeStruct((2, SHARD, D), F32),
            jax.ShapeDtypeStruct((8, 128), F32),
        ),
        in_specs=[VMEM_SPEC] * 2,
        out_specs=(VMEM_SPEC, VMEM_SPEC),
        scratch_shapes=[
            pltpu.VMEM((NY, NX, 2, HALF, D), BF16),
            pltpu.VMEM((2, 3, 4, HALF, D), BF16),
            pltpu.VMEM((2, 3, 4, HALF, D), BF16),
            pltpu.VMEM(quarter, F32),
            pltpu.VMEM((2, 3, HALF, D), F32),
            pltpu.VMEM((NZ, PIECE, 8, 128), F32),
            pltpu.VMEM((NZ, PIECE, 8, 128), F32),
            pltpu.VMEM((2, NZ, PIECE, 8, 128), F32),
            pltpu.VMEM((2, 8, 128), F32),
            pltpu.VMEM((NX, 8, 128), F32),
            pltpu.VMEM((NY, 8, 128), F32),
        ]
        + [dma((2, 4))] * 6
        + [dma((NZ,))] * 8,
        compiler_params=pltpu.CompilerParams(collective_id=1, has_side_effects=True),
        name="reduce",
    )(grads.reshape(2, NY, NX, 2, HALF, D), loss)
    update_fc1 = (sums[0].T + noise_weight * noise_fc1) / SELECTED
    update_fc2 = (sums[1].T + noise_weight * noise_fc2) / SELECTED
    return (update_fc1, update_fc2, total[0, 0] / SELECTED, moments.reshape(1, 1, -1))


def solution(mesh):
    split = Mesh(mesh.devices.reshape(NZ, NC, NY, NX), DP + FSDP)
    return jax.shard_map(
        per_device,
        mesh=split,
        in_specs=(
            P(FSDP, None, DP, None, None),
            P(),
            P(DP, FSDP, None),
            P(DP, FSDP, None),
            P(DP, FSDP, None, None),
            P(DP, FSDP, None),
            P(DP, FSDP, None, None),
            P(DP, FSDP),
            P(),
            P(),
            P(),
            P(None, FSDP),
            P(None, FSDP),
            P(),
            P(None, FSDP),
            P(None, FSDP),
        ),
        out_specs=(P(None, FSDP), P(None, FSDP), P(), P(DP, FSDP, None)),
        check_vma=False,
    )
```

```python
import math

import jax
import jax.numpy as jnp
import ml_dtypes
import numpy as np
from jax import lax
from jax.experimental import pallas as pl
from jax.experimental.pallas import tpu as pltpu
from jax.sharding import Mesh
from jax.sharding import PartitionSpec as P

MESH = pl.DeviceIdType.MESH
DP = ("dp_0", "dp_1")
FSDP = ("fsdp_0", "fsdp_1")
NZ, NC, NY, NX = 8, 2, 4, 4
NDP = NZ * NC
D, FF, TOK, FCH = 384, 1536, 1024, 512
SHARD = FF // (NY * NX)
HALF = SHARD // 2
SIDE, LC, AUG, TSTEPS = 32, 4, 4, 1000
SELECTED = 128
CHUNK = 384
PIECE = 5
TILES = NZ * PIECE
USED_TILES = (SHARD // 8) * (D // 128)
clip_offset = 1e-05
noise_weight = 16.0
norm_epsilon = 1e-06
VMEM_SPEC = pl.BlockSpec(memory_space=pltpu.VMEM)
SMEM_SPEC = pl.BlockSpec(memory_space=pltpu.SMEM)
F32, BF16 = jnp.float32, jnp.bfloat16


def three_parts(table):
    high = table.astype(np.float32).astype(ml_dtypes.bfloat16)
    rest = table.astype(np.float32) - high.astype(np.float32)
    middle = rest.astype(ml_dtypes.bfloat16)
    low = (rest - middle.astype(np.float32)).astype(ml_dtypes.bfloat16)
    return high, middle, low


def position_rows():
    side, quarter = SIDE // 2, D // 4
    frequency = 1.0 / 10000.0 ** (np.arange(quarter) / quarter)
    angles = np.arange(side)[:, None] * frequency[None, :]
    line = np.concatenate([np.sin(angles), np.cos(angles)], axis=1)
    parts = three_parts(line)
    zero = np.zeros_like(parts[0])
    rows = [np.concatenate([p, zero], axis=1) for p in parts]
    cols = [np.concatenate([zero, p], axis=1) for p in parts]
    return np.concatenate(rows + cols, axis=0)


def blend_tables():
    beta = 0.0001 + np.arange(TSTEPS) * (0.02 - 0.0001) / (TSTEPS - 1)
    alpha_bar = np.cumprod(1.0 - beta)
    return np.stack([np.sqrt(alpha_bar), np.sqrt(1.0 - alpha_bar)]).astype(np.float32)


def time_rates():
    steps = np.arange(128, dtype=np.float32)
    scaled = np.float32(-math.log(10000.0)) * steps / np.float32(128)
    return np.exp(scaled).astype(np.float32).reshape(1, 128)


def conv_kernel(x_ref, w_ref, msg_ref):
    taps = lax.dot_general(
        w_ref[...], x_ref[...], (((1,), (1,)), ((), ())), preferred_element_type=F32
    )
    lane = lax.broadcasted_iota(jnp.int32, (8, 128), 1)
    col = lane % SIDE
    zero = jnp.zeros((8, 128), F32)

    def tap(dy, dx, v):
        at = (dy * 3 + dx) * 8
        return taps[at : at + 8, 128 * v : 128 * v + 128]

    for v in range(8):
        rows = []
        for dy in range(3):
            left = jnp.where(col == 0, zero, pltpu.roll(tap(dy, 0, v), 1, 1))
            right = jnp.where(col == SIDE - 1, zero, pltpu.roll(tap(dy, 2, v), 127, 1))
            rows.append(left + tap(dy, 1, v) + right)
        for odd in range(2):
            parts = [pltpu.roll(r, 64, 1) if odd else r for r in rows]
            parts = [jnp.where(lane < 64, r, zero) for r in parts]
            msg_ref[2 * v + odd] = (
                parts[2] + pltpu.roll(parts[1], 32, 1) + pltpu.roll(parts[0], 64, 1)
            )


def place():
    return tuple(lax.axis_index(a) for a in ("dp_0", "dp_1", "fsdp_0", "fsdp_1"))


def gather_kernel(w1_ref, w2_ref, msg_ref, all_ref, got_ref, *sems):
    s1_send, s1_recv, s2_send, s2_recv, p_send, p_recv, m_send, m_recv = sems
    z, c, y, x = place()
    me = z * NC + c

    def x_at(k):
        return lax.rem(x + k, NX)

    def y_at(k):
        return lax.rem(y + k, NY)

    def dp_at(k):
        return lax.rem(me + k, NDP)

    def dp_device(k):
        other = dp_at(k)
        return {"dp_0": other // NC, "dp_1": lax.rem(other, NC)}

    barrier = pltpu.get_barrier_semaphore()
    for k in range(1, NX):
        pl.semaphore_signal(barrier, 1, device_id={"fsdp_1": x_at(k)}, device_id_type=MESH)
        pl.semaphore_signal(barrier, 1, device_id={"fsdp_0": y_at(k)}, device_id_type=MESH)
    for k in range(1, NDP):
        pl.semaphore_signal(barrier, 1, device_id=dp_device(k), device_id_type=MESH)
    own = jnp.where(c == 0, w1_ref[...], w2_ref[...])
    all_ref[c, y, x, 0] = own[:HALF]
    all_ref[c, y, x, 1] = own[HALF:]
    got_ref[me] = msg_ref[me]
    pl.semaphore_wait(barrier, NX - 1 + NY - 1 + NDP - 1)

    def remote(ref, at, send, recv, device):
        return pltpu.make_async_remote_copy(
            src_ref=ref.at[at],
            dst_ref=ref.at[at],
            send_sem=send,
            recv_sem=recv,
            device_id=device,
            device_id_type=MESH,
        )

    def message(k):
        return pltpu.make_async_remote_copy(
            src_ref=msg_ref.at[dp_at(k)],
            dst_ref=got_ref.at[me],
            send_sem=m_send.at[k],
            recv_sem=m_recv.at[k],
            device_id=dp_device(k),
            device_id_type=MESH,
        )

    def first(half, k):
        device = {"fsdp_1": x_at(k)} if half == 0 else {"fsdp_0": y_at(k)}
        return remote(
            all_ref, (c, y, x, half), s1_send.at[half, k], s1_recv.at[half, k], device
        )

    def line(half, k):
        if half == 0:
            return (c, y_at(NY - k), slice(None), 0)
        return (c, slice(None), x_at(NX - k), 1)

    def half_line(half, k, part):
        at = pl.ds(2 * part, 2)
        if half == 0:
            return (c, y_at(NY - k), at, 0)
        return (c, at, x_at(NX - k), 1)

    def second(half, slot):
        up = slot < 3
        k, part = ((0, 0), (0, 1), (1, 0), (0, 1), (0, 0), (3, 1))[slot]
        step = 1 if up else 3
        device = {"fsdp_0": y_at(step)} if half == 0 else {"fsdp_1": x_at(step)}
        return remote(
            all_ref,
            half_line(half, k, part),
            s2_send.at[half, slot],
            s2_recv.at[half, slot],
            device,
        )

    def across(half, k):
        return remote(
            all_ref, line(half, k), p_send.at[half, k], p_recv.at[half, k], {"dp_1": 1 - c}
        )

    messages = [message(k) for k in range(1, NDP)]
    firsts = [[first(h, k) for k in range(1, 4)] for h in range(2)]
    seconds = [[second(h, slot) for slot in range(6)] for h in range(2)]
    acrosses = [[across(h, k) for k in range(4)] for h in range(2)]
    for m in messages:
        m.start()
    for k in (1, 0, 2):
        for h in range(2):
            firsts[h][k].start()
    for h in range(2):
        for f in firsts[h]:
            f.wait_recv()
        for slot in (0, 3, 1, 4):
            seconds[h][slot].start()
        acrosses[h][0].start()
    for slot in (0, 3):
        for h in range(2):
            seconds[h][slot].wait_recv()
            seconds[h][slot + 2].start()
    for slot in (1, 4):
        for h in range(2):
            seconds[h][slot].wait_recv()
            acrosses[h][1 if slot == 1 else 3].start()
    for h in range(2):
        seconds[h][2].wait_recv()
        seconds[h][5].wait_recv()
        acrosses[h][2].start()
    for m in messages:
        m.wait_recv()
    for h in range(2):
        for a in acrosses[h]:
            a.wait_recv()
    for group in [messages] + firsts + seconds + acrosses:
        for copy in group:
            copy.wait_send()


def split_three(value):
    high = value.astype(BF16)
    rest = value - high.astype(F32)
    middle = rest.astype(BF16)
    low = (rest - middle.astype(F32)).astype(BF16)
    return jnp.concatenate([high, middle, low], axis=0)


def joined_three(value, rows):
    return (value[2 * rows :] + value[rows : 2 * rows]) + value[:rows]


def compute_kernel(
    flips_ref,
    crops_ref,
    steps_ref,
    selected_ref,
    table_ref,
    got_ref,
    weights_ref,
    vae_ref,
    noise_ref,
    wp_ref,
    pos_ref,
    rates_ref,
    wt_ref,
    wa_ref,
    wf_ref,
    grads_ref,
    loss_ref,
    moments_ref,
    rows_ref,
    pads_ref,
    shift_ref,
    scale_ref,
    gate_ref,
    tok_ref,
    modt_ref,
    mod_ref,
    w2_ref,
    hid_ref,
    slope_ref,
    target_ref,
    gbt_ref,
    gb_ref,
    raw_ref,
    square_ref,
):
    lane = lax.broadcasted_iota(jnp.int32, (8, 128), 1)
    zero = jnp.zeros((8, 128), F32)

    for k in range(8):
        low = pltpu.roll(got_ref[2 * k], 96, 1)
        above = pltpu.roll(got_ref[2 * k + 2], 96, 1) if k < 7 else zero
        high = pltpu.roll(got_ref[2 * k + 1], 32, 1)
        below = pltpu.roll(got_ref[2 * k - 1], 32, 1) if k > 0 else zero
        four = jnp.where(lane < 96, low, above) + jnp.where(lane >= 32, high, below)
        for r in range(4):
            at = (4 * k + r) * 8
            rows_ref[at : at + 8, :] = pltpu.roll(four, 128 - 32 * r, 1) if r else four
    wide = lax.broadcasted_iota(jnp.int32, (SIDE, 128), 1) // SIDE
    halves = []
    for h in range(2):
        value = rows_ref[pl.ds(4 * h, SIDE, stride=8), :]
        for ch in range(1, 4):
            part = rows_ref[pl.ds(4 * h + ch, SIDE, stride=8), :]
            value = jnp.where(wide == ch, pltpu.roll(part, 32 * ch, 1), value)
        halves.append(value)
    by_channel = jnp.concatenate(halves, axis=1)
    source = lax.broadcasted_iota(jnp.int32, (256, 512), 0)
    goal = lax.broadcasted_iota(jnp.int32, (256, 512), 1)
    channel, column = source // SIDE, source % SIDE
    natural = column * 8 + channel
    apart = 256 + (channel // 4) * 128 + column * 4 + channel % 4
    spread = jnp.where((goal == natural) | (goal == apart), 1.0, 0.0).astype(BF16)
    placed = joined_three(
        jnp.dot(split_three(by_channel), spread, preferred_element_type=F32), SIDE
    )
    moments_ref[pl.ds(0, SIDE, stride=2), :] = placed[:, 0:128]
    moments_ref[pl.ds(1, SIDE, stride=2), :] = placed[:, 128:256]

    @pl.when(selected_ref[0, 0] != 1)
    def _():
        grads_ref[...] = jnp.zeros_like(grads_ref)
        loss_ref[...] = jnp.zeros_like(loss_ref)

    @pl.when(selected_ref[0, 0] == 1)
    def _():
        latent = placed[:, 256:384] + jnp.exp(0.5 * placed[:, 384:512]) * vae_ref[...]
        source = lax.broadcasted_iota(jnp.int32, (128, 128), 0)
        goal = lax.broadcasted_iota(jnp.int32, (128, 128), 1)
        maps = []
        for a in range(AUG):
            cell = goal // LC + crops_ref[1, a] - 2
            inside = (cell >= 0) & (cell < SIDE)
            mirror = (flips_ref[0, a] == 1).astype(jnp.int32)
            cell = cell + mirror * (SIDE - 1 - 2 * cell)
            match = inside & (source == cell * LC + goal % LC)
            maps.append(jnp.where(match, 1.0, 0.0).astype(BF16))
        columns = jnp.dot(
            split_three(latent), jnp.concatenate(maps, axis=1), preferred_element_type=F32
        )
        columns = joined_three(columns, SIDE)
        noised, noises = [], []
        for a in range(AUG):
            pads_ref[a] = jnp.zeros((40, 128), F32)
            pads_ref[a, 2 : 2 + SIDE, :] = columns[:, 128 * a : 128 * a + 128]
        for dr in range(2):
            for a in range(AUG):
                view = pads_ref[a, pl.ds(crops_ref[0, a] + dr, 16, stride=2), :]
                noise = noise_ref[pl.ds(dr * 4 + a, 16, stride=8), :]
                step = steps_ref[0, a]
                noised.append(table_ref[0, step] * view + table_ref[1, step] * noise)
                noises.append(noise)

        def patched(pieces):
            turned = jnp.concatenate(pieces, axis=0).T
            first, last = [], []
            for m in range(8):
                even = turned[16 * m : 16 * m + 8]
                odd = turned[16 * m + 8 : 16 * m + 16]
                first.append(jnp.where(lane < 64, even, pltpu.roll(odd, 64, 1)))
                last.append(jnp.where(lane < 64, pltpu.roll(even, 64, 1), odd))
            return jnp.concatenate(
                [jnp.concatenate(first, axis=1), jnp.concatenate(last, axis=1)], axis=0
            )

        patches = patched(noised).astype(BF16)
        target_ref[...] = patched(noises)

        which = lax.broadcasted_iota(jnp.int32, (96, TOK), 0)
        token = lax.broadcasted_iota(jnp.int32, (96, TOK), 1)
        cell = jnp.where(which < 48, token % 16, token // 64)
        marks = jnp.where(which % 16 == cell, 1.0, 0.0).astype(BF16)
        tok_ref[...] = lax.dot_general(
            jnp.concatenate([wp_ref[...], pos_ref[...]], axis=0),
            jnp.concatenate([patches, marks], axis=0),
            (((0,), (0,)), ((), ())),
            preferred_element_type=F32,
        )

        row = lax.broadcasted_iota(jnp.int32, (8, 128), 0)
        steps = jnp.zeros((8, 128), F32)
        for a in range(AUG):
            steps = jnp.where(row == a, steps_ref[0, a].astype(F32), steps)
        phases = steps * rates_ref[...]
        stamp = jnp.concatenate([jnp.cos(phases), jnp.sin(phases)], axis=1).astype(BF16)
        raw = jnp.dot(stamp, wt_ref[...], preferred_element_type=F32)
        conditioning = (raw * (1.0 / (1.0 + jnp.exp(-raw)))).astype(BF16)
        modulation = jnp.dot(conditioning, wa_ref[...], preferred_element_type=F32)
        views = [jnp.broadcast_to(modulation[a : a + 1], (16, 3 * D)) for a in range(AUG)]
        turned = jnp.concatenate(views + views, axis=0).T
        shift_ref[...] = turned[:D]
        scale_ref[...] = 1.0 + turned[D : 2 * D]
        gate_ref[...] = turned[2 * D :]

        @pl.loop(0, TOK // 128)
        def _(m):
            at = pl.ds(pl.multiple_of(m * 128, 128), 128)
            value = tok_ref[:, at]
            center = value - jnp.sum(value, axis=0, keepdims=True) * (1.0 / D)
            variance = jnp.sum(center * center, axis=0, keepdims=True) * (1.0 / D)
            normed = center * lax.rsqrt(variance + norm_epsilon)
            out = normed * scale_ref[...] + shift_ref[...]
            modt_ref[:, at] = out.astype(BF16)
            mod_ref[at, :] = out.T.astype(BF16)

        @pl.loop(0, FF // 128)
        def _(m):
            at = pl.ds(pl.multiple_of(m * 128, 128), 128)
            w2_ref[:, at] = weights_ref[1, at, :].astype(F32).T.astype(BF16)

        root = math.sqrt(2.0 / math.pi)

        @pl.loop(0, FF // CHUNK)
        def _(f):
            at = pl.ds(pl.multiple_of(f * CHUNK, CHUNK), CHUNK)
            pre = jnp.dot(weights_ref[0, at, :], modt_ref[...], preferred_element_type=F32)
            squared = pre * pre
            inner = pre * (squared * (root * 0.044715) + root)
            share = 0.5 * jnp.tanh(inner) + 0.5
            hidden = pre * share
            hid_ref[at, :] = hidden.astype(BF16)
            slope = (1.0 - share) * hidden * (squared * (6.0 * root * 0.044715) + 2.0 * root)
            slope_ref[at, :] = slope + share

        loss_ref[...] = jnp.zeros_like(loss_ref)

        @pl.loop(0, TOK // 256)
        def _(m):
            at = pl.ds(pl.multiple_of(m * 256, 256), 256)
            branch = jnp.dot(w2_ref[...], hid_ref[:, at], preferred_element_type=F32)
            gate = jnp.concatenate([gate_ref[...], gate_ref[...]], axis=1)
            mixed = tok_ref[:, at] + gate * branch
            center = mixed - jnp.sum(mixed, axis=0, keepdims=True) * (1.0 / D)
            variance = jnp.sum(center * center, axis=0, keepdims=True) * (1.0 / D)
            inverse = lax.rsqrt(variance + norm_epsilon)
            normed = center * inverse
            predicted = jnp.dot(wf_ref[...], normed.astype(BF16), preferred_element_type=F32)
            residue = predicted - target_ref[:, at]
            loss_ref[...] += jnp.sum(residue * residue) * (1.0 / (TOK * 16))
            grad_pred = (residue * (2.0 / (TOK * 16))).astype(BF16)
            grad_normed = lax.dot_general(
                wf_ref[...], grad_pred, (((0,), (0,)), ((), ())), preferred_element_type=F32
            )
            mean = jnp.sum(grad_normed, axis=0, keepdims=True) * (1.0 / D)
            along = jnp.sum(grad_normed * normed, axis=0, keepdims=True) * (1.0 / D)
            grad_mixed = inverse * (grad_normed - mean - normed * along)
            grad_branch = gate * grad_mixed
            gbt_ref[:, at] = grad_branch.astype(BF16)
            gb_ref[at, :] = grad_branch.T.astype(BF16)

        square_ref[...] = jnp.zeros_like(square_ref)

        @pl.loop(0, FF // CHUNK)
        def _(f):
            at = pl.ds(pl.multiple_of(f * CHUNK, CHUNK), CHUNK)
            grad_hidden = jnp.dot(
                weights_ref[1, at, :], gbt_ref[...], preferred_element_type=F32
            )
            grad_pre = (slope_ref[at, :] * grad_hidden).astype(BF16)
            grad_1 = jnp.dot(grad_pre, mod_ref[...], preferred_element_type=F32)
            grad_2 = jnp.dot(hid_ref[at, :], gb_ref[...], preferred_element_type=F32)
            raw_ref[0, at, :] = grad_1
            raw_ref[1, at, :] = grad_2
            square_ref[...] += jnp.sum(
                grad_1 * grad_1 + grad_2 * grad_2, axis=0, keepdims=True
            )

        total = jnp.sum(square_ref[...], axis=1, keepdims=True)
        factor = 1.0 / (jnp.sqrt(total * (1.0 / (2 * D * FF))) + clip_offset)

        @pl.loop(0, FF // CHUNK)
        def _(f):
            at = pl.ds(pl.multiple_of(f * CHUNK, CHUNK), CHUNK)
            for w in range(2):
                grads_ref[w, at, :] = (raw_ref[w, at, :] * factor).astype(BF16)


def reduce_kernel(g_ref, loss_ref, sum_ref, total_ref, *scratch):
    (r0, s1, r1, acc, c2, r2, tiles, r3, whole, l0, l1, l2) = scratch[:12]
    (q_send, q_recv, s1_send, s1_recv, s2_send, s2_recv, z_send, z_recv) = scratch[12:20]
    (a_send, a_recv, f_send, f_recv, l_send, l_recv) = scratch[20:]
    z, c, y, x = place()
    partner = {"dp_1": 1 - c}

    def x_at(k):
        return lax.rem(x + k, NX)

    def y_at(k):
        return lax.rem(y + k, NY)

    def z_at(k):
        return lax.rem(z + k, NZ)

    barrier = pltpu.get_barrier_semaphore()
    pl.semaphore_signal(barrier, 1, device_id=partner, device_id_type=MESH)
    for k in range(1, NX):
        pl.semaphore_signal(barrier, 1, device_id={"fsdp_1": x_at(k)}, device_id_type=MESH)
        pl.semaphore_signal(barrier, 1, device_id={"fsdp_0": y_at(k)}, device_id_type=MESH)
    for k in range(1, NZ):
        pl.semaphore_signal(barrier, 1, device_id={"dp_0": z_at(k)}, device_id_type=MESH)
    l0[0] = loss_ref[...]
    pl.semaphore_wait(barrier, 1 + NX - 1 + NY - 1 + NZ - 1)

    def remote(src, dst, send, recv, device):
        return pltpu.make_async_remote_copy(
            src_ref=src,
            dst_ref=dst,
            send_sem=send,
            recv_sem=recv,
            device_id=device,
            device_id_type=MESH,
        )

    def piece(half, k):
        if half == 0:
            return (slice(None), x_at(k), 0)
        return (y_at(k), slice(None), 1)

    def part(half, k, j):
        if half == 0:
            return (j, x_at(k), 0)
        return (y_at(k), j, 1)

    def first_to(half, k):
        return {"fsdp_1": x_at(k)} if half == 0 else {"fsdp_0": y_at(k)}

    def second_to(half, k):
        return {"fsdp_0": y_at(k)} if half == 0 else {"fsdp_1": x_at(k)}

    def second_at(half, k):
        return y_at(k) if half == 0 else x_at(k)

    loss_0 = remote(l0.at[0], l0.at[1], l_send.at[0], l_recv.at[0], partner)
    loss_0.start()
    swaps = {}
    for k in (2, 1, 3, 0):
        for h in range(2):
            at = piece(h, k)
            swaps[h, k] = remote(
                g_ref.at[(1 - c,) + at], r0.at[at], q_send.at[h, k], q_recv.at[h, k], partner
            )
            swaps[h, k].start()
    firsts = {}

    def first(h, slot, src):
        firsts[h, slot] = remote(
            src,
            r1.at[h, slot],
            s1_send.at[h, slot],
            s1_recv.at[h, slot],
            first_to(h, 1 if slot < 3 else 3),
        )
        firsts[h, slot].start()

    def own(h, k, j):
        at = part(h, k, j)
        return g_ref[(c,) + at].astype(F32) + r0[at].astype(F32)

    for h in range(2):
        swaps[h, 2].wait_recv()
        for j in range(4):
            s1[h, 1, j] = own(h, 2, j).astype(BF16)
        first(h, 0, s1.at[h, 1, pl.ds(0, 2)])
        first(h, 3, s1.at[h, 1, pl.ds(2, 2)])
    for k, slot, low in ((1, 1, 2), (3, 4, 0)):
        for h in range(2):
            swaps[h, k].wait_recv()
            for j in (low, low + 1):
                s1[h, k - 1, j] = own(h, k, j).astype(BF16)
            first(h, slot, s1.at[h, k - 1, pl.ds(low, 2)])
    for k, slot, low in ((1, 0, 0), (3, 3, 2)):
        for h in range(2):
            firsts[h, slot].wait_recv()
            for i in range(2):
                j = low + i
                s1[h, k - 1, j] = (own(h, k, j) + r1[h, slot, i].astype(F32)).astype(BF16)
            first(h, slot + 2, s1.at[h, k - 1, pl.ds(low, 2)])
    for h in range(2):
        swaps[h, 0].wait_recv()
        for j in range(4):
            acc[h, j] = own(h, 0, j)
    loss_0.wait_recv()
    l1[x] = l0[0] + l0[1]
    losses = [loss_0]
    for k in range(1, NX):
        copy = remote(l1.at[x], l1.at[x], l_send.at[k], l_recv.at[k], {"fsdp_1": x_at(k)})
        copy.start()
        losses.append(copy)
    seconds = {}
    quarter = HALF // 2

    def second(h, slot, src):
        seconds[h, slot] = remote(
            src,
            r2.at[h, slot],
            s2_send.at[h, slot],
            s2_recv.at[h, slot],
            second_to(h, 1 if slot < 3 else 3),
        )
        seconds[h, slot].start()

    def rows(part):
        return pl.ds(part * quarter, quarter)

    for h in range(2):
        for slot in (4, 1, 2, 5):
            firsts[h, slot].wait_recv()
        for j in range(4):
            a, b = (2, 4) if j < 2 else (1, 5)
            acc[h, j] += r1[h, a, j % 2].astype(F32) + r1[h, b, j % 2].astype(F32)
        far, up, down = second_at(h, 2), second_at(h, 1), second_at(h, 3)
        second(h, 0, acc.at[h, far, rows(0)])
        second(h, 3, acc.at[h, far, rows(1)])
        second(h, 1, acc.at[h, up, rows(1)])
        second(h, 4, acc.at[h, down, rows(0)])
    for copy in losses[1:]:
        copy.wait_recv()
    l2[y] = (l1[0] + l1[1]) + (l1[2] + l1[3])
    for k in range(1, NY):
        copy = remote(
            l2.at[y], l2.at[y], l_send.at[3 + k], l_recv.at[3 + k], {"fsdp_0": y_at(k)}
        )
        copy.start()
        losses.append(copy)
    for slot, k, side in ((0, 1, 0), (3, 3, 1)):
        for h in range(2):
            seconds[h, slot].wait_recv()
            c2[h, side] = acc[h, second_at(h, k), rows(side), :] + r2[h, slot]
            second(h, slot + 2, c2.at[h, side])
    for h in range(2):
        for slot in (1, 4, 2, 5):
            seconds[h, slot].wait_recv()
        j = second_at(h, 0)
        value = jnp.concatenate(
            [
                acc[h, j, rows(0), :] + (r2[h, 2] + r2[h, 4]),
                acc[h, j, rows(1), :] + (r2[h, 1] + r2[h, 5]),
            ],
            axis=0,
        )
        for i in range(HALF // 8):
            for n in range(D // 128):
                t = (h * (HALF // 8) + i) * (D // 128) + n
                tiles[t // PIECE, t % PIECE] = value[8 * i : 8 * i + 8, 128 * n : 128 * n + 128]
    for copy in losses[4:]:
        copy.wait_recv()
    at = USED_TILES
    tiles[at // PIECE, at % PIECE] = (l2[0] + l2[1]) + (l2[2] + l2[3])
    for t in range(USED_TILES + 1, TILES):
        tiles[t // PIECE, t % PIECE] = jnp.zeros((8, 128), F32)

    order = (4, 3, 5, 2, 6, 1, 7)
    thirds = []
    for k in order:
        copy = remote(
            tiles.at[z_at(k)], r3.at[z], z_send.at[k], z_recv.at[k], {"dp_0": z_at(k)}
        )
        copy.start()
        thirds.append(copy)
    r3[z] = tiles[z]
    for copy in thirds:
        copy.wait_recv()
    value = r3[0]
    for k in range(1, NZ):
        value = value + r3[k]
    whole[c, z] = value
    spreads = {}
    for k in order:
        spreads[k] = remote(
            whole.at[c, z], whole.at[c, z], a_send.at[k], a_recv.at[k], {"dp_0": z_at(k)}
        )
        spreads[k].start()
    crossings = []
    for k in (0, 7, 1, 6, 2, 5, 3, 4):
        if k > 0:
            spreads[k].wait_recv()
        at = z_at(NZ - k) if k > 0 else z
        copy = remote(whole.at[c, at], whole.at[c, at], f_send.at[k], f_recv.at[k], partner)
        copy.start()
        crossings.append(copy)
    for copy in crossings:
        copy.wait_recv()
    for w in range(2):
        for t in range(USED_TILES):
            i, n = t // (D // 128), t % (D // 128)
            sum_ref[w, 8 * i : 8 * i + 8, 128 * n : 128 * n + 128] = whole[
                w, t // PIECE, t % PIECE
            ]
    total_ref[...] = whole[0, USED_TILES // PIECE, USED_TILES % PIECE]
    for group in (swaps, firsts, seconds, spreads):
        for copy in group.values():
            copy.wait_send()
    for group in (losses, thirds, crossings):
        for copy in group:
            copy.wait_send()


def finish_kernel(sum_ref, total_ref, n1_ref, n2_ref, u1_ref, u2_ref, mean_ref):
    u1_ref[...] = (sum_ref[0] + noise_weight * n1_ref[...]) * (1.0 / SELECTED)
    u2_ref[...] = (sum_ref[1] + noise_weight * n2_ref[...]) * (1.0 / SELECTED)
    mean_ref[...] = total_ref[0:1, 0:1] * (1.0 / SELECTED)


def per_device(
    features,
    conv_weight,
    vae_noise,
    flips,
    crops,
    tsteps,
    diffusion_noise,
    selected,
    w_patch,
    w_time,
    w_ada,
    w_fc1,
    w_fc2,
    w_final,
    noise_fc1,
    noise_fc2,
):
    dma = pltpu.SemaphoreType.DMA
    pixels = features.reshape(TOK, FCH)
    taps = conv_weight.transpose(0, 1, 3, 2).reshape(72, FCH)
    messages = pl.pallas_call(
        conv_kernel,
        out_shape=jax.ShapeDtypeStruct((NDP, 8, 128), F32),
        in_specs=[VMEM_SPEC] * 2,
        out_specs=VMEM_SPEC,
        name="conv",
    )(pixels, taps)
    gathered, received = pl.pallas_call(
        gather_kernel,
        out_shape=(
            jax.ShapeDtypeStruct((2, NY, NX, 2, HALF, D), BF16),
            jax.ShapeDtypeStruct((NDP, 8, 128), F32),
        ),
        in_specs=[VMEM_SPEC] * 3,
        out_specs=(VMEM_SPEC, VMEM_SPEC),
        scratch_shapes=[dma((2, 4))] * 2
        + [dma((2, 6))] * 2
        + [dma((2, 4))] * 2
        + [dma((NDP,))] * 2,
        compiler_params=pltpu.CompilerParams(collective_id=0, has_side_effects=True),
        name="gather",
    )(w_fc1.T, w_fc2.T, messages)
    weights = gathered.reshape(2, FF, D)
    views = diffusion_noise.reshape(AUG, SIDE, SIDE * LC).transpose(1, 0, 2)
    grads, loss, moments = pl.pallas_call(
        compute_kernel,
        out_shape=(
            jax.ShapeDtypeStruct((2, FF, D), BF16),
            jax.ShapeDtypeStruct((8, 128), F32),
            jax.ShapeDtypeStruct((2 * SIDE, 128), F32),
        ),
        in_specs=[SMEM_SPEC] * 5 + [VMEM_SPEC] * 10,
        out_specs=(VMEM_SPEC,) * 3,
        scratch_shapes=[
            pltpu.VMEM((256, 128), F32),
            pltpu.VMEM((AUG, 40, 128), F32),
            pltpu.VMEM((D, 128), F32),
            pltpu.VMEM((D, 128), F32),
            pltpu.VMEM((D, 128), F32),
            pltpu.VMEM((D, TOK), F32),
            pltpu.VMEM((D, TOK), BF16),
            pltpu.VMEM((TOK, D), BF16),
            pltpu.VMEM((D, FF), BF16),
            pltpu.VMEM((FF, TOK), BF16),
            pltpu.VMEM((FF, TOK), F32),
            pltpu.VMEM((16, TOK), F32),
            pltpu.VMEM((D, TOK), BF16),
            pltpu.VMEM((TOK, D), BF16),
            pltpu.VMEM((2, FF, D), F32),
            pltpu.VMEM((1, D), F32),
        ],
        compiler_params=pltpu.CompilerParams(vmem_limit_bytes=56 << 20),
        name="example",
    )(
        flips.reshape(1, AUG),
        crops.reshape(AUG, 2).T,
        tsteps.reshape(1, AUG),
        selected,
        jnp.asarray(blend_tables()),
        received,
        weights,
        vae_noise.reshape(SIDE, SIDE * LC),
        views.reshape(SIDE * AUG, SIDE * LC),
        w_patch,
        jnp.asarray(position_rows()),
        jnp.asarray(time_rates()),
        w_time,
        w_ada,
        w_final.T,
    )
    sums, total = pl.pallas_call(
        reduce_kernel,
        out_shape=(
            jax.ShapeDtypeStruct((2, SHARD, D), F32),
            jax.ShapeDtypeStruct((8, 128), F32),
        ),
        in_specs=[VMEM_SPEC] * 2,
        out_specs=(VMEM_SPEC, VMEM_SPEC),
        scratch_shapes=[
            pltpu.VMEM((NY, NX, 2, HALF, D), BF16),
            pltpu.VMEM((2, 3, 4, HALF, D), BF16),
            pltpu.VMEM((2, 6, 2, HALF, D), BF16),
            pltpu.VMEM((2, 4, HALF, D), F32),
            pltpu.VMEM((2, 2, HALF // 2, D), F32),
            pltpu.VMEM((2, 6, HALF // 2, D), F32),
            pltpu.VMEM((NZ, PIECE, 8, 128), F32),
            pltpu.VMEM((NZ, PIECE, 8, 128), F32),
            pltpu.VMEM((2, NZ, PIECE, 8, 128), F32),
            pltpu.VMEM((2, 8, 128), F32),
            pltpu.VMEM((NX, 8, 128), F32),
            pltpu.VMEM((NY, 8, 128), F32),
        ]
        + [dma((2, 4))] * 2
        + [dma((2, 6))] * 4
        + [dma((NZ,))] * 8,
        compiler_params=pltpu.CompilerParams(collective_id=1, has_side_effects=True),
        name="reduce",
    )(grads.reshape(2, NY, NX, 2, HALF, D), loss)
    update_1, update_2, mean_loss = pl.pallas_call(
        finish_kernel,
        out_shape=(
            jax.ShapeDtypeStruct((SHARD, D), F32),
            jax.ShapeDtypeStruct((SHARD, D), F32),
            jax.ShapeDtypeStruct((1, 1), F32),
        ),
        in_specs=[VMEM_SPEC] * 4,
        out_specs=(VMEM_SPEC,) * 3,
        name="finish",
    )(sums, total, noise_fc1.T, noise_fc2.T)
    return (update_1.T, update_2.T, mean_loss.reshape(()), moments.reshape(1, 1, -1))


def solution(mesh):
    split = Mesh(mesh.devices.reshape(NZ, NC, NY, NX), DP + FSDP)
    return jax.shard_map(
        per_device,
        mesh=split,
        in_specs=(
            P(FSDP, None, DP, None, None),
            P(),
            P(DP, FSDP, None),
            P(DP, FSDP, None),
            P(DP, FSDP, None, None),
            P(DP, FSDP, None),
            P(DP, FSDP, None, None),
            P(DP, FSDP),
            P(),
            P(),
            P(),
            P(None, FSDP),
            P(None, FSDP),
            P(),
            P(None, FSDP),
            P(None, FSDP),
        ),
        out_specs=(P(None, FSDP), P(None, FSDP), P(), P(DP, FSDP, None)),
        check_vma=False,
    )
```

```python
import math

import jax
import jax.numpy as jnp
import ml_dtypes
import numpy as np
from jax import lax
from jax.experimental import pallas as pl
from jax.experimental.pallas import tpu as pltpu
from jax.sharding import Mesh
from jax.sharding import PartitionSpec as P

MESH = pl.DeviceIdType.MESH
DP = ("dp_0", "dp_1")
FSDP = ("fsdp_0", "fsdp_1")
NZ, NC, NY, NX = 8, 2, 4, 4
NDP = NZ * NC
D, FF, TOK, FCH = 384, 1536, 1024, 512
SHARD = FF // (NY * NX)
HALF = SHARD // 2
SIDE, LC, AUG, TSTEPS = 32, 4, 4, 1000
SELECTED = 128
CHUNK = 384
PIECE = 5
TILES = NZ * PIECE
USED_TILES = (SHARD // 8) * (D // 128)
clip_offset = 1e-05
noise_weight = 16.0
norm_epsilon = 1e-06
VMEM_SPEC = pl.BlockSpec(memory_space=pltpu.VMEM)
ANY_SPEC = pl.BlockSpec(memory_space=pl.ANY)
SMEM_SPEC = pl.BlockSpec(memory_space=pltpu.SMEM)
F32, BF16 = jnp.float32, jnp.bfloat16


def three_parts(table):
    high = table.astype(np.float32).astype(ml_dtypes.bfloat16)
    rest = table.astype(np.float32) - high.astype(np.float32)
    middle = rest.astype(ml_dtypes.bfloat16)
    low = (rest - middle.astype(np.float32)).astype(ml_dtypes.bfloat16)
    return high, middle, low


def position_rows():
    side, quarter = SIDE // 2, D // 4
    frequency = 1.0 / 10000.0 ** (np.arange(quarter) / quarter)
    angles = np.arange(side)[:, None] * frequency[None, :]
    line = np.concatenate([np.sin(angles), np.cos(angles)], axis=1)
    parts = three_parts(line)
    zero = np.zeros_like(parts[0])
    rows = [np.concatenate([p, zero], axis=1) for p in parts]
    cols = [np.concatenate([zero, p], axis=1) for p in parts]
    return np.concatenate(rows + cols, axis=0)


def blend_tables():
    beta = 0.0001 + np.arange(TSTEPS) * (0.02 - 0.0001) / (TSTEPS - 1)
    alpha_bar = np.cumprod(1.0 - beta)
    return np.stack([np.sqrt(alpha_bar), np.sqrt(1.0 - alpha_bar)]).astype(np.float32)


def time_rates():
    steps = np.arange(128, dtype=np.float32)
    scaled = np.float32(-math.log(10000.0)) * steps / np.float32(128)
    return np.exp(scaled).astype(np.float32).reshape(1, 128)


def place():
    return tuple(lax.axis_index(a) for a in ("dp_0", "dp_1", "fsdp_0", "fsdp_1"))


def split_three(value):
    high = value.astype(BF16)
    rest = value - high.astype(F32)
    middle = rest.astype(BF16)
    low = (rest - middle.astype(F32)).astype(BF16)
    return jnp.concatenate([high, middle, low], axis=0)


def joined_three(value, rows):
    return (value[2 * rows :] + value[rows : 2 * rows]) + value[:rows]


def step_kernel(
    flips_ref,
    crops_ref,
    steps_ref,
    selected_ref,
    table_ref,
    x_ref,
    taps_ref,
    w1_ref,
    w2s_ref,
    vae_ref,
    noise_ref,
    wp_ref,
    pos_ref,
    rates_ref,
    wt_ref,
    wa_ref,
    wf_ref,
    sum_ref,
    total_ref,
    moments_ref,
    *scratch,
):
    (x_buf, wt_buf, wa_buf, all_ref, msg_ref, got_ref) = scratch[:6]
    (rows_ref, pads_ref, shift_ref, scale_ref, gate_ref, tok_ref, modt_ref) = scratch[6:13]
    (mod_ref, w2_ref, hid_ref, slope_ref, target_ref, gbt_ref, gb_ref) = scratch[13:20]
    (square_ref, own_ref, keep_ref, send_ref, r0, s1, r1, acc, r2) = scratch[20:29]
    (tiles, r3, whole, l1, l2) = scratch[29:34]
    (g1_send, g1_recv, g2_send, g2_recv, p_send, p_recv) = scratch[34:40]
    (s1_send, s1_recv, s2_send, s2_recv) = scratch[40:44]
    (m_send, m_recv, q_send, q_recv, z_send, z_recv) = scratch[44:50]
    (a_send, a_recv, f_send, f_recv, l_send, l_recv, c_sem) = scratch[50:]
    z, c, y, x = place()
    me = z * NC + c
    partner = {"dp_1": 1 - c}
    lane = lax.broadcasted_iota(jnp.int32, (8, 128), 1)
    zero = jnp.zeros((8, 128), F32)

    def x_at(k):
        return lax.rem(x + k, NX)

    def y_at(k):
        return lax.rem(y + k, NY)

    def z_at(k):
        return lax.rem(z + k, NZ)

    def dp_at(k):
        return lax.rem(me + k, NDP)

    def dp_device(k):
        other = dp_at(k)
        return {"dp_0": other // NC, "dp_1": lax.rem(other, NC)}

    def remote(src, dst, send, recv, device):
        return pltpu.make_async_remote_copy(
            src_ref=src,
            dst_ref=dst,
            send_sem=send,
            recv_sem=recv,
            device_id=device,
            device_id_type=MESH,
        )

    def first_to(half, k):
        return {"fsdp_1": x_at(k)} if half == 0 else {"fsdp_0": y_at(k)}

    def second_to(half, k):
        return {"fsdp_0": y_at(k)} if half == 0 else {"fsdp_1": x_at(k)}

    def second_at(half, k):
        return y_at(k) if half == 0 else x_at(k)

    barrier = pltpu.get_barrier_semaphore()
    for k in range(1, NX):
        pl.semaphore_signal(barrier, 1, device_id={"fsdp_1": x_at(k)}, device_id_type=MESH)
        pl.semaphore_signal(barrier, 1, device_id={"fsdp_0": y_at(k)}, device_id_type=MESH)
    for k in range(1, NDP):
        pl.semaphore_signal(barrier, 1, device_id=dp_device(k), device_id_type=MESH)
    x_copy = pltpu.make_async_copy(x_ref, x_buf, c_sem.at[0])
    wt_copy = pltpu.make_async_copy(wt_ref, wt_buf, c_sem.at[1])
    wa_copy = pltpu.make_async_copy(wa_ref, wa_buf, c_sem.at[2])
    x_copy.start()
    wt_copy.start()
    wa_copy.start()
    own_shard = jnp.where(c == 0, w1_ref[...], w2s_ref[...])
    all_ref[c, y, x, 0] = own_shard[:HALF]
    all_ref[c, y, x, 1] = own_shard[HALF:]
    pl.semaphore_wait(barrier, NX - 1 + NY - 1 + NDP - 1)

    def message(k):
        return remote(
            msg_ref.at[dp_at(k)], got_ref.at[me], m_send.at[k], m_recv.at[k], dp_device(k)
        )

    def gather_first(half, k):
        at = all_ref.at[c, y, x, half]
        return remote(at, at, g1_send.at[half, k], g1_recv.at[half, k], first_to(half, k))

    def line(half, k):
        if half == 0:
            return all_ref.at[c, y_at(NY - k), :, 0]
        return all_ref.at[c, :, x_at(NX - k), 1]

    def gather_second(half, k):
        at = line(half, 0)
        return remote(at, at, g2_send.at[half, k], g2_recv.at[half, k], second_to(half, k))

    def across(half, k):
        at = line(half, k)
        return remote(at, at, p_send.at[half, k], p_recv.at[half, k], partner)

    messages = [message(k) for k in range(1, NDP)]
    early = {(h, k): gather_first(h, k) for k in (1, 3, 2) for h in range(2)}
    late = {(h, k): gather_second(h, k) for k in (1, 3, 2) for h in range(2)}
    crossed = {(h, k): across(h, k) for k in (0, 1, 3, 2) for h in range(2)}
    for copy in early.values():
        copy.start()
    x_copy.wait()
    taps = lax.dot_general(
        taps_ref[...], x_buf[...], (((1,), (1,)), ((), ())), preferred_element_type=F32
    )
    col = lane % SIDE

    def tap(dy, dx, v):
        at = (dy * 3 + dx) * 8
        return taps[at : at + 8, 128 * v : 128 * v + 128]

    for v in range(8):
        rows = []
        for dy in range(3):
            left = jnp.where(col == 0, zero, pltpu.roll(tap(dy, 0, v), 1, 1))
            right = jnp.where(col == SIDE - 1, zero, pltpu.roll(tap(dy, 2, v), 127, 1))
            rows.append(left + tap(dy, 1, v) + right)
        for odd in range(2):
            parts = [pltpu.roll(r, 64, 1) if odd else r for r in rows]
            parts = [jnp.where(lane < 64, r, zero) for r in parts]
            msg_ref[2 * v + odd] = (
                parts[2] + pltpu.roll(parts[1], 32, 1) + pltpu.roll(parts[0], 64, 1)
            )
    got_ref[me] = msg_ref[me]
    for m in messages:
        m.start()
    for copy in early.values():
        copy.wait_recv()
    for copy in late.values():
        copy.start()
    for h in range(2):
        crossed[h, 0].start()
    wt_copy.wait()
    wa_copy.wait()

    row = lax.broadcasted_iota(jnp.int32, (8, 128), 0)
    steps = jnp.zeros((8, 128), F32)
    for a in range(AUG):
        steps = jnp.where(row == a, steps_ref[0, a].astype(F32), steps)
    phases = steps * rates_ref[...]
    stamp = jnp.concatenate([jnp.cos(phases), jnp.sin(phases)], axis=1).astype(BF16)
    raw = jnp.dot(stamp, wt_buf[...], preferred_element_type=F32)
    conditioning = (raw * (1.0 / (1.0 + jnp.exp(-raw)))).astype(BF16)
    modulation = jnp.dot(conditioning, wa_buf[...], preferred_element_type=F32)
    views = [jnp.broadcast_to(modulation[a : a + 1], (16, 3 * D)) for a in range(AUG)]
    turned = jnp.concatenate(views + views, axis=0).T
    shift_ref[...] = turned[:D]
    scale_ref[...] = 1.0 + turned[D : 2 * D]
    gate_ref[...] = turned[2 * D :]

    for m in messages:
        m.wait_recv()
    for k in range(8):
        low = pltpu.roll(got_ref[2 * k], 96, 1)
        above = pltpu.roll(got_ref[2 * k + 2], 96, 1) if k < 7 else zero
        high = pltpu.roll(got_ref[2 * k + 1], 32, 1)
        below = pltpu.roll(got_ref[2 * k - 1], 32, 1) if k > 0 else zero
        four = jnp.where(lane < 96, low, above) + jnp.where(lane >= 32, high, below)
        for r in range(4):
            at = (4 * k + r) * 8
            rows_ref[at : at + 8, :] = pltpu.roll(four, 128 - 32 * r, 1) if r else four
    wide = lax.broadcasted_iota(jnp.int32, (SIDE, 128), 1) // SIDE
    halves = []
    for h in range(2):
        value = rows_ref[pl.ds(4 * h, SIDE, stride=8), :]
        for ch in range(1, 4):
            part = rows_ref[pl.ds(4 * h + ch, SIDE, stride=8), :]
            value = jnp.where(wide == ch, pltpu.roll(part, 32 * ch, 1), value)
        halves.append(value)
    by_channel = jnp.concatenate(halves, axis=1)
    source = lax.broadcasted_iota(jnp.int32, (256, 512), 0)
    goal = lax.broadcasted_iota(jnp.int32, (256, 512), 1)
    channel, column = source // SIDE, source % SIDE
    natural = column * 8 + channel
    apart = 256 + (channel // 4) * 128 + column * 4 + channel % 4
    spread = jnp.where((goal == natural) | (goal == apart), 1.0, 0.0).astype(BF16)
    placed = joined_three(
        jnp.dot(split_three(by_channel), spread, preferred_element_type=F32), SIDE
    )
    moments_ref[pl.ds(0, SIDE, stride=2), :] = placed[:, 0:128]
    moments_ref[pl.ds(1, SIDE, stride=2), :] = placed[:, 128:256]

    latent = placed[:, 256:384] + jnp.exp(0.5 * placed[:, 384:512]) * vae_ref[...]
    source = lax.broadcasted_iota(jnp.int32, (128, 128), 0)
    goal = lax.broadcasted_iota(jnp.int32, (128, 128), 1)
    maps = []
    for a in range(AUG):
        cell = goal // LC + crops_ref[1, a] - 2
        inside = (cell >= 0) & (cell < SIDE)
        mirror = (flips_ref[0, a] == 1).astype(jnp.int32)
        cell = cell + mirror * (SIDE - 1 - 2 * cell)
        match = inside & (source == cell * LC + goal % LC)
        maps.append(jnp.where(match, 1.0, 0.0).astype(BF16))
    columns = jnp.dot(
        split_three(latent), jnp.concatenate(maps, axis=1), preferred_element_type=F32
    )
    columns = joined_three(columns, SIDE)
    noised, noises = [], []
    for a in range(AUG):
        pads_ref[a] = jnp.zeros((40, 128), F32)
        pads_ref[a, 2 : 2 + SIDE, :] = columns[:, 128 * a : 128 * a + 128]
    for dr in range(2):
        for a in range(AUG):
            view = pads_ref[a, pl.ds(crops_ref[0, a] + dr, 16, stride=2), :]
            noise = noise_ref[pl.ds(dr * 4 + a, 16, stride=8), :]
            step = steps_ref[0, a]
            noised.append(table_ref[0, step] * view + table_ref[1, step] * noise)
            noises.append(noise)

    def patched(pieces):
        turned = jnp.concatenate(pieces, axis=0).T
        first, last = [], []
        for m in range(8):
            even = turned[16 * m : 16 * m + 8]
            odd = turned[16 * m + 8 : 16 * m + 16]
            first.append(jnp.where(lane < 64, even, pltpu.roll(odd, 64, 1)))
            last.append(jnp.where(lane < 64, pltpu.roll(even, 64, 1), odd))
        return jnp.concatenate(
            [jnp.concatenate(first, axis=1), jnp.concatenate(last, axis=1)], axis=0
        )

    patches = patched(noised).astype(BF16)
    target_ref[...] = patched(noises)

    which = lax.broadcasted_iota(jnp.int32, (96, TOK), 0)
    token = lax.broadcasted_iota(jnp.int32, (96, TOK), 1)
    cell = jnp.where(which < 48, token % 16, token // 64)
    marks = jnp.where(which % 16 == cell, 1.0, 0.0).astype(BF16)
    tok_ref[...] = lax.dot_general(
        jnp.concatenate([wp_ref[...], pos_ref[...]], axis=0),
        jnp.concatenate([patches, marks], axis=0),
        (((0,), (0,)), ((), ())),
        preferred_element_type=F32,
    )

    for k in (1, 3):
        for h in range(2):
            late[h, k].wait_recv()
            crossed[h, k].start()

    @pl.loop(0, TOK // 128)
    def _(m):
        at = pl.ds(pl.multiple_of(m * 128, 128), 128)
        value = tok_ref[:, at]
        center = value - jnp.sum(value, axis=0, keepdims=True) * (1.0 / D)
        variance = jnp.sum(center * center, axis=0, keepdims=True) * (1.0 / D)
        normed = center * lax.rsqrt(variance + norm_epsilon)
        out = normed * scale_ref[...] + shift_ref[...]
        modt_ref[:, at] = out.astype(BF16)
        mod_ref[at, :] = out.T.astype(BF16)

    for k in (2,):
        for h in range(2):
            late[h, k].wait_recv()
            crossed[h, k].start()

    for copy in crossed.values():
        copy.wait_recv()
    flat_weights = all_ref.reshape(2, FF, D)

    def weights(w, at):
        return flat_weights[w, at, :]

    @pl.loop(0, FF // 128)
    def _(m):
        at = pl.ds(pl.multiple_of(m * 128, 128), 128)
        w2_ref[:, at] = weights(1, at).astype(F32).T.astype(BF16)

    root = math.sqrt(2.0 / math.pi)

    @pl.loop(0, FF // CHUNK)
    def _(f):
        at = pl.ds(pl.multiple_of(f * CHUNK, CHUNK), CHUNK)
        pre = jnp.dot(weights(0, at), modt_ref[...], preferred_element_type=F32)
        squared = pre * pre
        inner = pre * (squared * (root * 0.044715) + root)
        share = 0.5 * jnp.tanh(inner) + 0.5
        hidden = pre * share
        hid_ref[at, :] = hidden.astype(BF16)
        slope = (1.0 - share) * hidden * (squared * (6.0 * root * 0.044715) + 2.0 * root)
        slope_ref[at, :] = slope + share

    own_ref[1] = jnp.zeros((8, 128), F32)

    @pl.loop(0, TOK // 256)
    def _(m):
        at = pl.ds(pl.multiple_of(m * 256, 256), 256)
        branch = jnp.dot(w2_ref[...], hid_ref[:, at], preferred_element_type=F32)
        gate = jnp.concatenate([gate_ref[...], gate_ref[...]], axis=1)
        mixed = tok_ref[:, at] + gate * branch
        center = mixed - jnp.sum(mixed, axis=0, keepdims=True) * (1.0 / D)
        variance = jnp.sum(center * center, axis=0, keepdims=True) * (1.0 / D)
        inverse = lax.rsqrt(variance + norm_epsilon)
        normed = center * inverse
        predicted = jnp.dot(wf_ref[...], normed.astype(BF16), preferred_element_type=F32)
        residue = predicted - target_ref[:, at]
        own_ref[1] += jnp.sum(residue * residue) * (1.0 / (TOK * 16))
        grad_pred = (residue * (2.0 / (TOK * 16))).astype(BF16)
        grad_normed = lax.dot_general(
            wf_ref[...], grad_pred, (((0,), (0,)), ((), ())), preferred_element_type=F32
        )
        mean = jnp.sum(grad_normed, axis=0, keepdims=True) * (1.0 / D)
        along = jnp.sum(grad_normed * normed, axis=0, keepdims=True) * (1.0 / D)
        grad_mixed = inverse * (grad_normed - mean - normed * along)
        grad_branch = gate * grad_mixed
        gbt_ref[:, at] = grad_branch.astype(BF16)
        gb_ref[at, :] = grad_branch.T.astype(BF16)

    square_ref[...] = jnp.zeros_like(square_ref)
    chosen = selected_ref[0, 0] == 1

    def swap(f):
        return remote(send_ref.at[f], r0.at[f], q_send.at[f], q_recv.at[f], partner)

    @pl.loop(0, NY)
    def _(f):
        at = pl.ds(pl.multiple_of(f * CHUNK, CHUNK), CHUNK)
        grad_hidden = jnp.dot(weights(1, at), gbt_ref[...], preferred_element_type=F32)
        grad_pre = (slope_ref[at, :] * grad_hidden).astype(BF16)
        grad_1 = jnp.dot(grad_pre, mod_ref[...], preferred_element_type=F32)
        grad_2 = jnp.dot(hid_ref[at, :], gb_ref[...], preferred_element_type=F32)
        grad_1 = jnp.where(chosen, grad_1, 0.0)
        grad_2 = jnp.where(chosen, grad_2, 0.0)
        kept = jnp.where(c == 0, grad_1, grad_2)
        sent = jnp.where(c == 0, grad_2, grad_1)
        keep_ref[f] = kept.reshape(NX, 2, HALF, D)
        send_ref[f] = sent.astype(BF16).reshape(NX, 2, HALF, D)
        swap(f).start()
        square_ref[...] += jnp.sum(
            grad_1 * grad_1 + grad_2 * grad_2, axis=0, keepdims=True
        )

    total = jnp.sum(square_ref[...], axis=1, keepdims=True)
    factor = 1.0 / (jnp.sqrt(total * (1.0 / (2 * D * FF))) + clip_offset)
    own_ref[0] = jnp.broadcast_to(factor, (8, 128))
    own_ref[1] = jnp.where(chosen, own_ref[1], 0.0)
    loss_0 = remote(own_ref.at[pl.ds(0, 2)], own_ref.at[pl.ds(2, 2)], l_send.at[0], l_recv.at[0], partner)
    loss_0.start()
    for f in range(NY):
        swap(f).wait_recv()
    loss_0.wait_recv()
    mine = own_ref[0, 0:1, 0:1]
    other = own_ref[2, 0:1, 0:1]

    def part(half, k, j):
        if half == 0:
            return (j, x_at(k), 0)
        return (y_at(k), j, 1)

    def chip(half, k, j):
        at = part(half, k, j)
        return keep_ref[at] * mine + r0[at].astype(F32) * other

    firsts = {}
    for k in (2, 1, 3, 0):
        for h in range(2):
            for j in range(4):
                value = chip(h, k, j)
                if k == 0:
                    acc[h, j] = value
                else:
                    s1[h, k - 1, j] = value.astype(BF16)
            if k > 0:
                firsts[h, k] = remote(
                    s1.at[h, k - 1],
                    r1.at[h, k - 1],
                    s1_send.at[h, k],
                    s1_recv.at[h, k],
                    first_to(h, k),
                )
                firsts[h, k].start()
    l1[x] = own_ref[1] + own_ref[3]
    losses = [loss_0]
    for k in range(1, NX):
        copy = remote(l1.at[x], l1.at[x], l_send.at[k], l_recv.at[k], {"fsdp_1": x_at(k)})
        copy.start()
        losses.append(copy)
    seconds = {}
    for h in range(2):
        for k in (1, 3, 2):
            firsts[h, k].wait_recv()
        for k in (2, 1, 3, 0):
            j = second_at(h, k)
            acc[h, j] = (acc[h, j] + r1[h, 0, j].astype(F32)) + (
                r1[h, 1, j].astype(F32) + r1[h, 2, j].astype(F32)
            )
            if k > 0:
                seconds[h, k] = remote(
                    acc.at[h, j],
                    r2.at[h, k - 1],
                    s2_send.at[h, k],
                    s2_recv.at[h, k],
                    second_to(h, k),
                )
                seconds[h, k].start()
    for copy in losses[1:]:
        copy.wait_recv()
    l2[y] = (l1[0] + l1[1]) + (l1[2] + l1[3])
    for k in range(1, NY):
        copy = remote(
            l2.at[y], l2.at[y], l_send.at[3 + k], l_recv.at[3 + k], {"fsdp_0": y_at(k)}
        )
        copy.start()
        losses.append(copy)
    for h in range(2):
        for k in (1, 3, 2):
            seconds[h, k].wait_recv()
        j = second_at(h, 0)
        value = (acc[h, j] + r2[h, 0]) + (r2[h, 1] + r2[h, 2])
        for i in range(HALF // 8):
            for n in range(D // 128):
                t = (h * (HALF // 8) + i) * (D // 128) + n
                tiles[t // PIECE, t % PIECE] = value[8 * i : 8 * i + 8, 128 * n : 128 * n + 128]
    for copy in losses[4:]:
        copy.wait_recv()
    at = USED_TILES
    tiles[at // PIECE, at % PIECE] = (l2[0] + l2[1]) + (l2[2] + l2[3])
    for t in range(USED_TILES + 1, TILES):
        tiles[t // PIECE, t % PIECE] = jnp.zeros((8, 128), F32)

    order = (4, 3, 5, 2, 6, 1, 7)
    thirds = []
    for k in order:
        copy = remote(
            tiles.at[z_at(k)], r3.at[z], z_send.at[k], z_recv.at[k], {"dp_0": z_at(k)}
        )
        copy.start()
        thirds.append(copy)
    r3[z] = tiles[z]
    for copy in thirds:
        copy.wait_recv()
    value = r3[0]
    for k in range(1, NZ):
        value = value + r3[k]
    whole[c, z] = value
    spreads = {}
    for k in order:
        spreads[k] = remote(
            whole.at[c, z], whole.at[c, z], a_send.at[k], a_recv.at[k], {"dp_0": z_at(k)}
        )
        spreads[k].start()
    crossings = []
    for k in (0, 7, 1, 6, 2, 5, 3, 4):
        if k > 0:
            spreads[k].wait_recv()
        at = z_at(NZ - k) if k > 0 else z
        copy = remote(whole.at[c, at], whole.at[c, at], f_send.at[k], f_recv.at[k], partner)
        copy.start()
        crossings.append(copy)
    for copy in crossings:
        copy.wait_recv()
    for w in range(2):
        for t in range(USED_TILES):
            i, n = t // (D // 128), t % (D // 128)
            sum_ref[w, 8 * i : 8 * i + 8, 128 * n : 128 * n + 128] = whole[
                w, t // PIECE, t % PIECE
            ]
    total_ref[...] = whole[0, USED_TILES // PIECE, USED_TILES % PIECE]
    for f in range(NY):
        swap(f).wait_send()
    for group in (early, late, crossed, firsts, seconds, spreads):
        for copy in group.values():
            copy.wait_send()
    for group in (messages, losses, thirds, crossings):
        for copy in group:
            copy.wait_send()


def finish_kernel(sum_ref, total_ref, moved_ref, n1_ref, n2_ref, *outs):
    u1_ref, u2_ref, mean_ref, moments_ref = outs
    u1_ref[...] = (sum_ref[0] + noise_weight * n1_ref[...]) * (1.0 / SELECTED)
    u2_ref[...] = (sum_ref[1] + noise_weight * n2_ref[...]) * (1.0 / SELECTED)
    mean_ref[...] = total_ref[0:1, 0:1] * (1.0 / SELECTED)
    moments_ref[...] = moved_ref[...]


def per_device(
    features,
    conv_weight,
    vae_noise,
    flips,
    crops,
    tsteps,
    diffusion_noise,
    selected,
    w_patch,
    w_time,
    w_ada,
    w_fc1,
    w_fc2,
    w_final,
    noise_fc1,
    noise_fc2,
):
    dma = pltpu.SemaphoreType.DMA
    pixels = features.reshape(TOK, FCH)
    taps = conv_weight.transpose(0, 1, 3, 2).reshape(72, FCH)
    views = diffusion_noise.reshape(AUG, SIDE, SIDE * LC).transpose(1, 0, 2)
    grid = (NY, NX, 2, HALF, D)
    tile = (8, 128)
    vmem = pltpu.VMEM
    sums, total, moved = pl.pallas_call(
        step_kernel,
        out_shape=(
            jax.ShapeDtypeStruct((2, SHARD, D), F32),
            jax.ShapeDtypeStruct(tile, F32),
            jax.ShapeDtypeStruct((2 * SIDE, 128), F32),
        ),
        in_specs=[SMEM_SPEC] * 5
        + [ANY_SPEC]
        + [VMEM_SPEC] * 8
        + [ANY_SPEC] * 2
        + [VMEM_SPEC],
        out_specs=(VMEM_SPEC,) * 3,
        scratch_shapes=[
            vmem((TOK, FCH), BF16),
            vmem((256, D), BF16),
            vmem((D, 3 * D), BF16),
            vmem((2,) + grid, BF16),
            vmem((NDP,) + tile, F32),
            vmem((NDP,) + tile, F32),
            vmem((256, 128), F32),
            vmem((AUG, 40, 128), F32),
            vmem((D, 128), F32),
            vmem((D, 128), F32),
            vmem((D, 128), F32),
            vmem((D, TOK), F32),
            vmem((D, TOK), BF16),
            vmem((TOK, D), BF16),
            vmem((D, FF), BF16),
            vmem((FF, TOK), BF16),
            vmem((FF, TOK), F32),
            vmem((16, TOK), F32),
            vmem((D, TOK), BF16),
            vmem((TOK, D), BF16),
            vmem((1, D), F32),
            vmem((4,) + tile, F32),
            vmem(grid, F32),
            vmem(grid, BF16),
            vmem(grid, BF16),
            vmem((2, 3, 4, HALF, D), BF16),
            vmem((2, 3, 4, HALF, D), BF16),
            vmem((2, 4, HALF, D), F32),
            vmem((2, 3, HALF, D), F32),
            vmem((NZ, PIECE) + tile, F32),
            vmem((NZ, PIECE) + tile, F32),
            vmem((2, NZ, PIECE) + tile, F32),
            vmem((NX,) + tile, F32),
            vmem((NY,) + tile, F32),
        ]
        + [dma((2, 4))] * 10
        + [dma((NDP,))] * 2
        + [dma((NZ,))] * 10
        + [dma((3,))],
        compiler_params=pltpu.CompilerParams(
            collective_id=0, has_side_effects=True, vmem_limit_bytes=56 << 20
        ),
        name="step",
    )(
        flips.reshape(1, AUG),
        crops.reshape(AUG, 2).T,
        tsteps.reshape(1, AUG),
        selected,
        jnp.asarray(blend_tables()),
        pixels,
        taps,
        w_fc1.T,
        w_fc2.T,
        vae_noise.reshape(SIDE, SIDE * LC),
        views.reshape(SIDE * AUG, SIDE * LC),
        w_patch,
        jnp.asarray(position_rows()),
        jnp.asarray(time_rates()),
        w_time,
        w_ada,
        w_final.T,
    )
    update_1, update_2, mean_loss, moments = pl.pallas_call(
        finish_kernel,
        out_shape=(
            jax.ShapeDtypeStruct((SHARD, D), F32),
            jax.ShapeDtypeStruct((SHARD, D), F32),
            jax.ShapeDtypeStruct((1, 1), F32),
            jax.ShapeDtypeStruct((2 * SIDE, 128), F32),
        ),
        in_specs=[VMEM_SPEC] * 5,
        out_specs=(VMEM_SPEC,) * 4,
        name="finish",
    )(sums, total, moved, noise_fc1.T, noise_fc2.T)
    return (update_1.T, update_2.T, mean_loss.reshape(()), moments.reshape(1, 1, -1))


def solution(mesh):
    split = Mesh(mesh.devices.reshape(NZ, NC, NY, NX), DP + FSDP)
    return jax.shard_map(
        per_device,
        mesh=split,
        in_specs=(
            P(FSDP, None, DP, None, None),
            P(),
            P(DP, FSDP, None),
            P(DP, FSDP, None),
            P(DP, FSDP, None, None),
            P(DP, FSDP, None),
            P(DP, FSDP, None, None),
            P(DP, FSDP),
            P(),
            P(),
            P(),
            P(None, FSDP),
            P(None, FSDP),
            P(),
            P(None, FSDP),
            P(None, FSDP),
        ),
        out_specs=(P(None, FSDP), P(None, FSDP), P(), P(DP, FSDP, None)),
        check_vma=False,
    )
```

```python
import math

import jax
import jax.numpy as jnp
import ml_dtypes
import numpy as np
from jax import lax
from jax.experimental import pallas as pl
from jax.experimental.pallas import tpu as pltpu
from jax.sharding import Mesh
from jax.sharding import PartitionSpec as P

MESH = pl.DeviceIdType.MESH
DP = ("dp_0", "dp_1")
FSDP = ("fsdp_0", "fsdp_1")
NZ, NC, NY, NX = 8, 2, 4, 4
NDP = NZ * NC
D, FF, TOK, FCH = 384, 1536, 1024, 512
SHARD = FF // (NY * NX)
HALF = SHARD // 2
SIDE, LC, AUG, TSTEPS = 32, 4, 4, 1000
SELECTED = 128
CHUNK = 384
WIDE = 512
PIECE = 5
TILES = NZ * PIECE
USED_TILES = (SHARD // 8) * (D // 128)
clip_offset = 1e-05
noise_weight = 16.0
norm_epsilon = 1e-06
VMEM_SPEC = pl.BlockSpec(memory_space=pltpu.VMEM)
ANY_SPEC = pl.BlockSpec(memory_space=pl.ANY)
SMEM_SPEC = pl.BlockSpec(memory_space=pltpu.SMEM)
F32, BF16 = jnp.float32, jnp.bfloat16


def three_parts(table):
    high = table.astype(np.float32).astype(ml_dtypes.bfloat16)
    rest = table.astype(np.float32) - high.astype(np.float32)
    middle = rest.astype(ml_dtypes.bfloat16)
    low = (rest - middle.astype(np.float32)).astype(ml_dtypes.bfloat16)
    return high, middle, low


def position_rows():
    side, quarter = SIDE // 2, D // 4
    frequency = 1.0 / 10000.0 ** (np.arange(quarter) / quarter)
    angles = np.arange(side)[:, None] * frequency[None, :]
    line = np.concatenate([np.sin(angles), np.cos(angles)], axis=1)
    parts = three_parts(line)
    zero = np.zeros_like(parts[0])
    rows = [np.concatenate([p, zero], axis=1) for p in parts]
    cols = [np.concatenate([zero, p], axis=1) for p in parts]
    return np.concatenate(rows + cols, axis=0)


def blend_tables():
    beta = 0.0001 + np.arange(TSTEPS) * (0.02 - 0.0001) / (TSTEPS - 1)
    alpha_bar = np.cumprod(1.0 - beta)
    return np.stack([np.sqrt(alpha_bar), np.sqrt(1.0 - alpha_bar)]).astype(np.float32)


def time_rates():
    steps = np.arange(128, dtype=np.float32)
    scaled = np.float32(-math.log(10000.0)) * steps / np.float32(128)
    return np.exp(scaled).astype(np.float32).reshape(1, 128)


def place():
    return tuple(lax.axis_index(a) for a in ("dp_0", "dp_1", "fsdp_0", "fsdp_1"))


def widened(ref):
    return jnp.concatenate([ref[...]] * (WIDE // 128), axis=1)


def split_three(value):
    high = value.astype(BF16)
    rest = value - high.astype(F32)
    middle = rest.astype(BF16)
    low = (rest - middle.astype(F32)).astype(BF16)
    return jnp.concatenate([high, middle, low], axis=0)


def joined_three(value, rows):
    return (value[2 * rows :] + value[rows : 2 * rows]) + value[:rows]


def step_kernel(*refs):
    inputs, (sum_ref, total_ref, moments_ref) = refs[:17], refs[17:20]
    buffers, scratch = refs[20:37], refs[37:]
    (flips_ref, crops_ref, steps_ref, selected_ref, table_ref) = buffers[:5]
    (x_buf, taps_ref, w1_ref, w2s_ref, vae_ref, noise_ref, wp_ref) = buffers[5:12]
    (pos_ref, rates_ref, wt_buf, wa_buf, wf_ref) = buffers[12:]
    (all_ref, msg_ref, got_ref) = scratch[:3]
    (rows_ref, pads_ref, shift_ref, scale_ref, gate_ref, tok_ref, modt_ref) = scratch[3:10]
    (mod_ref, w2_ref, hid_ref, slope_ref, target_ref, gbt_ref, gb_ref) = scratch[10:17]
    (square_ref, own_ref, keep_ref, send_ref, r0, s1, r1, acc, c2, r2) = scratch[17:27]
    (tiles, r3, whole, l0, l1, l2) = scratch[27:33]
    (g1_send, g1_recv, g2_send, g2_recv, p_send, p_recv) = scratch[33:39]
    (s2_send, s2_recv, s1_send, s1_recv) = scratch[39:43]
    (m_send, m_recv, q_send, q_recv, z_send, z_recv) = scratch[43:49]
    (a_send, a_recv, f_send, f_recv, l_send, l_recv, c_sem) = scratch[49:]
    z, c, y, x = place()
    me = z * NC + c
    partner = {"dp_1": 1 - c}
    lane = lax.broadcasted_iota(jnp.int32, (8, 128), 1)
    zero = jnp.zeros((8, 128), F32)

    def x_at(k):
        return lax.rem(x + k, NX)

    def y_at(k):
        return lax.rem(y + k, NY)

    def z_at(k):
        return lax.rem(z + k, NZ)

    def dp_at(k):
        return lax.rem(me + k, NDP)

    def dp_device(k):
        other = dp_at(k)
        return {"dp_0": other // NC, "dp_1": lax.rem(other, NC)}

    def remote(src, dst, send, recv, device):
        return pltpu.make_async_remote_copy(
            src_ref=src,
            dst_ref=dst,
            send_sem=send,
            recv_sem=recv,
            device_id=device,
            device_id_type=MESH,
        )

    def first_to(half, k):
        return {"fsdp_1": x_at(k)} if half == 0 else {"fsdp_0": y_at(k)}

    def second_to(half, k):
        return {"fsdp_0": y_at(k)} if half == 0 else {"fsdp_1": x_at(k)}

    def second_at(half, k):
        return y_at(k) if half == 0 else x_at(k)

    barrier = pltpu.get_barrier_semaphore()
    for k in range(1, NX):
        pl.semaphore_signal(barrier, 1, device_id={"fsdp_1": x_at(k)}, device_id_type=MESH)
        pl.semaphore_signal(barrier, 1, device_id={"fsdp_0": y_at(k)}, device_id_type=MESH)
    for k in range(1, NDP):
        pl.semaphore_signal(barrier, 1, device_id=dp_device(k), device_id_type=MESH)
    loads = [
        pltpu.make_async_copy(inputs[i], buffers[i], c_sem.at[i]) for i in range(len(inputs))
    ]
    shards, pictures = (7, 8), (5, 6)
    for i in shards + pictures:
        loads[i].start()
    for i in range(len(inputs)):
        if i not in shards + pictures:
            loads[i].start()
    for i in shards:
        loads[i].wait()
    own_shard = jnp.where(c == 0, w1_ref[...], w2s_ref[...])
    all_ref[c, y, x, 0] = own_shard[:HALF]
    all_ref[c, y, x, 1] = own_shard[HALF:]
    pl.semaphore_wait(barrier, NX - 1 + NY - 1 + NDP - 1)

    def message(k):
        return remote(
            msg_ref.at[dp_at(k)], got_ref.at[me], m_send.at[k], m_recv.at[k], dp_device(k)
        )

    def gather_first(half, k):
        at = all_ref.at[c, y, x, half]
        return remote(at, at, g1_send.at[half, k], g1_recv.at[half, k], first_to(half, k))

    def line(half, k):
        if half == 0:
            return all_ref.at[c, y_at(NY - k), :, 0]
        return all_ref.at[c, :, x_at(NX - k), 1]

    def gather_second(half, k):
        at = line(half, 0)
        return remote(at, at, g2_send.at[half, k], g2_recv.at[half, k], second_to(half, k))

    def across(half, k):
        at = line(half, k)
        return remote(at, at, p_send.at[half, k], p_recv.at[half, k], partner)

    messages = [message(k) for k in range(1, NDP)]
    early = {(h, k): gather_first(h, k) for k in (1, 3, 2) for h in range(2)}
    late = {(h, k): gather_second(h, k) for k in (1, 3, 2) for h in range(2)}
    crossed = {(h, k): across(h, k) for k in (0, 1, 3, 2) for h in range(2)}
    for copy in early.values():
        copy.start()
    for i in pictures:
        loads[i].wait()
    taps = lax.dot_general(
        taps_ref[...], x_buf[...], (((1,), (1,)), ((), ())), preferred_element_type=F32
    )
    col = lane % SIDE

    def tap(dy, dx, v):
        at = (dy * 3 + dx) * 8
        return taps[at : at + 8, 128 * v : 128 * v + 128]

    for v in range(8):
        rows = []
        for dy in range(3):
            left = jnp.where(col == 0, zero, pltpu.roll(tap(dy, 0, v), 1, 1))
            right = jnp.where(col == SIDE - 1, zero, pltpu.roll(tap(dy, 2, v), 127, 1))
            rows.append(left + tap(dy, 1, v) + right)
        for odd in range(2):
            parts = [pltpu.roll(r, 64, 1) if odd else r for r in rows]
            parts = [jnp.where(lane < 64, r, zero) for r in parts]
            msg_ref[2 * v + odd] = (
                parts[2] + pltpu.roll(parts[1], 32, 1) + pltpu.roll(parts[0], 64, 1)
            )
    got_ref[me] = msg_ref[me]
    for m in messages:
        m.start()
    for copy in early.values():
        copy.wait_recv()
    for copy in late.values():
        copy.start()
    for h in range(2):
        crossed[h, 0].start()
    for i in range(len(inputs)):
        if i not in shards + pictures:
            loads[i].wait()

    row = lax.broadcasted_iota(jnp.int32, (8, 128), 0)
    steps = jnp.zeros((8, 128), F32)
    for a in range(AUG):
        steps = jnp.where(row == a, steps_ref[0, a].astype(F32), steps)
    phases = steps * rates_ref[...]
    stamp = jnp.concatenate([jnp.cos(phases), jnp.sin(phases)], axis=1).astype(BF16)
    raw = jnp.dot(stamp, wt_buf[...], preferred_element_type=F32)
    conditioning = (raw * (1.0 / (1.0 + jnp.exp(-raw)))).astype(BF16)
    modulation = jnp.dot(conditioning, wa_buf[...], preferred_element_type=F32)
    views = [jnp.broadcast_to(modulation[a : a + 1], (16, 3 * D)) for a in range(AUG)]
    turned = jnp.concatenate(views + views, axis=0).T
    shift_ref[...] = turned[:D]
    scale_ref[...] = 1.0 + turned[D : 2 * D]
    gate_ref[...] = turned[2 * D :]

    for m in messages:
        m.wait_recv()
    for k in range(8):
        low = pltpu.roll(got_ref[2 * k], 96, 1)
        above = pltpu.roll(got_ref[2 * k + 2], 96, 1) if k < 7 else zero
        high = pltpu.roll(got_ref[2 * k + 1], 32, 1)
        below = pltpu.roll(got_ref[2 * k - 1], 32, 1) if k > 0 else zero
        four = jnp.where(lane < 96, low, above) + jnp.where(lane >= 32, high, below)
        for r in range(4):
            at = (4 * k + r) * 8
            rows_ref[at : at + 8, :] = pltpu.roll(four, 128 - 32 * r, 1) if r else four
    wide = lax.broadcasted_iota(jnp.int32, (SIDE, 128), 1) // SIDE
    halves = []
    for h in range(2):
        value = rows_ref[pl.ds(4 * h, SIDE, stride=8), :]
        for ch in range(1, 4):
            part = rows_ref[pl.ds(4 * h + ch, SIDE, stride=8), :]
            value = jnp.where(wide == ch, pltpu.roll(part, 32 * ch, 1), value)
        halves.append(value)
    by_channel = jnp.concatenate(halves, axis=1)
    source = lax.broadcasted_iota(jnp.int32, (256, 512), 0)
    goal = lax.broadcasted_iota(jnp.int32, (256, 512), 1)
    channel, column = source // SIDE, source % SIDE
    natural = column * 8 + channel
    apart = 256 + (channel // 4) * 128 + column * 4 + channel % 4
    spread = jnp.where((goal == natural) | (goal == apart), 1.0, 0.0).astype(BF16)
    placed = joined_three(
        jnp.dot(split_three(by_channel), spread, preferred_element_type=F32), SIDE
    )
    moments_ref[pl.ds(0, SIDE, stride=2), :] = placed[:, 0:128]
    moments_ref[pl.ds(1, SIDE, stride=2), :] = placed[:, 128:256]

    latent = placed[:, 256:384] + jnp.exp(0.5 * placed[:, 384:512]) * vae_ref[...]
    source = lax.broadcasted_iota(jnp.int32, (128, 128), 0)
    goal = lax.broadcasted_iota(jnp.int32, (128, 128), 1)
    maps = []
    for a in range(AUG):
        cell = goal // LC + crops_ref[1, a] - 2
        inside = (cell >= 0) & (cell < SIDE)
        mirror = (flips_ref[0, a] == 1).astype(jnp.int32)
        cell = cell + mirror * (SIDE - 1 - 2 * cell)
        match = inside & (source == cell * LC + goal % LC)
        maps.append(jnp.where(match, 1.0, 0.0).astype(BF16))
    columns = jnp.dot(
        split_three(latent), jnp.concatenate(maps, axis=1), preferred_element_type=F32
    )
    columns = joined_three(columns, SIDE)
    noised, noises = [], []
    for a in range(AUG):
        pads_ref[a] = jnp.zeros((40, 128), F32)
        pads_ref[a, 2 : 2 + SIDE, :] = columns[:, 128 * a : 128 * a + 128]
    for dr in range(2):
        for a in range(AUG):
            view = pads_ref[a, pl.ds(crops_ref[0, a] + dr, 16, stride=2), :]
            noise = noise_ref[pl.ds(dr * 4 + a, 16, stride=8), :]
            step = steps_ref[0, a]
            noised.append(table_ref[0, step] * view + table_ref[1, step] * noise)
            noises.append(noise)

    def patched(pieces):
        turned = jnp.concatenate(pieces, axis=0).T
        first, last = [], []
        for m in range(8):
            even = turned[16 * m : 16 * m + 8]
            odd = turned[16 * m + 8 : 16 * m + 16]
            first.append(jnp.where(lane < 64, even, pltpu.roll(odd, 64, 1)))
            last.append(jnp.where(lane < 64, pltpu.roll(even, 64, 1), odd))
        return jnp.concatenate(
            [jnp.concatenate(first, axis=1), jnp.concatenate(last, axis=1)], axis=0
        )

    patches = patched(noised).astype(BF16)
    target_ref[...] = patched(noises)

    which = lax.broadcasted_iota(jnp.int32, (96, TOK), 0)
    token = lax.broadcasted_iota(jnp.int32, (96, TOK), 1)
    cell = jnp.where(which < 48, token % 16, token // 64)
    marks = jnp.where(which % 16 == cell, 1.0, 0.0).astype(BF16)
    tok_ref[...] = lax.dot_general(
        jnp.concatenate([wp_ref[...], pos_ref[...]], axis=0),
        jnp.concatenate([patches, marks], axis=0),
        (((0,), (0,)), ((), ())),
        preferred_element_type=F32,
    )

    for k in (1, 3):
        for h in range(2):
            late[h, k].wait_recv()
            crossed[h, k].start()

    @pl.loop(0, TOK // WIDE)
    def _(m):
        at = pl.ds(pl.multiple_of(m * WIDE, WIDE), WIDE)
        value = tok_ref[:, at]
        center = value - jnp.sum(value, axis=0, keepdims=True) * (1.0 / D)
        variance = jnp.sum(center * center, axis=0, keepdims=True) * (1.0 / D)
        normed = center * lax.rsqrt(variance + norm_epsilon)
        out = normed * widened(scale_ref) + widened(shift_ref)
        modt_ref[:, at] = out.astype(BF16)
        mod_ref[at, :] = out.T.astype(BF16)

    for k in (2,):
        for h in range(2):
            late[h, k].wait_recv()
            crossed[h, k].start()

    for copy in crossed.values():
        copy.wait_recv()
    flat_weights = all_ref.reshape(2, FF, D)

    def weights(w, at):
        return flat_weights[w, at, :]

    @pl.loop(0, FF // 128)
    def _(m):
        at = pl.ds(pl.multiple_of(m * 128, 128), 128)
        w2_ref[:, at] = weights(1, at).astype(F32).T.astype(BF16)

    root = math.sqrt(2.0 / math.pi)

    @pl.loop(0, FF // CHUNK)
    def _(f):
        at = pl.ds(pl.multiple_of(f * CHUNK, CHUNK), CHUNK)
        pre = jnp.dot(weights(0, at), modt_ref[...], preferred_element_type=F32)
        squared = pre * pre
        inner = pre * (squared * (root * 0.044715) + root)
        share = 0.5 * jnp.tanh(inner) + 0.5
        hidden = pre * share
        hid_ref[at, :] = hidden.astype(BF16)
        slope = (1.0 - share) * hidden * (squared * (6.0 * root * 0.044715) + 2.0 * root)
        slope_ref[at, :] = slope + share

    own_ref[1] = jnp.zeros((8, 128), F32)

    @pl.loop(0, TOK // WIDE)
    def _(m):
        at = pl.ds(pl.multiple_of(m * WIDE, WIDE), WIDE)
        branch = jnp.dot(w2_ref[...], hid_ref[:, at], preferred_element_type=F32)
        gate = widened(gate_ref)
        mixed = tok_ref[:, at] + gate * branch
        center = mixed - jnp.sum(mixed, axis=0, keepdims=True) * (1.0 / D)
        variance = jnp.sum(center * center, axis=0, keepdims=True) * (1.0 / D)
        inverse = lax.rsqrt(variance + norm_epsilon)
        normed = center * inverse
        predicted = jnp.dot(wf_ref[...], normed.astype(BF16), preferred_element_type=F32)
        residue = predicted - target_ref[:, at]
        own_ref[1] += jnp.sum(residue * residue) * (1.0 / (TOK * 16))
        grad_pred = (residue * (2.0 / (TOK * 16))).astype(BF16)
        grad_normed = lax.dot_general(
            wf_ref[...], grad_pred, (((0,), (0,)), ((), ())), preferred_element_type=F32
        )
        mean = jnp.sum(grad_normed, axis=0, keepdims=True) * (1.0 / D)
        along = jnp.sum(grad_normed * normed, axis=0, keepdims=True) * (1.0 / D)
        grad_mixed = inverse * (grad_normed - mean - normed * along)
        grad_branch = gate * grad_mixed
        gbt_ref[:, at] = grad_branch.astype(BF16)
        gb_ref[at, :] = grad_branch.T.astype(BF16)

    square_ref[...] = jnp.zeros_like(square_ref)
    chosen = selected_ref[0, 0] == 1
    l0[0] = jnp.where(chosen, own_ref[1], 0.0)
    losses = [remote(l0.at[0], l0.at[1], l_send.at[0], l_recv.at[0], partner)]
    losses[0].start()

    def swap(f):
        return remote(send_ref.at[f], r0.at[f], q_send.at[f], q_recv.at[f], partner)

    @pl.loop(0, NY)
    def _(f):
        at = pl.ds(pl.multiple_of(f * CHUNK, CHUNK), CHUNK)
        grad_hidden = jnp.dot(weights(1, at), gbt_ref[...], preferred_element_type=F32)
        grad_pre = (slope_ref[at, :] * grad_hidden).astype(BF16)
        grad_1 = jnp.dot(grad_pre, mod_ref[...], preferred_element_type=F32)
        grad_2 = jnp.dot(hid_ref[at, :], gb_ref[...], preferred_element_type=F32)
        grad_1 = jnp.where(chosen, grad_1, 0.0)
        grad_2 = jnp.where(chosen, grad_2, 0.0)
        kept = jnp.where(c == 0, grad_1, grad_2)
        sent = jnp.where(c == 0, grad_2, grad_1)
        keep_ref[f] = kept.reshape(NX, 2, HALF, D)
        send_ref[f] = sent.astype(BF16).reshape(NX, 2, HALF, D)
        swap(f).start()
        square_ref[...] += jnp.sum(
            grad_1 * grad_1 + grad_2 * grad_2, axis=0, keepdims=True
        )

    total = jnp.sum(square_ref[...], axis=1, keepdims=True)
    factor = 1.0 / (jnp.sqrt(total * (1.0 / (2 * D * FF))) + clip_offset)
    own_ref[0] = jnp.broadcast_to(factor, (8, 128))
    factors = remote(own_ref.at[0], own_ref.at[2], l_send.at[7], l_recv.at[7], partner)
    factors.start()
    losses[0].wait_recv()
    l1[x] = l0[0] + l0[1]
    for k in range(1, NX):
        copy = remote(l1.at[x], l1.at[x], l_send.at[k], l_recv.at[k], {"fsdp_1": x_at(k)})
        copy.start()
        losses.append(copy)
    for f in range(NY):
        swap(f).wait_recv()
    factors.wait_recv()
    mine = own_ref[0, 0:1, 0:1]
    other = own_ref[2, 0:1, 0:1]

    def part(half, k, j):
        if half == 0:
            return (j, x_at(k), 0)
        return (y_at(k), j, 1)

    def chip(half, k, j):
        at = part(half, k, j)
        return keep_ref[at] * mine + r0[at].astype(F32) * other

    offsets = (2, 1, 3, 0)
    firsts = {}
    for group in range(2):
        for k in (2, 1, 3):
            for h in range(2):
                for q in (2 * group, 2 * group + 1):
                    value = chip(h, k, second_at(h, offsets[q]))
                    s1[h, k - 1, q] = value.astype(BF16)
                firsts[h, k, group] = remote(
                    s1.at[h, k - 1, pl.ds(2 * group, 2)],
                    r1.at[h, k - 1, pl.ds(2 * group, 2)],
                    s1_send.at[h, 2 * k + group],
                    s1_recv.at[h, 2 * k + group],
                    first_to(h, k),
                )
                firsts[h, k, group].start()
    for h in range(2):
        for q in range(4):
            acc[h, q] = chip(h, 0, second_at(h, offsets[q]))
    for copy in losses[1:]:
        copy.wait_recv()
    l2[y] = (l1[0] + l1[1]) + (l1[2] + l1[3])
    for k in range(1, NY):
        copy = remote(
            l2.at[y], l2.at[y], l_send.at[3 + k], l_recv.at[3 + k], {"fsdp_0": y_at(k)}
        )
        copy.start()
        losses.append(copy)
    seconds = {}
    for group in range(2):
        for h in range(2):
            for k in (1, 3, 2):
                firsts[h, k, group].wait_recv()
            for q in (2 * group, 2 * group + 1):
                k = offsets[q]
                value = (acc[h, q] + r1[h, 0, q].astype(F32)) + (
                    r1[h, 1, q].astype(F32) + r1[h, 2, q].astype(F32)
                )
                if k == 0:
                    acc[h, q] = value
                else:
                    c2[h, k - 1] = value.astype(BF16)
                    seconds[h, k] = remote(
                        c2.at[h, k - 1],
                        r2.at[h, k - 1],
                        s2_send.at[h, k],
                        s2_recv.at[h, k],
                        second_to(h, k),
                    )
                    seconds[h, k].start()
    for copy in losses[4:]:
        copy.wait_recv()
    at = USED_TILES
    tiles[at // PIECE, at % PIECE] = (l2[0] + l2[1]) + (l2[2] + l2[3])
    for t in range(USED_TILES + 1, TILES):
        tiles[t // PIECE, t % PIECE] = jnp.zeros((8, 128), F32)
    for h in range(2):
        for k in (1, 3, 2):
            seconds[h, k].wait_recv()
        value = (acc[h, 3] + r2[h, 0].astype(F32)) + (
            r2[h, 1].astype(F32) + r2[h, 2].astype(F32)
        )
        for i in range(HALF // 8):
            for n in range(D // 128):
                t = (h * (HALF // 8) + i) * (D // 128) + n
                tiles[t // PIECE, t % PIECE] = value[8 * i : 8 * i + 8, 128 * n : 128 * n + 128]

    order = (4, 3, 5, 2, 6, 1, 7)
    thirds = []
    for k in order:
        copy = remote(
            tiles.at[z_at(k)], r3.at[z], z_send.at[k], z_recv.at[k], {"dp_0": z_at(k)}
        )
        copy.start()
        thirds.append(copy)
    r3[z] = tiles[z]
    for copy in thirds:
        copy.wait_recv()
    value = r3[0]
    for k in range(1, NZ):
        value = value + r3[k]
    whole[c, z] = value
    spreads = {}
    for k in order:
        spreads[k] = remote(
            whole.at[c, z], whole.at[c, z], a_send.at[k], a_recv.at[k], {"dp_0": z_at(k)}
        )
        spreads[k].start()
    crossings = []
    for k in (0, 7, 1, 6, 2, 5, 3, 4):
        if k > 0:
            spreads[k].wait_recv()
        at = z_at(NZ - k) if k > 0 else z
        copy = remote(whole.at[c, at], whole.at[c, at], f_send.at[k], f_recv.at[k], partner)
        copy.start()
        crossings.append(copy)
    for copy in crossings:
        copy.wait_recv()
    for w in range(2):
        for t in range(USED_TILES):
            i, n = t // (D // 128), t % (D // 128)
            sum_ref[w, 8 * i : 8 * i + 8, 128 * n : 128 * n + 128] = whole[
                w, t // PIECE, t % PIECE
            ]
    total_ref[...] = whole[0, USED_TILES // PIECE, USED_TILES % PIECE]
    for f in range(NY):
        swap(f).wait_send()
    for group in (early, late, crossed, firsts, seconds, spreads):
        for copy in group.values():
            copy.wait_send()
    for group in (messages, losses, thirds, crossings, [factors]):
        for copy in group:
            copy.wait_send()


def finish_kernel(sum_ref, total_ref, moved_ref, n1_ref, n2_ref, *outs):
    u1_ref, u2_ref, mean_ref, moments_ref = outs
    u1_ref[...] = (sum_ref[0] + noise_weight * n1_ref[...]) * (1.0 / SELECTED)
    u2_ref[...] = (sum_ref[1] + noise_weight * n2_ref[...]) * (1.0 / SELECTED)
    mean_ref[...] = total_ref[0:1, 0:1] * (1.0 / SELECTED)
    moments_ref[...] = moved_ref[...]


def per_device(
    features,
    conv_weight,
    vae_noise,
    flips,
    crops,
    tsteps,
    diffusion_noise,
    selected,
    w_patch,
    w_time,
    w_ada,
    w_fc1,
    w_fc2,
    w_final,
    noise_fc1,
    noise_fc2,
):
    dma = pltpu.SemaphoreType.DMA
    pixels = features.reshape(TOK, FCH)
    taps = conv_weight.transpose(0, 1, 3, 2).reshape(72, FCH)
    views = diffusion_noise.reshape(AUG, SIDE, SIDE * LC).transpose(1, 0, 2)
    grid = (NY, NX, 2, HALF, D)
    tile = (8, 128)
    vmem = pltpu.VMEM
    sums, total, moved = pl.pallas_call(
        step_kernel,
        out_shape=(
            jax.ShapeDtypeStruct((2, SHARD, D), F32),
            jax.ShapeDtypeStruct(tile, F32),
            jax.ShapeDtypeStruct((2 * SIDE, 128), F32),
        ),
        in_specs=[ANY_SPEC] * 17,
        out_specs=(VMEM_SPEC,) * 3,
        scratch_shapes=[
            pltpu.SMEM((1, AUG), jnp.int32),
            pltpu.SMEM((2, AUG), jnp.int32),
            pltpu.SMEM((1, AUG), jnp.int32),
            pltpu.SMEM((1, 1), jnp.int32),
            pltpu.SMEM((2, TSTEPS), F32),
            vmem((TOK, FCH), BF16),
            vmem((72, FCH), BF16),
            vmem((SHARD, D), BF16),
            vmem((SHARD, D), BF16),
            vmem((SIDE, 128), F32),
            vmem((SIDE * AUG, 128), F32),
            vmem((16, D), BF16),
            vmem((96, D), BF16),
            vmem((1, 128), F32),
            vmem((256, D), BF16),
            vmem((D, 3 * D), BF16),
            vmem((16, D), BF16),
            vmem((2,) + grid, BF16),
            vmem((NDP,) + tile, F32),
            vmem((NDP,) + tile, F32),
            vmem((256, 128), F32),
            vmem((AUG, 40, 128), F32),
            vmem((D, 128), F32),
            vmem((D, 128), F32),
            vmem((D, 128), F32),
            vmem((D, TOK), F32),
            vmem((D, TOK), BF16),
            vmem((TOK, D), BF16),
            vmem((D, FF), BF16),
            vmem((FF, TOK), BF16),
            vmem((FF, TOK), F32),
            vmem((16, TOK), F32),
            vmem((D, TOK), BF16),
            vmem((TOK, D), BF16),
            vmem((1, D), F32),
            vmem((4,) + tile, F32),
            vmem(grid, F32),
            vmem(grid, BF16),
            vmem(grid, BF16),
            vmem((2, 3, 4, HALF, D), BF16),
            vmem((2, 3, 4, HALF, D), BF16),
            vmem((2, 4, HALF, D), F32),
            vmem((2, 3, HALF, D), BF16),
            vmem((2, 3, HALF, D), BF16),
            vmem((NZ, PIECE) + tile, F32),
            vmem((NZ, PIECE) + tile, F32),
            vmem((2, NZ, PIECE) + tile, F32),
            vmem((2,) + tile, F32),
            vmem((NX,) + tile, F32),
            vmem((NY,) + tile, F32),
        ]
        + [dma((2, 4))] * 8
        + [dma((2, 8))] * 2
        + [dma((NDP,))] * 2
        + [dma((NZ,))] * 10
        + [dma((17,))],
        compiler_params=pltpu.CompilerParams(
            collective_id=0, has_side_effects=True, vmem_limit_bytes=56 << 20
        ),
        name="step",
    )(
        flips.reshape(1, AUG),
        crops.reshape(AUG, 2).T,
        tsteps.reshape(1, AUG),
        selected,
        jnp.asarray(blend_tables()),
        pixels,
        taps,
        w_fc1.T,
        w_fc2.T,
        vae_noise.reshape(SIDE, SIDE * LC),
        views.reshape(SIDE * AUG, SIDE * LC),
        w_patch,
        jnp.asarray(position_rows()),
        jnp.asarray(time_rates()),
        w_time,
        w_ada,
        w_final.T,
    )
    update_1, update_2, mean_loss, moments = pl.pallas_call(
        finish_kernel,
        out_shape=(
            jax.ShapeDtypeStruct((SHARD, D), F32),
            jax.ShapeDtypeStruct((SHARD, D), F32),
            jax.ShapeDtypeStruct((1, 1), F32),
            jax.ShapeDtypeStruct((2 * SIDE, 128), F32),
        ),
        in_specs=[VMEM_SPEC] * 5,
        out_specs=(VMEM_SPEC,) * 4,
        name="finish",
    )(sums, total, moved, noise_fc1.T, noise_fc2.T)
    return (update_1.T, update_2.T, mean_loss.reshape(()), moments.reshape(1, 1, -1))


def solution(mesh):
    split = Mesh(mesh.devices.reshape(NZ, NC, NY, NX), DP + FSDP)
    return jax.shard_map(
        per_device,
        mesh=split,
        in_specs=(
            P(FSDP, None, DP, None, None),
            P(),
            P(DP, FSDP, None),
            P(DP, FSDP, None),
            P(DP, FSDP, None, None),
            P(DP, FSDP, None),
            P(DP, FSDP, None, None),
            P(DP, FSDP),
            P(),
            P(),
            P(),
            P(None, FSDP),
            P(None, FSDP),
            P(),
            P(None, FSDP),
            P(None, FSDP),
        ),
        out_specs=(P(None, FSDP), P(None, FSDP), P(), P(DP, FSDP, None)),
        check_vma=False,
    )
```

```python
import math

import jax
import jax.numpy as jnp
import ml_dtypes
import numpy as np
from jax import lax
from jax.experimental import pallas as pl
from jax.experimental.pallas import tpu as pltpu
from jax.sharding import Mesh
from jax.sharding import PartitionSpec as P

MESH = pl.DeviceIdType.MESH
DP = ("dp_0", "dp_1")
FSDP = ("fsdp_0", "fsdp_1")
NZ, NC, NY, NX = 8, 2, 4, 4
NDP = NZ * NC
D, FF, TOK, FCH = 384, 1536, 1024, 512
SHARD = FF // (NY * NX)
HALF = SHARD // 2
SIDE, LC, AUG, TSTEPS = 32, 4, 4, 1000
SELECTED = 128
CHUNK = 384
WIDE = 1024
PIECE = 5
TILES = NZ * PIECE
USED_TILES = (SHARD // 8) * (D // 128)
clip_offset = 1e-05
noise_weight = 16.0
norm_epsilon = 1e-06
VMEM_SPEC = pl.BlockSpec(memory_space=pltpu.VMEM)
HBM_SPEC = pl.BlockSpec(memory_space=pltpu.HBM)
SMEM_SPEC = pl.BlockSpec(memory_space=pltpu.SMEM)
F32, BF16 = jnp.float32, jnp.bfloat16


def three_parts(table):
    high = table.astype(np.float32).astype(ml_dtypes.bfloat16)
    rest = table.astype(np.float32) - high.astype(np.float32)
    middle = rest.astype(ml_dtypes.bfloat16)
    low = (rest - middle.astype(np.float32)).astype(ml_dtypes.bfloat16)
    return high, middle, low


def position_rows():
    side, quarter = SIDE // 2, D // 4
    frequency = 1.0 / 10000.0 ** (np.arange(quarter) / quarter)
    angles = np.arange(side)[:, None] * frequency[None, :]
    line = np.concatenate([np.sin(angles), np.cos(angles)], axis=1)
    parts = three_parts(line)
    zero = np.zeros_like(parts[0])
    rows = [np.concatenate([p, zero], axis=1) for p in parts]
    cols = [np.concatenate([zero, p], axis=1) for p in parts]
    return np.concatenate(rows + cols, axis=0)


def blend_tables():
    beta = 0.0001 + np.arange(TSTEPS) * (0.02 - 0.0001) / (TSTEPS - 1)
    alpha_bar = np.cumprod(1.0 - beta)
    return np.stack([np.sqrt(alpha_bar), np.sqrt(1.0 - alpha_bar)]).astype(np.float32)


def time_rates():
    steps = np.arange(128, dtype=np.float32)
    scaled = np.float32(-math.log(10000.0)) * steps / np.float32(128)
    return np.exp(scaled).astype(np.float32).reshape(1, 128)


def place():
    return tuple(lax.axis_index(a) for a in ("dp_0", "dp_1", "fsdp_0", "fsdp_1"))


def widened(ref):
    return jnp.concatenate([ref[...]] * (WIDE // 128), axis=1)


def split_three(value):
    high = value.astype(BF16)
    rest = value - high.astype(F32)
    middle = rest.astype(BF16)
    low = (rest - middle.astype(F32)).astype(BF16)
    return jnp.concatenate([high, middle, low], axis=0)


def joined_three(value, rows):
    return (value[2 * rows :] + value[rows : 2 * rows]) + value[:rows]


def step_kernel(*refs):
    inputs, (sum_ref, total_ref, moments_ref) = refs[:17], refs[17:20]
    buffers, scratch = refs[20:37], refs[37:]
    (flips_ref, crops_ref, steps_ref, selected_ref, table_ref) = buffers[:5]
    (x_buf, taps_ref, w1_ref, w2s_ref, vae_ref, noise_ref, wp_ref) = buffers[5:12]
    (pos_ref, rates_ref, wt_buf, wa_buf, wf_ref) = buffers[12:]
    (all_ref, msg_ref, got_ref) = scratch[:3]
    (rows_ref, pads_ref, shift_ref, scale_ref, gate_ref, tok_ref, modt_ref) = scratch[3:10]
    (mod_ref, w2_ref, hid_ref, slope_ref, target_ref, gbt_ref, gb_ref) = scratch[10:17]
    (square_ref, own_ref, keep_ref, send_ref, r0, s1, r1, acc, c2, r2) = scratch[17:27]
    (tiles, r3, whole, l0, l1, l2) = scratch[27:33]
    (g1_send, g1_recv, g2_send, g2_recv, p_send, p_recv) = scratch[33:39]
    (s2_send, s2_recv, q_send, q_recv, s1_send, s1_recv) = scratch[39:45]
    (m_send, m_recv, z_send, z_recv) = scratch[45:49]
    (a_send, a_recv, f_send, f_recv, l_send, l_recv, c_sem) = scratch[49:]
    z, c, y, x = place()
    me = z * NC + c
    partner = {"dp_1": 1 - c}
    lane = lax.broadcasted_iota(jnp.int32, (8, 128), 1)
    zero = jnp.zeros((8, 128), F32)

    def x_at(k):
        return lax.rem(x + k, NX)

    def y_at(k):
        return lax.rem(y + k, NY)

    def z_at(k):
        return lax.rem(z + k, NZ)

    def dp_at(k):
        return lax.rem(me + k, NDP)

    def dp_device(k):
        other = dp_at(k)
        return {"dp_0": other // NC, "dp_1": lax.rem(other, NC)}

    def remote(src, dst, send, recv, device):
        return pltpu.make_async_remote_copy(
            src_ref=src,
            dst_ref=dst,
            send_sem=send,
            recv_sem=recv,
            device_id=device,
            device_id_type=MESH,
        )

    def first_to(half, k):
        return {"fsdp_1": x_at(k)} if half == 0 else {"fsdp_0": y_at(k)}

    def second_to(half, k):
        return {"fsdp_0": y_at(k)} if half == 0 else {"fsdp_1": x_at(k)}

    def second_at(half, k):
        return y_at(k) if half == 0 else x_at(k)

    barrier = pltpu.get_barrier_semaphore()
    for k in range(1, NX):
        pl.semaphore_signal(barrier, 1, device_id={"fsdp_1": x_at(k)}, device_id_type=MESH)
        pl.semaphore_signal(barrier, 1, device_id={"fsdp_0": y_at(k)}, device_id_type=MESH)
    for k in range(1, NDP):
        pl.semaphore_signal(barrier, 1, device_id=dp_device(k), device_id_type=MESH)
    loads = [
        pltpu.make_async_copy(inputs[i], buffers[i], c_sem.at[i]) for i in range(len(inputs))
    ]
    shards, pictures = (7, 8), (5, 6)
    for i in shards + pictures:
        loads[i].start()
    for i in range(len(inputs)):
        if i not in shards + pictures:
            loads[i].start()
    for i in shards:
        loads[i].wait()
    own_shard = jnp.where(c == 0, w1_ref[...], w2s_ref[...])
    all_ref[c, y, x, 0] = own_shard[:HALF]
    all_ref[c, y, x, 1] = own_shard[HALF:]
    pl.semaphore_wait(barrier, NX - 1 + NY - 1 + NDP - 1)

    def message(k):
        return remote(
            msg_ref.at[dp_at(k)], got_ref.at[me], m_send.at[k], m_recv.at[k], dp_device(k)
        )

    def gather_first(half, k):
        at = all_ref.at[c, y, x, half]
        return remote(at, at, g1_send.at[half, k], g1_recv.at[half, k], first_to(half, k))

    def line(half, k):
        if half == 0:
            return all_ref.at[c, y_at(NY - k), :, 0]
        return all_ref.at[c, :, x_at(NX - k), 1]

    def gather_second(half, k):
        at = line(half, 0)
        return remote(at, at, g2_send.at[half, k], g2_recv.at[half, k], second_to(half, k))

    def across(half, k):
        at = line(half, k)
        return remote(at, at, p_send.at[half, k], p_recv.at[half, k], partner)

    messages = [message(k) for k in range(1, NDP)]
    early = {(h, k): gather_first(h, k) for k in (1, 3, 2) for h in range(2)}
    late = {(h, k): gather_second(h, k) for k in (1, 3, 2) for h in range(2)}
    crossed = {(h, k): across(h, k) for k in (0, 1, 3, 2) for h in range(2)}
    for copy in early.values():
        copy.start()
    for i in pictures:
        loads[i].wait()
    taps = lax.dot_general(
        taps_ref[...], x_buf[...], (((1,), (1,)), ((), ())), preferred_element_type=F32
    )
    col = lane % SIDE

    def tap(dy, dx, v):
        at = (dy * 3 + dx) * 8
        return taps[at : at + 8, 128 * v : 128 * v + 128]

    for v in range(8):
        rows = []
        for dy in range(3):
            left = jnp.where(col == 0, zero, pltpu.roll(tap(dy, 0, v), 1, 1))
            right = jnp.where(col == SIDE - 1, zero, pltpu.roll(tap(dy, 2, v), 127, 1))
            rows.append(left + tap(dy, 1, v) + right)
        for odd in range(2):
            parts = [pltpu.roll(r, 64, 1) if odd else r for r in rows]
            parts = [jnp.where(lane < 64, r, zero) for r in parts]
            msg_ref[2 * v + odd] = (
                parts[2] + pltpu.roll(parts[1], 32, 1) + pltpu.roll(parts[0], 64, 1)
            )
    got_ref[me] = msg_ref[me]
    for m in messages:
        m.start()
    for copy in early.values():
        copy.wait_recv()
    for copy in late.values():
        copy.start()
    for h in range(2):
        crossed[h, 0].start()
    for i in range(len(inputs)):
        if i not in shards + pictures:
            loads[i].wait()

    row = lax.broadcasted_iota(jnp.int32, (8, 128), 0)
    steps = jnp.zeros((8, 128), F32)
    for a in range(AUG):
        steps = jnp.where(row == a, steps_ref[0, a].astype(F32), steps)
    phases = steps * rates_ref[...]
    stamp = jnp.concatenate([jnp.cos(phases), jnp.sin(phases)], axis=1).astype(BF16)
    raw = jnp.dot(stamp, wt_buf[...], preferred_element_type=F32)
    conditioning = (raw * (1.0 / (1.0 + jnp.exp(-raw)))).astype(BF16)
    modulation = jnp.dot(conditioning, wa_buf[...], preferred_element_type=F32)
    views = [jnp.broadcast_to(modulation[a : a + 1], (16, 3 * D)) for a in range(AUG)]
    turned = jnp.concatenate(views + views, axis=0).T
    shift_ref[...] = turned[:D]
    scale_ref[...] = 1.0 + turned[D : 2 * D]
    gate_ref[...] = turned[2 * D :]

    for m in messages:
        m.wait_recv()
    for k in range(8):
        low = pltpu.roll(got_ref[2 * k], 96, 1)
        above = pltpu.roll(got_ref[2 * k + 2], 96, 1) if k < 7 else zero
        high = pltpu.roll(got_ref[2 * k + 1], 32, 1)
        below = pltpu.roll(got_ref[2 * k - 1], 32, 1) if k > 0 else zero
        four = jnp.where(lane < 96, low, above) + jnp.where(lane >= 32, high, below)
        for r in range(4):
            at = (4 * k + r) * 8
            rows_ref[at : at + 8, :] = pltpu.roll(four, 128 - 32 * r, 1) if r else four
    wide = lax.broadcasted_iota(jnp.int32, (SIDE, 128), 1) // SIDE
    halves = []
    for h in range(2):
        value = rows_ref[pl.ds(4 * h, SIDE, stride=8), :]
        for ch in range(1, 4):
            part = rows_ref[pl.ds(4 * h + ch, SIDE, stride=8), :]
            value = jnp.where(wide == ch, pltpu.roll(part, 32 * ch, 1), value)
        halves.append(value)
    by_channel = jnp.concatenate(halves, axis=1)
    source = lax.broadcasted_iota(jnp.int32, (256, 512), 0)
    goal = lax.broadcasted_iota(jnp.int32, (256, 512), 1)
    channel, column = source // SIDE, source % SIDE
    natural = column * 8 + channel
    apart = 256 + (channel // 4) * 128 + column * 4 + channel % 4
    spread = jnp.where((goal == natural) | (goal == apart), 1.0, 0.0).astype(BF16)
    placed = joined_three(
        jnp.dot(split_three(by_channel), spread, preferred_element_type=F32), SIDE
    )
    moments_ref[pl.ds(0, SIDE, stride=2), :] = placed[:, 0:128]
    moments_ref[pl.ds(1, SIDE, stride=2), :] = placed[:, 128:256]

    latent = placed[:, 256:384] + jnp.exp(0.5 * placed[:, 384:512]) * vae_ref[...]
    source = lax.broadcasted_iota(jnp.int32, (128, 128), 0)
    goal = lax.broadcasted_iota(jnp.int32, (128, 128), 1)
    maps = []
    for a in range(AUG):
        cell = goal // LC + crops_ref[1, a] - 2
        inside = (cell >= 0) & (cell < SIDE)
        mirror = (flips_ref[0, a] == 1).astype(jnp.int32)
        cell = cell + mirror * (SIDE - 1 - 2 * cell)
        match = inside & (source == cell * LC + goal % LC)
        maps.append(jnp.where(match, 1.0, 0.0).astype(BF16))
    columns = jnp.dot(
        split_three(latent), jnp.concatenate(maps, axis=1), preferred_element_type=F32
    )
    columns = joined_three(columns, SIDE)
    noised, noises = [], []
    for a in range(AUG):
        pads_ref[a] = jnp.zeros((40, 128), F32)
        pads_ref[a, 2 : 2 + SIDE, :] = columns[:, 128 * a : 128 * a + 128]
    for dr in range(2):
        for a in range(AUG):
            view = pads_ref[a, pl.ds(crops_ref[0, a] + dr, 16, stride=2), :]
            noise = noise_ref[pl.ds(dr * 4 + a, 16, stride=8), :]
            step = steps_ref[0, a]
            noised.append(table_ref[0, step] * view + table_ref[1, step] * noise)
            noises.append(noise)

    def patched(pieces):
        turned = jnp.concatenate(pieces, axis=0).T
        first, last = [], []
        for m in range(8):
            even = turned[16 * m : 16 * m + 8]
            odd = turned[16 * m + 8 : 16 * m + 16]
            first.append(jnp.where(lane < 64, even, pltpu.roll(odd, 64, 1)))
            last.append(jnp.where(lane < 64, pltpu.roll(even, 64, 1), odd))
        return jnp.concatenate(
            [jnp.concatenate(first, axis=1), jnp.concatenate(last, axis=1)], axis=0
        )

    patches = patched(noised).astype(BF16)
    target_ref[...] = patched(noises)

    which = lax.broadcasted_iota(jnp.int32, (96, TOK), 0)
    token = lax.broadcasted_iota(jnp.int32, (96, TOK), 1)
    cell = jnp.where(which < 48, token % 16, token // 64)
    marks = jnp.where(which % 16 == cell, 1.0, 0.0).astype(BF16)
    tok_ref[...] = lax.dot_general(
        jnp.concatenate([wp_ref[...], pos_ref[...]], axis=0),
        jnp.concatenate([patches, marks], axis=0),
        (((0,), (0,)), ((), ())),
        preferred_element_type=F32,
    )

    @pl.loop(0, TOK // WIDE)
    def _(m):
        at = pl.ds(pl.multiple_of(m * WIDE, WIDE), WIDE)
        value = tok_ref[:, at]
        center = value - jnp.sum(value, axis=0, keepdims=True) * (1.0 / D)
        variance = jnp.sum(center * center, axis=0, keepdims=True) * (1.0 / D)
        normed = center * lax.rsqrt(variance + norm_epsilon)
        out = normed * widened(scale_ref) + widened(shift_ref)
        modt_ref[:, at] = out.astype(BF16)
        mod_ref[at, :] = out.T.astype(BF16)

    def weights(w, k):
        near = all_ref[w, y_at(NY - k), :, 0].reshape(CHUNK // 2, D)
        other = all_ref[w, :, x_at(NX - k), 1].reshape(CHUNK // 2, D)
        return jnp.concatenate([near, other], axis=0)

    root = math.sqrt(2.0 / math.pi)

    def forward(k):
        for h in range(2):
            crossed[h, k].wait_recv()
        at = pl.ds(k * CHUNK, CHUNK)
        pre = jnp.dot(weights(0, k), modt_ref[...], preferred_element_type=F32)
        squared = pre * pre
        inner = pre * (squared * (root * 0.044715) + root)
        share = 0.5 * jnp.tanh(inner) + 0.5
        hidden = pre * share
        hid_ref[at, :] = hidden.astype(BF16)
        slope = (1.0 - share) * hidden * (squared * (6.0 * root * 0.044715) + 2.0 * root)
        slope_ref[at, :] = slope + share
        w2_ref[:, at] = weights(1, k).astype(F32).T.astype(BF16)

    def pass_on(k):
        for h in range(2):
            late[h, k].wait_recv()
            crossed[h, k].start()

    forward(0)
    pass_on(1)
    pass_on(3)
    forward(1)
    pass_on(2)
    forward(3)
    forward(2)

    own_ref[1] = jnp.zeros((8, 128), F32)

    @pl.loop(0, TOK // WIDE)
    def _(m):
        at = pl.ds(pl.multiple_of(m * WIDE, WIDE), WIDE)
        branch = jnp.dot(w2_ref[...], hid_ref[:, at], preferred_element_type=F32)
        gate = widened(gate_ref)
        mixed = tok_ref[:, at] + gate * branch
        center = mixed - jnp.sum(mixed, axis=0, keepdims=True) * (1.0 / D)
        variance = jnp.sum(center * center, axis=0, keepdims=True) * (1.0 / D)
        inverse = lax.rsqrt(variance + norm_epsilon)
        normed = center * inverse
        predicted = jnp.dot(wf_ref[...], normed.astype(BF16), preferred_element_type=F32)
        residue = predicted - target_ref[:, at]
        own_ref[1] += jnp.sum(residue * residue) * (1.0 / (TOK * 16))
        grad_pred = (residue * (2.0 / (TOK * 16))).astype(BF16)
        grad_normed = lax.dot_general(
            wf_ref[...], grad_pred, (((0,), (0,)), ((), ())), preferred_element_type=F32
        )
        mean = jnp.sum(grad_normed, axis=0, keepdims=True) * (1.0 / D)
        along = jnp.sum(grad_normed * normed, axis=0, keepdims=True) * (1.0 / D)
        grad_mixed = inverse * (grad_normed - mean - normed * along)
        grad_branch = gate * grad_mixed
        gbt_ref[:, at] = grad_branch.astype(BF16)
        gb_ref[at, :] = grad_branch.T.astype(BF16)

    square_ref[...] = jnp.zeros_like(square_ref)
    chosen = selected_ref[0, 0] == 1
    l0[0] = jnp.where(chosen, own_ref[1], 0.0)
    losses = [remote(l0.at[0], l0.at[1], l_send.at[0], l_recv.at[0], partner)]
    losses[0].start()

    def swap(half, k):
        if half == 0:
            at = (y_at(NY - k), slice(None), 0)
        else:
            at = (slice(None), x_at(NX - k), 1)
        return remote(
            send_ref.at[at], r0.at[at], q_send.at[half, k], q_recv.at[half, k], partner
        )

    for k in range(4):
        at = pl.ds(k * CHUNK, CHUNK)
        grad_hidden = jnp.dot(weights(1, k), gbt_ref[...], preferred_element_type=F32)
        grad_pre = (slope_ref[at, :] * grad_hidden).astype(BF16)
        grad_1 = jnp.dot(grad_pre, mod_ref[...], preferred_element_type=F32)
        grad_2 = jnp.dot(hid_ref[at, :], gb_ref[...], preferred_element_type=F32)
        grad_1 = jnp.where(chosen, grad_1, 0.0)
        grad_2 = jnp.where(chosen, grad_2, 0.0)
        kept = jnp.where(c == 0, grad_1, grad_2)
        sent = jnp.where(c == 0, grad_2, grad_1).astype(BF16)
        for h in range(2):
            rows = slice(h * CHUNK // 2, (h + 1) * CHUNK // 2)
            kept_half = kept[rows].reshape(4, HALF, D)
            sent_half = sent[rows].reshape(4, HALF, D)
            if h == 0:
                keep_ref[y_at(NY - k), :, 0] = kept_half
                send_ref[y_at(NY - k), :, 0] = sent_half
            else:
                keep_ref[:, x_at(NX - k), 1] = kept_half
                send_ref[:, x_at(NX - k), 1] = sent_half
            swap(h, k).start()
        square_ref[...] += jnp.sum(
            grad_1 * grad_1 + grad_2 * grad_2, axis=0, keepdims=True
        )

    total = jnp.sum(square_ref[...], axis=1, keepdims=True)
    factor = 1.0 / (jnp.sqrt(total * (1.0 / (2 * D * FF))) + clip_offset)
    own_ref[0] = jnp.broadcast_to(factor, (8, 128))
    factors = remote(own_ref.at[0], own_ref.at[2], l_send.at[7], l_recv.at[7], partner)
    factors.start()
    losses[0].wait_recv()
    l1[x] = l0[0] + l0[1]
    for k in range(1, NX):
        copy = remote(l1.at[x], l1.at[x], l_send.at[k], l_recv.at[k], {"fsdp_1": x_at(k)})
        copy.start()
        losses.append(copy)
    for k in range(4):
        for h in range(2):
            swap(h, k).wait_recv()
    factors.wait_recv()
    mine = own_ref[0, 0:1, 0:1]
    other = own_ref[2, 0:1, 0:1]

    def part(half, k, j):
        if half == 0:
            return (j, x_at(k), 0)
        return (y_at(k), j, 1)

    def chip(half, k, j):
        at = part(half, k, j)
        return keep_ref[at] * mine + r0[at].astype(F32) * other

    offsets = (2, 1, 3, 0)
    firsts = {}
    for group in range(2):
        for k in (2, 1, 3):
            for h in range(2):
                for q in (2 * group, 2 * group + 1):
                    value = chip(h, k, second_at(h, offsets[q]))
                    s1[h, k - 1, q] = value.astype(BF16)
                firsts[h, k, group] = remote(
                    s1.at[h, k - 1, pl.ds(2 * group, 2)],
                    r1.at[h, k - 1, pl.ds(2 * group, 2)],
                    s1_send.at[h, 2 * k + group],
                    s1_recv.at[h, 2 * k + group],
                    first_to(h, k),
                )
                firsts[h, k, group].start()
    for h in range(2):
        for q in range(4):
            acc[h, q] = chip(h, 0, second_at(h, offsets[q]))
    for copy in losses[1:]:
        copy.wait_recv()
    l2[y] = (l1[0] + l1[1]) + (l1[2] + l1[3])
    for k in range(1, NY):
        copy = remote(
            l2.at[y], l2.at[y], l_send.at[3 + k], l_recv.at[3 + k], {"fsdp_0": y_at(k)}
        )
        copy.start()
        losses.append(copy)
    seconds = {}
    for group in range(2):
        for h in range(2):
            for k in (1, 3, 2):
                firsts[h, k, group].wait_recv()
            for q in (2 * group, 2 * group + 1):
                k = offsets[q]
                value = (acc[h, q] + r1[h, 0, q].astype(F32)) + (
                    r1[h, 1, q].astype(F32) + r1[h, 2, q].astype(F32)
                )
                if k == 0:
                    acc[h, q] = value
                else:
                    c2[h, k - 1] = value.astype(BF16)
                    seconds[h, k] = remote(
                        c2.at[h, k - 1],
                        r2.at[h, k - 1],
                        s2_send.at[h, k],
                        s2_recv.at[h, k],
                        second_to(h, k),
                    )
                    seconds[h, k].start()
    for copy in losses[4:]:
        copy.wait_recv()
    at = USED_TILES
    tiles[at // PIECE, at % PIECE] = (l2[0] + l2[1]) + (l2[2] + l2[3])
    for t in range(USED_TILES + 1, TILES):
        tiles[t // PIECE, t % PIECE] = jnp.zeros((8, 128), F32)
    for h in range(2):
        for k in (1, 3, 2):
            seconds[h, k].wait_recv()
        value = (acc[h, 3] + r2[h, 0].astype(F32)) + (
            r2[h, 1].astype(F32) + r2[h, 2].astype(F32)
        )
        for i in range(HALF // 8):
            for n in range(D // 128):
                t = (h * (HALF // 8) + i) * (D // 128) + n
                tiles[t // PIECE, t % PIECE] = value[8 * i : 8 * i + 8, 128 * n : 128 * n + 128]

    order = (4, 3, 5, 2, 6, 1, 7)
    thirds = []
    for k in order:
        copy = remote(
            tiles.at[z_at(k)], r3.at[z], z_send.at[k], z_recv.at[k], {"dp_0": z_at(k)}
        )
        copy.start()
        thirds.append(copy)
    r3[z] = tiles[z]
    for copy in thirds:
        copy.wait_recv()
    value = r3[0]
    for k in range(1, NZ):
        value = value + r3[k]
    whole[c, z] = value
    spreads = {}
    for k in order:
        spreads[k] = remote(
            whole.at[c, z], whole.at[c, z], a_send.at[k], a_recv.at[k], {"dp_0": z_at(k)}
        )
        spreads[k].start()
    crossings = []
    for k in (0, 7, 1, 6, 2, 5, 3, 4):
        if k > 0:
            spreads[k].wait_recv()
        at = z_at(NZ - k) if k > 0 else z
        copy = remote(whole.at[c, at], whole.at[c, at], f_send.at[k], f_recv.at[k], partner)
        copy.start()
        crossings.append(copy)
    for copy in crossings:
        copy.wait_recv()
    for w in range(2):
        for t in range(USED_TILES):
            i, n = t // (D // 128), t % (D // 128)
            sum_ref[w, 8 * i : 8 * i + 8, 128 * n : 128 * n + 128] = whole[
                w, t // PIECE, t % PIECE
            ]
    total_ref[...] = whole[0, USED_TILES // PIECE, USED_TILES % PIECE]
    for k in range(4):
        for h in range(2):
            swap(h, k).wait_send()
    for group in (early, late, crossed, firsts, seconds, spreads):
        for copy in group.values():
            copy.wait_send()
    for group in (messages, losses, thirds, crossings, [factors]):
        for copy in group:
            copy.wait_send()


def finish_kernel(sum_ref, total_ref, moved_ref, n1_ref, n2_ref, *outs):
    u1_ref, u2_ref, mean_ref, moments_ref = outs
    u1_ref[...] = (sum_ref[0] + noise_weight * n1_ref[...]) * (1.0 / SELECTED)
    u2_ref[...] = (sum_ref[1] + noise_weight * n2_ref[...]) * (1.0 / SELECTED)
    mean_ref[...] = total_ref[0:1, 0:1] * (1.0 / SELECTED)
    moments_ref[...] = moved_ref[...]


def per_device(
    features,
    conv_weight,
    vae_noise,
    flips,
    crops,
    tsteps,
    diffusion_noise,
    selected,
    w_patch,
    w_time,
    w_ada,
    w_fc1,
    w_fc2,
    w_final,
    noise_fc1,
    noise_fc2,
):
    dma = pltpu.SemaphoreType.DMA
    pixels = features.reshape(TOK, FCH)
    taps = conv_weight.transpose(0, 1, 3, 2).reshape(72, FCH)
    views = diffusion_noise.reshape(AUG, SIDE, SIDE * LC).transpose(1, 0, 2)
    grid = (NY, NX, 2, HALF, D)
    tile = (8, 128)
    vmem = pltpu.VMEM
    sums, total, moved = pl.pallas_call(
        step_kernel,
        out_shape=(
            jax.ShapeDtypeStruct((2, SHARD, D), F32),
            jax.ShapeDtypeStruct(tile, F32),
            jax.ShapeDtypeStruct((2 * SIDE, 128), F32),
        ),
        in_specs=[HBM_SPEC] * 17,
        out_specs=(VMEM_SPEC,) * 3,
        scratch_shapes=[
            pltpu.SMEM((1, AUG), jnp.int32),
            pltpu.SMEM((2, AUG), jnp.int32),
            pltpu.SMEM((1, AUG), jnp.int32),
            pltpu.SMEM((1, 1), jnp.int32),
            pltpu.SMEM((2, TSTEPS), F32),
            vmem((TOK, FCH), BF16),
            vmem((72, FCH), BF16),
            vmem((SHARD, D), BF16),
            vmem((SHARD, D), BF16),
            vmem((SIDE, 128), F32),
            vmem((SIDE * AUG, 128), F32),
            vmem((16, D), BF16),
            vmem((96, D), BF16),
            vmem((1, 128), F32),
            vmem((256, D), BF16),
            vmem((D, 3 * D), BF16),
            vmem((16, D), BF16),
            vmem((2,) + grid, BF16),
            vmem((NDP,) + tile, F32),
            vmem((NDP,) + tile, F32),
            vmem((256, 128), F32),
            vmem((AUG, 40, 128), F32),
            vmem((D, 128), F32),
            vmem((D, 128), F32),
            vmem((D, 128), F32),
            vmem((D, TOK), F32),
            vmem((D, TOK), BF16),
            vmem((TOK, D), BF16),
            vmem((D, FF), BF16),
            vmem((FF, TOK), BF16),
            vmem((FF, TOK), F32),
            vmem((16, TOK), F32),
            vmem((D, TOK), BF16),
            vmem((TOK, D), BF16),
            vmem((1, D), F32),
            vmem((4,) + tile, F32),
            vmem(grid, F32),
            vmem(grid, BF16),
            vmem(grid, BF16),
            vmem((2, 3, 4, HALF, D), BF16),
            vmem((2, 3, 4, HALF, D), BF16),
            vmem((2, 4, HALF, D), F32),
            vmem((2, 3, HALF, D), BF16),
            vmem((2, 3, HALF, D), BF16),
            vmem((NZ, PIECE) + tile, F32),
            vmem((NZ, PIECE) + tile, F32),
            vmem((2, NZ, PIECE) + tile, F32),
            vmem((2,) + tile, F32),
            vmem((NX,) + tile, F32),
            vmem((NY,) + tile, F32),
        ]
        + [dma((2, 4))] * 10
        + [dma((2, 8))] * 2
        + [dma((NDP,))] * 2
        + [dma((NZ,))] * 8
        + [dma((17,))],
        compiler_params=pltpu.CompilerParams(
            collective_id=0, has_side_effects=True, vmem_limit_bytes=56 << 20
        ),
        name="step",
    )(
        flips.reshape(1, AUG),
        crops.reshape(AUG, 2).T,
        tsteps.reshape(1, AUG),
        selected,
        jnp.asarray(blend_tables()),
        pixels,
        taps,
        w_fc1.T,
        w_fc2.T,
        vae_noise.reshape(SIDE, SIDE * LC),
        views.reshape(SIDE * AUG, SIDE * LC),
        w_patch,
        jnp.asarray(position_rows()),
        jnp.asarray(time_rates()),
        w_time,
        w_ada,
        w_final.T,
    )
    update_1, update_2, mean_loss, moments = pl.pallas_call(
        finish_kernel,
        out_shape=(
            jax.ShapeDtypeStruct((SHARD, D), F32),
            jax.ShapeDtypeStruct((SHARD, D), F32),
            jax.ShapeDtypeStruct((1, 1), F32),
            jax.ShapeDtypeStruct((2 * SIDE, 128), F32),
        ),
        in_specs=[VMEM_SPEC] * 5,
        out_specs=(VMEM_SPEC,) * 4,
        name="finish",
    )(sums, total, moved, noise_fc1.T, noise_fc2.T)
    return (update_1.T, update_2.T, mean_loss.reshape(()), moments.reshape(1, 1, -1))


def solution(mesh):
    split = Mesh(mesh.devices.reshape(NZ, NC, NY, NX), DP + FSDP)
    return jax.shard_map(
        per_device,
        mesh=split,
        in_specs=(
            P(FSDP, None, DP, None, None),
            P(),
            P(DP, FSDP, None),
            P(DP, FSDP, None),
            P(DP, FSDP, None, None),
            P(DP, FSDP, None),
            P(DP, FSDP, None, None),
            P(DP, FSDP),
            P(),
            P(),
            P(),
            P(None, FSDP),
            P(None, FSDP),
            P(),
            P(None, FSDP),
            P(None, FSDP),
        ),
        out_specs=(P(None, FSDP), P(None, FSDP), P(), P(DP, FSDP, None)),
        check_vma=False,
    )
```

```python
import math

import jax
import jax.numpy as jnp
import ml_dtypes
import numpy as np
from jax import lax
from jax.experimental import pallas as pl
from jax.experimental.pallas import tpu as pltpu
from jax.sharding import Mesh
from jax.sharding import PartitionSpec as P

MESH = pl.DeviceIdType.MESH
DP = ("dp_0", "dp_1")
FSDP = ("fsdp_0", "fsdp_1")
NZ, NC, NY, NX = 8, 2, 4, 4
NDP = NZ * NC
D, FF, TOK, FCH = 384, 1536, 1024, 512
SHARD = FF // (NY * NX)
HALF = SHARD // 2
SIDE, LC, AUG, TSTEPS = 32, 4, 4, 1000
SELECTED = 128
CHUNK = 384
WIDE = 1024
BATCHES, ROWS = 3, 16
clip_offset = 1e-05
noise_weight = 16.0
norm_epsilon = 1e-06
VMEM_SPEC = pl.BlockSpec(memory_space=pltpu.VMEM)
HBM_SPEC = pl.BlockSpec(memory_space=pltpu.HBM)
SMEM_SPEC = pl.BlockSpec(memory_space=pltpu.SMEM)
F32, BF16 = jnp.float32, jnp.bfloat16


def three_parts(table):
    high = table.astype(np.float32).astype(ml_dtypes.bfloat16)
    rest = table.astype(np.float32) - high.astype(np.float32)
    middle = rest.astype(ml_dtypes.bfloat16)
    low = (rest - middle.astype(np.float32)).astype(ml_dtypes.bfloat16)
    return high, middle, low


def position_rows():
    side, quarter = SIDE // 2, D // 4
    frequency = 1.0 / 10000.0 ** (np.arange(quarter) / quarter)
    angles = np.arange(side)[:, None] * frequency[None, :]
    line = np.concatenate([np.sin(angles), np.cos(angles)], axis=1)
    parts = three_parts(line)
    zero = np.zeros_like(parts[0])
    rows = [np.concatenate([p, zero], axis=1) for p in parts]
    cols = [np.concatenate([zero, p], axis=1) for p in parts]
    return np.concatenate(rows + cols, axis=0)


def blend_tables():
    beta = 0.0001 + np.arange(TSTEPS) * (0.02 - 0.0001) / (TSTEPS - 1)
    alpha_bar = np.cumprod(1.0 - beta)
    return np.stack([np.sqrt(alpha_bar), np.sqrt(1.0 - alpha_bar)]).astype(np.float32)


def time_rates():
    steps = np.arange(128, dtype=np.float32)
    scaled = np.float32(-math.log(10000.0)) * steps / np.float32(128)
    return np.exp(scaled).astype(np.float32).reshape(1, 128)


def place():
    return tuple(lax.axis_index(a) for a in ("dp_0", "dp_1", "fsdp_0", "fsdp_1"))


def widened(ref):
    return jnp.concatenate([ref[...]] * (WIDE // 128), axis=1)


def split_three(value):
    high = value.astype(BF16)
    rest = value - high.astype(F32)
    middle = rest.astype(BF16)
    low = (rest - middle.astype(F32)).astype(BF16)
    return jnp.concatenate([high, middle, low], axis=0)


def joined_three(value, rows):
    return (value[2 * rows :] + value[rows : 2 * rows]) + value[:rows]


def step_kernel(*refs):
    inputs, (sum_ref, total_ref, moments_ref) = refs[:17], refs[17:20]
    buffers, scratch = refs[20:37], refs[37:]
    (flips_ref, crops_ref, steps_ref, selected_ref, table_ref) = buffers[:5]
    (x_buf, taps_ref, w1_ref, w2s_ref, vae_ref, noise_ref, wp_ref) = buffers[5:12]
    (pos_ref, rates_ref, wt_buf, wa_buf, wf_ref) = buffers[12:]
    (all_ref, msg_ref, got_ref) = scratch[:3]
    (rows_ref, pads_ref, shift_ref, scale_ref, gate_ref, tok_ref, modt_ref) = scratch[3:10]
    (mod_ref, w2_ref, hid_ref, slope_ref, target_ref, gbt_ref, gb_ref) = scratch[10:17]
    (square_ref, own_ref, keep_ref, send_ref, r0, s1, r1, acc, c2, r2) = scratch[17:27]
    (tiles, r3, whole, l0, l1, l2, l3) = scratch[27:34]
    (g1_send, g1_recv, g2_send, g2_recv, p_send, p_recv) = scratch[34:40]
    (q_send, q_recv, s1_send, s1_recv, s2_send, s2_recv) = scratch[40:46]
    (z_send, z_recv, a_send, a_recv) = scratch[46:50]
    (m_send, m_recv, l_send, l_recv, f_send, f_recv, c_sem) = scratch[50:]
    z, c, y, x = place()
    me = z * NC + c
    partner = {"dp_1": 1 - c}
    lane = lax.broadcasted_iota(jnp.int32, (8, 128), 1)
    zero = jnp.zeros((8, 128), F32)

    def x_at(k):
        return lax.rem(x + k, NX)

    def y_at(k):
        return lax.rem(y + k, NY)

    def z_at(k):
        return lax.rem(z + k, NZ)

    def dp_at(k):
        return lax.rem(me + k, NDP)

    def dp_device(k):
        other = dp_at(k)
        return {"dp_0": other // NC, "dp_1": lax.rem(other, NC)}

    def remote(src, dst, send, recv, device):
        return pltpu.make_async_remote_copy(
            src_ref=src,
            dst_ref=dst,
            send_sem=send,
            recv_sem=recv,
            device_id=device,
            device_id_type=MESH,
        )

    def first_to(half, k):
        return {"fsdp_1": x_at(k)} if half == 0 else {"fsdp_0": y_at(k)}

    def second_to(half, k):
        return {"fsdp_0": y_at(k)} if half == 0 else {"fsdp_1": x_at(k)}

    def second_at(half, k):
        return y_at(k) if half == 0 else x_at(k)

    barrier = pltpu.get_barrier_semaphore()
    for k in range(1, NX):
        pl.semaphore_signal(barrier, 1, device_id={"fsdp_1": x_at(k)}, device_id_type=MESH)
        pl.semaphore_signal(barrier, 1, device_id={"fsdp_0": y_at(k)}, device_id_type=MESH)
    for k in range(1, NDP):
        pl.semaphore_signal(barrier, 1, device_id=dp_device(k), device_id_type=MESH)
    loads = [
        pltpu.make_async_copy(inputs[i], buffers[i], c_sem.at[i]) for i in range(len(inputs))
    ]
    shards, pictures = (7, 8), (5, 6)
    for i in shards + pictures:
        loads[i].start()
    for i in range(len(inputs)):
        if i not in shards + pictures:
            loads[i].start()
    for i in shards:
        loads[i].wait()
    own_shard = jnp.where(c == 0, w1_ref[...], w2s_ref[...])
    all_ref[c, y, x, 0] = own_shard[:HALF]
    all_ref[c, y, x, 1] = own_shard[HALF:]
    pl.semaphore_wait(barrier, NX - 1 + NY - 1 + NDP - 1)

    def message(k):
        return remote(
            msg_ref.at[dp_at(k)], got_ref.at[me], m_send.at[k], m_recv.at[k], dp_device(k)
        )

    def gather_first(half, k):
        at = all_ref.at[c, y, x, half]
        return remote(at, at, g1_send.at[half, k], g1_recv.at[half, k], first_to(half, k))

    def line(half, k):
        if half == 0:
            return all_ref.at[c, y_at(NY - k), :, 0]
        return all_ref.at[c, :, x_at(NX - k), 1]

    def gather_second(half, k):
        at = line(half, 0)
        return remote(at, at, g2_send.at[half, k], g2_recv.at[half, k], second_to(half, k))

    def across(half, k):
        at = line(half, k)
        return remote(at, at, p_send.at[half, k], p_recv.at[half, k], partner)

    messages = [message(k) for k in range(1, NDP)]
    early = {(h, k): gather_first(h, k) for k in (1, 3, 2) for h in range(2)}
    late = {(h, k): gather_second(h, k) for k in (1, 3, 2) for h in range(2)}
    crossed = {(h, k): across(h, k) for k in (0, 1, 3, 2) for h in range(2)}
    for copy in early.values():
        copy.start()
    for i in pictures:
        loads[i].wait()
    taps = lax.dot_general(
        taps_ref[...], x_buf[...], (((1,), (1,)), ((), ())), preferred_element_type=F32
    )
    col = lane % SIDE

    def tap(dy, dx, v):
        at = (dy * 3 + dx) * 8
        return taps[at : at + 8, 128 * v : 128 * v + 128]

    for v in range(8):
        rows = []
        for dy in range(3):
            left = jnp.where(col == 0, zero, pltpu.roll(tap(dy, 0, v), 1, 1))
            right = jnp.where(col == SIDE - 1, zero, pltpu.roll(tap(dy, 2, v), 127, 1))
            rows.append(left + tap(dy, 1, v) + right)
        for odd in range(2):
            parts = [pltpu.roll(r, 64, 1) if odd else r for r in rows]
            parts = [jnp.where(lane < 64, r, zero) for r in parts]
            msg_ref[2 * v + odd] = (
                parts[2] + pltpu.roll(parts[1], 32, 1) + pltpu.roll(parts[0], 64, 1)
            )
    got_ref[me] = msg_ref[me]
    for m in messages:
        m.start()
    for copy in early.values():
        copy.wait_recv()
    for copy in late.values():
        copy.start()
    for h in range(2):
        crossed[h, 0].start()
    for i in range(len(inputs)):
        if i not in shards + pictures:
            loads[i].wait()

    row = lax.broadcasted_iota(jnp.int32, (8, 128), 0)
    steps = jnp.zeros((8, 128), F32)
    for a in range(AUG):
        steps = jnp.where(row == a, steps_ref[0, a].astype(F32), steps)
    phases = steps * rates_ref[...]
    stamp = jnp.concatenate([jnp.cos(phases), jnp.sin(phases)], axis=1).astype(BF16)
    raw = jnp.dot(stamp, wt_buf[...], preferred_element_type=F32)
    conditioning = (raw * (1.0 / (1.0 + jnp.exp(-raw)))).astype(BF16)
    modulation = jnp.dot(conditioning, wa_buf[...], preferred_element_type=F32)
    views = [jnp.broadcast_to(modulation[a : a + 1], (16, 3 * D)) for a in range(AUG)]
    turned = jnp.concatenate(views + views, axis=0).T
    shift_ref[...] = turned[:D]
    scale_ref[...] = 1.0 + turned[D : 2 * D]
    gate_ref[...] = turned[2 * D :]

    for m in messages:
        m.wait_recv()
    for k in range(8):
        low = pltpu.roll(got_ref[2 * k], 96, 1)
        above = pltpu.roll(got_ref[2 * k + 2], 96, 1) if k < 7 else zero
        high = pltpu.roll(got_ref[2 * k + 1], 32, 1)
        below = pltpu.roll(got_ref[2 * k - 1], 32, 1) if k > 0 else zero
        four = jnp.where(lane < 96, low, above) + jnp.where(lane >= 32, high, below)
        for r in range(4):
            at = (4 * k + r) * 8
            rows_ref[at : at + 8, :] = pltpu.roll(four, 128 - 32 * r, 1) if r else four
    wide = lax.broadcasted_iota(jnp.int32, (SIDE, 128), 1) // SIDE
    halves = []
    for h in range(2):
        value = rows_ref[pl.ds(4 * h, SIDE, stride=8), :]
        for ch in range(1, 4):
            part = rows_ref[pl.ds(4 * h + ch, SIDE, stride=8), :]
            value = jnp.where(wide == ch, pltpu.roll(part, 32 * ch, 1), value)
        halves.append(value)
    by_channel = jnp.concatenate(halves, axis=1)
    source = lax.broadcasted_iota(jnp.int32, (256, 512), 0)
    goal = lax.broadcasted_iota(jnp.int32, (256, 512), 1)
    channel, column = source // SIDE, source % SIDE
    natural = column * 8 + channel
    apart = 256 + (channel // 4) * 128 + column * 4 + channel % 4
    spread = jnp.where((goal == natural) | (goal == apart), 1.0, 0.0).astype(BF16)
    placed = joined_three(
        jnp.dot(split_three(by_channel), spread, preferred_element_type=F32), SIDE
    )
    moments_ref[pl.ds(0, SIDE, stride=2), :] = placed[:, 0:128]
    moments_ref[pl.ds(1, SIDE, stride=2), :] = placed[:, 128:256]

    latent = placed[:, 256:384] + jnp.exp(0.5 * placed[:, 384:512]) * vae_ref[...]
    source = lax.broadcasted_iota(jnp.int32, (128, 128), 0)
    goal = lax.broadcasted_iota(jnp.int32, (128, 128), 1)
    maps = []
    for a in range(AUG):
        cell = goal // LC + crops_ref[1, a] - 2
        inside = (cell >= 0) & (cell < SIDE)
        mirror = (flips_ref[0, a] == 1).astype(jnp.int32)
        cell = cell + mirror * (SIDE - 1 - 2 * cell)
        match = inside & (source == cell * LC + goal % LC)
        maps.append(jnp.where(match, 1.0, 0.0).astype(BF16))
    columns = jnp.dot(
        split_three(latent), jnp.concatenate(maps, axis=1), preferred_element_type=F32
    )
    columns = joined_three(columns, SIDE)
    noised, noises = [], []
    for a in range(AUG):
        pads_ref[a] = jnp.zeros((40, 128), F32)
        pads_ref[a, 2 : 2 + SIDE, :] = columns[:, 128 * a : 128 * a + 128]
    for dr in range(2):
        for a in range(AUG):
            view = pads_ref[a, pl.ds(crops_ref[0, a] + dr, 16, stride=2), :]
            noise = noise_ref[pl.ds(dr * 4 + a, 16, stride=8), :]
            step = steps_ref[0, a]
            noised.append(table_ref[0, step] * view + table_ref[1, step] * noise)
            noises.append(noise)

    def patched(pieces):
        turned = jnp.concatenate(pieces, axis=0).T
        first, last = [], []
        for m in range(8):
            even = turned[16 * m : 16 * m + 8]
            odd = turned[16 * m + 8 : 16 * m + 16]
            first.append(jnp.where(lane < 64, even, pltpu.roll(odd, 64, 1)))
            last.append(jnp.where(lane < 64, pltpu.roll(even, 64, 1), odd))
        return jnp.concatenate(
            [jnp.concatenate(first, axis=1), jnp.concatenate(last, axis=1)], axis=0
        )

    patches = patched(noised).astype(BF16)
    target_ref[...] = patched(noises)

    which = lax.broadcasted_iota(jnp.int32, (96, TOK), 0)
    token = lax.broadcasted_iota(jnp.int32, (96, TOK), 1)
    cell = jnp.where(which < 48, token % 16, token // 64)
    marks = jnp.where(which % 16 == cell, 1.0, 0.0).astype(BF16)
    tok_ref[...] = lax.dot_general(
        jnp.concatenate([wp_ref[...], pos_ref[...]], axis=0),
        jnp.concatenate([patches, marks], axis=0),
        (((0,), (0,)), ((), ())),
        preferred_element_type=F32,
    )

    @pl.loop(0, TOK // WIDE)
    def _(m):
        at = pl.ds(pl.multiple_of(m * WIDE, WIDE), WIDE)
        value = tok_ref[:, at]
        center = value - jnp.sum(value, axis=0, keepdims=True) * (1.0 / D)
        variance = jnp.sum(center * center, axis=0, keepdims=True) * (1.0 / D)
        normed = center * lax.rsqrt(variance + norm_epsilon)
        out = normed * widened(scale_ref) + widened(shift_ref)
        modt_ref[:, at] = out.astype(BF16)
        mod_ref[at, :] = out.T.astype(BF16)

    def weights(w, k):
        near = all_ref[w, y_at(NY - k), :, 0].reshape(CHUNK // 2, D)
        other = all_ref[w, :, x_at(NX - k), 1].reshape(CHUNK // 2, D)
        return jnp.concatenate([near, other], axis=0)

    root = math.sqrt(2.0 / math.pi)

    def forward(k):
        for h in range(2):
            crossed[h, k].wait_recv()
        at = pl.ds(k * CHUNK, CHUNK)
        pre = jnp.dot(weights(0, k), modt_ref[...], preferred_element_type=F32)
        squared = pre * pre
        inner = pre * (squared * (root * 0.044715) + root)
        share = 0.5 * jnp.tanh(inner) + 0.5
        hidden = pre * share
        hid_ref[at, :] = hidden.astype(BF16)
        slope = (1.0 - share) * hidden * (squared * (6.0 * root * 0.044715) + 2.0 * root)
        slope_ref[at, :] = slope + share
        w2_ref[:, at] = weights(1, k).astype(F32).T.astype(BF16)

    def pass_on(k):
        for h in range(2):
            late[h, k].wait_recv()
            crossed[h, k].start()

    forward(0)
    pass_on(1)
    pass_on(3)
    forward(1)
    pass_on(2)
    forward(3)
    forward(2)

    own_ref[1] = jnp.zeros((8, 128), F32)

    @pl.loop(0, TOK // WIDE)
    def _(m):
        at = pl.ds(pl.multiple_of(m * WIDE, WIDE), WIDE)
        branch = jnp.dot(w2_ref[...], hid_ref[:, at], preferred_element_type=F32)
        gate = widened(gate_ref)
        mixed = tok_ref[:, at] + gate * branch
        center = mixed - jnp.sum(mixed, axis=0, keepdims=True) * (1.0 / D)
        variance = jnp.sum(center * center, axis=0, keepdims=True) * (1.0 / D)
        inverse = lax.rsqrt(variance + norm_epsilon)
        normed = center * inverse
        predicted = jnp.dot(wf_ref[...], normed.astype(BF16), preferred_element_type=F32)
        residue = predicted - target_ref[:, at]
        own_ref[1] += jnp.sum(residue * residue) * (1.0 / (TOK * 16))
        grad_pred = (residue * (2.0 / (TOK * 16))).astype(BF16)
        grad_normed = lax.dot_general(
            wf_ref[...], grad_pred, (((0,), (0,)), ((), ())), preferred_element_type=F32
        )
        mean = jnp.sum(grad_normed, axis=0, keepdims=True) * (1.0 / D)
        along = jnp.sum(grad_normed * normed, axis=0, keepdims=True) * (1.0 / D)
        grad_mixed = inverse * (grad_normed - mean - normed * along)
        grad_branch = gate * grad_mixed
        gbt_ref[:, at] = grad_branch.astype(BF16)
        gb_ref[at, :] = grad_branch.T.astype(BF16)

    square_ref[...] = jnp.zeros_like(square_ref)
    chosen = selected_ref[0, 0] == 1
    l0[0] = jnp.where(chosen, own_ref[1], 0.0)
    losses = [remote(l0.at[0], l0.at[1], l_send.at[0], l_recv.at[0], partner)]
    losses[0].start()

    def swap(half, k):
        if half == 0:
            at = (y_at(NY - k), slice(None), 0)
        else:
            at = (slice(None), x_at(NX - k), 1)
        return remote(
            send_ref.at[at], r0.at[at], q_send.at[half, k], q_recv.at[half, k], partner
        )

    for k in range(4):
        at = pl.ds(k * CHUNK, CHUNK)
        grad_hidden = jnp.dot(weights(1, k), gbt_ref[...], preferred_element_type=F32)
        grad_pre = (slope_ref[at, :] * grad_hidden).astype(BF16)
        grad_1 = jnp.dot(grad_pre, mod_ref[...], preferred_element_type=F32)
        grad_2 = jnp.dot(hid_ref[at, :], gb_ref[...], preferred_element_type=F32)
        grad_1 = jnp.where(chosen, grad_1, 0.0)
        grad_2 = jnp.where(chosen, grad_2, 0.0)
        kept = jnp.where(c == 0, grad_1, grad_2)
        sent = jnp.where(c == 0, grad_2, grad_1).astype(BF16)
        for h in range(2):
            rows = slice(h * CHUNK // 2, (h + 1) * CHUNK // 2)
            kept_half = kept[rows].reshape(4, HALF, D)
            sent_half = sent[rows].reshape(4, HALF, D)
            if h == 0:
                keep_ref[y_at(NY - k), :, 0] = kept_half
                send_ref[y_at(NY - k), :, 0] = sent_half
            else:
                keep_ref[:, x_at(NX - k), 1] = kept_half
                send_ref[:, x_at(NX - k), 1] = sent_half
            swap(h, k).start()
        square_ref[...] += jnp.sum(
            grad_1 * grad_1 + grad_2 * grad_2, axis=0, keepdims=True
        )

    total = jnp.sum(square_ref[...], axis=1, keepdims=True)
    factor = 1.0 / (jnp.sqrt(total * (1.0 / (2 * D * FF))) + clip_offset)
    own_ref[0] = jnp.broadcast_to(factor, (8, 128))
    factors = remote(own_ref.at[0], own_ref.at[2], l_send.at[7], l_recv.at[7], partner)
    factors.start()
    losses[0].wait_recv()
    l1[x] = l0[0] + l0[1]
    for k in range(1, NX):
        copy = remote(l1.at[x], l1.at[x], l_send.at[k], l_recv.at[k], {"fsdp_1": x_at(k)})
        copy.start()
        losses.append(copy)
    for k in range(4):
        for h in range(2):
            swap(h, k).wait_recv()
    factors.wait_recv()
    mine = own_ref[0, 0:1, 0:1]
    other = own_ref[2, 0:1, 0:1]

    def chip(half, k, j, b):
        rows = pl.ds(b * ROWS, ROWS)
        at = (j, x_at(k), 0, rows) if half == 0 else (y_at(k), j, 1, rows)
        return keep_ref[at] * mine + r0[at].astype(F32) * other

    offsets = (2, 1, 3, 0)
    firsts, seconds, thirds, spreads, crossings = {}, {}, {}, {}, {}
    for b in range(BATCHES):
        for k in (2, 1, 3):
            for h in range(2):
                for q in range(4):
                    value = chip(h, k, second_at(h, offsets[q]), b)
                    s1[b, h, k - 1, q] = value.astype(BF16)
                firsts[b, h, k] = remote(
                    s1.at[b, h, k - 1],
                    r1.at[b, h, k - 1],
                    s1_send.at[b, h, k],
                    s1_recv.at[b, h, k],
                    first_to(h, k),
                )
                firsts[b, h, k].start()
    for b in range(BATCHES):
        for h in range(2):
            for q in range(4):
                acc[b, h, q] = chip(h, 0, second_at(h, offsets[q]), b)
    for copy in losses[1:]:
        copy.wait_recv()
    l2[y] = (l1[0] + l1[1]) + (l1[2] + l1[3])
    for k in range(1, NY):
        copy = remote(
            l2.at[y], l2.at[y], l_send.at[3 + k], l_recv.at[3 + k], {"fsdp_0": y_at(k)}
        )
        copy.start()
        losses.append(copy)

    def add_first(b):
        for h in range(2):
            for k in (1, 3, 2):
                firsts[b, h, k].wait_recv()
            for q in range(4):
                k = offsets[q]
                value = (acc[b, h, q] + r1[b, h, 0, q].astype(F32)) + (
                    r1[b, h, 1, q].astype(F32) + r1[b, h, 2, q].astype(F32)
                )
                if k == 0:
                    acc[b, h, q] = value
                else:
                    c2[b, h, k - 1] = value.astype(BF16)
                    seconds[b, h, k] = remote(
                        c2.at[b, h, k - 1],
                        r2.at[b, h, k - 1],
                        s2_send.at[b, h, k],
                        s2_recv.at[b, h, k],
                        second_to(h, k),
                    )
                    seconds[b, h, k].start()

    order = (4, 3, 5, 2, 6, 1, 7)

    def add_second(b):
        for h in range(2):
            for k in (1, 3, 2):
                seconds[b, h, k].wait_recv()
            value = (acc[b, h, 3] + r2[b, h, 0].astype(F32)) + (
                r2[b, h, 1].astype(F32) + r2[b, h, 2].astype(F32)
            )
            for i in range(4):
                tiles[b, 4 * h + i] = value[4 * i : 4 * i + 4]
        for k in order:
            thirds[b, k] = remote(
                tiles.at[b, z_at(k)],
                r3.at[b, z],
                z_send.at[b, k],
                z_recv.at[b, k],
                {"dp_0": z_at(k)},
            )
            thirds[b, k].start()
        r3[b, z] = tiles[b, z]

    def add_third(b):
        for k in order:
            thirds[b, k].wait_recv()
        value = r3[b, 0]
        for k in range(1, NZ):
            value = value + r3[b, k]
        whole[c, b, z] = value
        for k in order:
            at = whole.at[c, b, z]
            spreads[b, k] = remote(
                at, at, a_send.at[b, k], a_recv.at[b, k], {"dp_0": z_at(k)}
            )
            spreads[b, k].start()

    def cross(b):
        for k in order:
            spreads[b, k].wait_recv()
        at = whole.at[c, b]
        crossings[b] = remote(at, at, f_send.at[b], f_recv.at[b], partner)
        crossings[b].start()

    add_first(0)
    add_first(1)
    add_second(0)
    for copy in losses[4:]:
        copy.wait_recv()
    l3[z] = (l2[0] + l2[1]) + (l2[2] + l2[3])
    for k in range(1, NZ):
        copy = remote(
            l3.at[z], l3.at[z], l_send.at[7 + k], l_recv.at[7 + k], {"dp_0": z_at(k)}
        )
        copy.start()
        losses.append(copy)
    add_first(2)
    add_second(1)
    add_third(0)
    add_second(2)
    add_third(1)
    cross(0)
    add_third(2)
    cross(1)
    cross(2)
    for copy in losses[7:]:
        copy.wait_recv()
    value = l3[0]
    for k in range(1, NZ):
        value = value + l3[k]
    total_ref[...] = value
    for b in range(BATCHES):
        crossings[b].wait_recv()
        for w in range(2):
            for i in range(NZ):
                at = (i // 4) * HALF + b * ROWS + (i % 4) * 4
                sum_ref[w, at : at + 4, :] = whole[w, b, i]
    for k in range(4):
        for h in range(2):
            swap(h, k).wait_send()
    for group in (early, late, crossed, firsts, seconds, thirds, spreads, crossings):
        for copy in group.values():
            copy.wait_send()
    for group in (messages, losses, [factors]):
        for copy in group:
            copy.wait_send()


def finish_kernel(sum_ref, total_ref, moved_ref, n1_ref, n2_ref, *outs):
    u1_ref, u2_ref, mean_ref, moments_ref = outs
    u1_ref[...] = (sum_ref[0] + noise_weight * n1_ref[...]) * (1.0 / SELECTED)
    u2_ref[...] = (sum_ref[1] + noise_weight * n2_ref[...]) * (1.0 / SELECTED)
    mean_ref[...] = total_ref[0:1, 0:1] * (1.0 / SELECTED)
    moments_ref[...] = moved_ref[...]


def per_device(
    features,
    conv_weight,
    vae_noise,
    flips,
    crops,
    tsteps,
    diffusion_noise,
    selected,
    w_patch,
    w_time,
    w_ada,
    w_fc1,
    w_fc2,
    w_final,
    noise_fc1,
    noise_fc2,
):
    dma = pltpu.SemaphoreType.DMA
    pixels = features.reshape(TOK, FCH)
    taps = conv_weight.transpose(0, 1, 3, 2).reshape(72, FCH)
    views = diffusion_noise.reshape(AUG, SIDE, SIDE * LC).transpose(1, 0, 2)
    grid = (NY, NX, 2, HALF, D)
    tile = (8, 128)
    vmem = pltpu.VMEM
    sums, total, moved = pl.pallas_call(
        step_kernel,
        out_shape=(
            jax.ShapeDtypeStruct((2, SHARD, D), F32),
            jax.ShapeDtypeStruct(tile, F32),
            jax.ShapeDtypeStruct((2 * SIDE, 128), F32),
        ),
        in_specs=[HBM_SPEC] * 17,
        out_specs=(VMEM_SPEC,) * 3,
        scratch_shapes=[
            pltpu.SMEM((1, AUG), jnp.int32),
            pltpu.SMEM((2, AUG), jnp.int32),
            pltpu.SMEM((1, AUG), jnp.int32),
            pltpu.SMEM((1, 1), jnp.int32),
            pltpu.SMEM((2, TSTEPS), F32),
            vmem((TOK, FCH), BF16),
            vmem((72, FCH), BF16),
            vmem((SHARD, D), BF16),
            vmem((SHARD, D), BF16),
            vmem((SIDE, 128), F32),
            vmem((SIDE * AUG, 128), F32),
            vmem((16, D), BF16),
            vmem((96, D), BF16),
            vmem((1, 128), F32),
            vmem((256, D), BF16),
            vmem((D, 3 * D), BF16),
            vmem((16, D), BF16),
            vmem((2,) + grid, BF16),
            vmem((NDP,) + tile, F32),
            vmem((NDP,) + tile, F32),
            vmem((256, 128), F32),
            vmem((AUG, 40, 128), F32),
            vmem((D, 128), F32),
            vmem((D, 128), F32),
            vmem((D, 128), F32),
            vmem((D, TOK), F32),
            vmem((D, TOK), BF16),
            vmem((TOK, D), BF16),
            vmem((D, FF), BF16),
            vmem((FF, TOK), BF16),
            vmem((FF, TOK), F32),
            vmem((16, TOK), F32),
            vmem((D, TOK), BF16),
            vmem((TOK, D), BF16),
            vmem((1, D), F32),
            vmem((4,) + tile, F32),
            vmem(grid, F32),
            vmem(grid, BF16),
            vmem(grid, BF16),
            vmem((BATCHES, 2, 3, 4, ROWS, D), BF16),
            vmem((BATCHES, 2, 3, 4, ROWS, D), BF16),
            vmem((BATCHES, 2, 4, ROWS, D), F32),
            vmem((BATCHES, 2, 3, ROWS, D), BF16),
            vmem((BATCHES, 2, 3, ROWS, D), BF16),
            vmem((BATCHES, NZ, 4, D), F32),
            vmem((BATCHES, NZ, 4, D), F32),
            vmem((2, BATCHES, NZ, 4, D), F32),
            vmem((2,) + tile, F32),
            vmem((NX,) + tile, F32),
            vmem((NY,) + tile, F32),
            vmem((NZ,) + tile, F32),
        ]
        + [dma((2, 4))] * 8
        + [dma((BATCHES, 2, 4))] * 4
        + [dma((BATCHES, NZ))] * 4
        + [dma((NDP,))] * 4
        + [dma((BATCHES,))] * 2
        + [dma((17,))],
        compiler_params=pltpu.CompilerParams(
            collective_id=0, has_side_effects=True, vmem_limit_bytes=56 << 20
        ),
        name="step",
    )(
        flips.reshape(1, AUG),
        crops.reshape(AUG, 2).T,
        tsteps.reshape(1, AUG),
        selected,
        jnp.asarray(blend_tables()),
        pixels,
        taps,
        w_fc1.T,
        w_fc2.T,
        vae_noise.reshape(SIDE, SIDE * LC),
        views.reshape(SIDE * AUG, SIDE * LC),
        w_patch,
        jnp.asarray(position_rows()),
        jnp.asarray(time_rates()),
        w_time,
        w_ada,
        w_final.T,
    )
    update_1, update_2, mean_loss, moments = pl.pallas_call(
        finish_kernel,
        out_shape=(
            jax.ShapeDtypeStruct((SHARD, D), F32),
            jax.ShapeDtypeStruct((SHARD, D), F32),
            jax.ShapeDtypeStruct((1, 1), F32),
            jax.ShapeDtypeStruct((2 * SIDE, 128), F32),
        ),
        in_specs=[VMEM_SPEC] * 5,
        out_specs=(VMEM_SPEC,) * 4,
        name="finish",
    )(sums, total, moved, noise_fc1.T, noise_fc2.T)
    return (update_1.T, update_2.T, mean_loss.reshape(()), moments.reshape(1, 1, -1))


def solution(mesh):
    split = Mesh(mesh.devices.reshape(NZ, NC, NY, NX), DP + FSDP)
    return jax.shard_map(
        per_device,
        mesh=split,
        in_specs=(
            P(FSDP, None, DP, None, None),
            P(),
            P(DP, FSDP, None),
            P(DP, FSDP, None),
            P(DP, FSDP, None, None),
            P(DP, FSDP, None),
            P(DP, FSDP, None, None),
            P(DP, FSDP),
            P(),
            P(),
            P(),
            P(None, FSDP),
            P(None, FSDP),
            P(),
            P(None, FSDP),
            P(None, FSDP),
        ),
        out_specs=(P(None, FSDP), P(None, FSDP), P(), P(DP, FSDP, None)),
        check_vma=False,
    )
```

```python
import math

import jax
import jax.numpy as jnp
import ml_dtypes
import numpy as np
from jax import lax
from jax.experimental import pallas as pl
from jax.experimental.pallas import tpu as pltpu
from jax.sharding import Mesh
from jax.sharding import PartitionSpec as P

MESH = pl.DeviceIdType.MESH
DP = ("dp_0", "dp_1")
FSDP = ("fsdp_0", "fsdp_1")
NZ, NC, NY, NX = 8, 2, 4, 4
NDP = NZ * NC
D, FF, TOK, FCH = 384, 1536, 1024, 512
SHARD = FF // (NY * NX)
HALF = SHARD // 2
SIDE, LC, AUG, TSTEPS = 32, 4, 4, 1000
SELECTED = 128
CHUNK = 384
WIDE = 1024
PIECE = 5
FAR = (3, 4, 5)
TILES = NZ * PIECE
USED_TILES = (SHARD // 8) * (D // 128)
clip_offset = 1e-05
noise_weight = 16.0
norm_epsilon = 1e-06
VMEM_SPEC = pl.BlockSpec(memory_space=pltpu.VMEM)
HBM_SPEC = pl.BlockSpec(memory_space=pltpu.HBM)
SMEM_SPEC = pl.BlockSpec(memory_space=pltpu.SMEM)
F32, BF16 = jnp.float32, jnp.bfloat16


def three_parts(table):
    high = table.astype(np.float32).astype(ml_dtypes.bfloat16)
    rest = table.astype(np.float32) - high.astype(np.float32)
    middle = rest.astype(ml_dtypes.bfloat16)
    low = (rest - middle.astype(np.float32)).astype(ml_dtypes.bfloat16)
    return high, middle, low


def position_rows():
    side, quarter = SIDE // 2, D // 4
    frequency = 1.0 / 10000.0 ** (np.arange(quarter) / quarter)
    angles = np.arange(side)[:, None] * frequency[None, :]
    line = np.concatenate([np.sin(angles), np.cos(angles)], axis=1)
    parts = three_parts(line)
    zero = np.zeros_like(parts[0])
    rows = [np.concatenate([p, zero], axis=1) for p in parts]
    cols = [np.concatenate([zero, p], axis=1) for p in parts]
    return np.concatenate(rows + cols, axis=0)


def blend_tables():
    beta = 0.0001 + np.arange(TSTEPS) * (0.02 - 0.0001) / (TSTEPS - 1)
    alpha_bar = np.cumprod(1.0 - beta)
    return np.stack([np.sqrt(alpha_bar), np.sqrt(1.0 - alpha_bar)]).astype(np.float32)


def time_rates():
    steps = np.arange(128, dtype=np.float32)
    scaled = np.float32(-math.log(10000.0)) * steps / np.float32(128)
    return np.exp(scaled).astype(np.float32).reshape(1, 128)


def place():
    return tuple(lax.axis_index(a) for a in ("dp_0", "dp_1", "fsdp_0", "fsdp_1"))


def widened(ref):
    return jnp.concatenate([ref[...]] * (WIDE // 128), axis=1)


def split_three(value):
    high = value.astype(BF16)
    rest = value - high.astype(F32)
    middle = rest.astype(BF16)
    low = (rest - middle.astype(F32)).astype(BF16)
    return jnp.concatenate([high, middle, low], axis=0)


def joined_three(value, rows):
    return (value[2 * rows :] + value[rows : 2 * rows]) + value[:rows]


def step_kernel(*refs):
    inputs, (sum_ref, total_ref, moments_ref) = refs[:17], refs[17:20]
    buffers, scratch = refs[20:37], refs[37:]
    (flips_ref, crops_ref, steps_ref, selected_ref, table_ref) = buffers[:5]
    (x_buf, taps_ref, w1_ref, w2s_ref, vae_ref, noise_ref, wp_ref) = buffers[5:12]
    (pos_ref, rates_ref, wt_buf, wa_buf, wf_ref) = buffers[12:]
    (all_ref, msg_ref, got_ref) = scratch[:3]
    (rows_ref, pads_ref, shift_ref, scale_ref, gate_ref, tok_ref, modt_ref) = scratch[3:10]
    (mod_ref, w2_ref, hid_ref, slope_ref, target_ref, gbt_ref, gb_ref) = scratch[10:17]
    (square_ref, own_ref, keep_ref, send_ref, r0, s1, r1, acc, c2, r2) = scratch[17:27]
    (tiles, r3, whole, l0, l1, l2, far_ref, r3_far) = scratch[27:35]
    (g1_send, g1_recv, g2_send, g2_recv, p_send, p_recv) = scratch[35:41]
    (s2_send, s2_recv, q_send, q_recv, s1_send, s1_recv) = scratch[41:47]
    (m_send, m_recv, z_send, z_recv) = scratch[47:51]
    (a_send, a_recv, f_send, f_recv, l_send, l_recv, c_sem) = scratch[51:]
    z, c, y, x = place()
    me = z * NC + c
    partner = {"dp_1": 1 - c}
    lane = lax.broadcasted_iota(jnp.int32, (8, 128), 1)
    zero = jnp.zeros((8, 128), F32)

    def x_at(k):
        return lax.rem(x + k, NX)

    def y_at(k):
        return lax.rem(y + k, NY)

    def z_at(k):
        return lax.rem(z + k, NZ)

    def dp_at(k):
        return lax.rem(me + k, NDP)

    def dp_device(k):
        other = dp_at(k)
        return {"dp_0": other // NC, "dp_1": lax.rem(other, NC)}

    def remote(src, dst, send, recv, device):
        return pltpu.make_async_remote_copy(
            src_ref=src,
            dst_ref=dst,
            send_sem=send,
            recv_sem=recv,
            device_id=device,
            device_id_type=MESH,
        )

    def first_to(half, k):
        return {"fsdp_1": x_at(k)} if half == 0 else {"fsdp_0": y_at(k)}

    def second_to(half, k):
        return {"fsdp_0": y_at(k)} if half == 0 else {"fsdp_1": x_at(k)}

    def second_at(half, k):
        return y_at(k) if half == 0 else x_at(k)

    barrier = pltpu.get_barrier_semaphore()
    for k in range(1, NX):
        pl.semaphore_signal(barrier, 1, device_id={"fsdp_1": x_at(k)}, device_id_type=MESH)
        pl.semaphore_signal(barrier, 1, device_id={"fsdp_0": y_at(k)}, device_id_type=MESH)
    for k in range(1, NDP):
        pl.semaphore_signal(barrier, 1, device_id=dp_device(k), device_id_type=MESH)
    loads = [
        pltpu.make_async_copy(inputs[i], buffers[i], c_sem.at[i]) for i in range(len(inputs))
    ]
    shards, pictures = (7, 8), (5, 6)
    for i in shards + pictures:
        loads[i].start()
    for i in range(len(inputs)):
        if i not in shards + pictures:
            loads[i].start()
    for i in shards:
        loads[i].wait()
    own_shard = jnp.where(c == 0, w1_ref[...], w2s_ref[...])
    all_ref[c, y, x, 0] = own_shard[:HALF]
    all_ref[c, y, x, 1] = own_shard[HALF:]
    pl.semaphore_wait(barrier, NX - 1 + NY - 1 + NDP - 1)

    def message(k):
        return remote(
            msg_ref.at[dp_at(k)], got_ref.at[me], m_send.at[k], m_recv.at[k], dp_device(k)
        )

    def gather_first(half, k):
        at = all_ref.at[c, y, x, half]
        return remote(at, at, g1_send.at[half, k], g1_recv.at[half, k], first_to(half, k))

    def line(half, k):
        if half == 0:
            return all_ref.at[c, y_at(NY - k), :, 0]
        return all_ref.at[c, :, x_at(NX - k), 1]

    def gather_second(half, k):
        at = line(half, 0)
        return remote(at, at, g2_send.at[half, k], g2_recv.at[half, k], second_to(half, k))

    def across(half, k):
        at = line(half, k)
        return remote(at, at, p_send.at[half, k], p_recv.at[half, k], partner)

    messages = [message(k) for k in range(1, NDP)]
    early = {(h, k): gather_first(h, k) for k in (1, 3, 2) for h in range(2)}
    late = {(h, k): gather_second(h, k) for k in (1, 3, 2) for h in range(2)}
    crossed = {(h, k): across(h, k) for k in (0, 1, 3, 2) for h in range(2)}
    for copy in early.values():
        copy.start()
    for i in pictures:
        loads[i].wait()
    taps = lax.dot_general(
        taps_ref[...], x_buf[...], (((1,), (1,)), ((), ())), preferred_element_type=F32
    )
    col = lane % SIDE

    def tap(dy, dx, v):
        at = (dy * 3 + dx) * 8
        return taps[at : at + 8, 128 * v : 128 * v + 128]

    for v in range(8):
        rows = []
        for dy in range(3):
            left = jnp.where(col == 0, zero, pltpu.roll(tap(dy, 0, v), 1, 1))
            right = jnp.where(col == SIDE - 1, zero, pltpu.roll(tap(dy, 2, v), 127, 1))
            rows.append(left + tap(dy, 1, v) + right)
        for odd in range(2):
            parts = [pltpu.roll(r, 64, 1) if odd else r for r in rows]
            parts = [jnp.where(lane < 64, r, zero) for r in parts]
            msg_ref[2 * v + odd] = (
                parts[2] + pltpu.roll(parts[1], 32, 1) + pltpu.roll(parts[0], 64, 1)
            )
    got_ref[me] = msg_ref[me]
    for m in messages:
        m.start()
    for copy in early.values():
        copy.wait_recv()
    for copy in late.values():
        copy.start()
    for h in range(2):
        crossed[h, 0].start()
    for i in range(len(inputs)):
        if i not in shards + pictures:
            loads[i].wait()

    row = lax.broadcasted_iota(jnp.int32, (8, 128), 0)
    steps = jnp.zeros((8, 128), F32)
    for a in range(AUG):
        steps = jnp.where(row == a, steps_ref[0, a].astype(F32), steps)
    phases = steps * rates_ref[...]
    stamp = jnp.concatenate([jnp.cos(phases), jnp.sin(phases)], axis=1).astype(BF16)
    raw = jnp.dot(stamp, wt_buf[...], preferred_element_type=F32)
    conditioning = (raw * (1.0 / (1.0 + jnp.exp(-raw)))).astype(BF16)
    modulation = jnp.dot(conditioning, wa_buf[...], preferred_element_type=F32)
    views = [jnp.broadcast_to(modulation[a : a + 1], (16, 3 * D)) for a in range(AUG)]
    turned = jnp.concatenate(views + views, axis=0).T
    shift_ref[...] = turned[:D]
    scale_ref[...] = 1.0 + turned[D : 2 * D]
    gate_ref[...] = turned[2 * D :]

    for m in messages:
        m.wait_recv()
    for k in range(8):
        low = pltpu.roll(got_ref[2 * k], 96, 1)
        above = pltpu.roll(got_ref[2 * k + 2], 96, 1) if k < 7 else zero
        high = pltpu.roll(got_ref[2 * k + 1], 32, 1)
        below = pltpu.roll(got_ref[2 * k - 1], 32, 1) if k > 0 else zero
        four = jnp.where(lane < 96, low, above) + jnp.where(lane >= 32, high, below)
        for r in range(4):
            at = (4 * k + r) * 8
            rows_ref[at : at + 8, :] = pltpu.roll(four, 128 - 32 * r, 1) if r else four
    wide = lax.broadcasted_iota(jnp.int32, (SIDE, 128), 1) // SIDE
    halves = []
    for h in range(2):
        value = rows_ref[pl.ds(4 * h, SIDE, stride=8), :]
        for ch in range(1, 4):
            part = rows_ref[pl.ds(4 * h + ch, SIDE, stride=8), :]
            value = jnp.where(wide == ch, pltpu.roll(part, 32 * ch, 1), value)
        halves.append(value)
    by_channel = jnp.concatenate(halves, axis=1)
    source = lax.broadcasted_iota(jnp.int32, (256, 512), 0)
    goal = lax.broadcasted_iota(jnp.int32, (256, 512), 1)
    channel, column = source // SIDE, source % SIDE
    natural = column * 8 + channel
    apart = 256 + (channel // 4) * 128 + column * 4 + channel % 4
    spread = jnp.where((goal == natural) | (goal == apart), 1.0, 0.0).astype(BF16)
    placed = joined_three(
        jnp.dot(split_three(by_channel), spread, preferred_element_type=F32), SIDE
    )
    moments_ref[pl.ds(0, SIDE, stride=2), :] = placed[:, 0:128]
    moments_ref[pl.ds(1, SIDE, stride=2), :] = placed[:, 128:256]

    latent = placed[:, 256:384] + jnp.exp(0.5 * placed[:, 384:512]) * vae_ref[...]
    source = lax.broadcasted_iota(jnp.int32, (128, 128), 0)
    goal = lax.broadcasted_iota(jnp.int32, (128, 128), 1)
    maps = []
    for a in range(AUG):
        cell = goal // LC + crops_ref[1, a] - 2
        inside = (cell >= 0) & (cell < SIDE)
        mirror = (flips_ref[0, a] == 1).astype(jnp.int32)
        cell = cell + mirror * (SIDE - 1 - 2 * cell)
        match = inside & (source == cell * LC + goal % LC)
        maps.append(jnp.where(match, 1.0, 0.0).astype(BF16))
    columns = jnp.dot(
        split_three(latent), jnp.concatenate(maps, axis=1), preferred_element_type=F32
    )
    columns = joined_three(columns, SIDE)
    noised, noises = [], []
    for a in range(AUG):
        pads_ref[a] = jnp.zeros((40, 128), F32)
        pads_ref[a, 2 : 2 + SIDE, :] = columns[:, 128 * a : 128 * a + 128]
    for dr in range(2):
        for a in range(AUG):
            view = pads_ref[a, pl.ds(crops_ref[0, a] + dr, 16, stride=2), :]
            noise = noise_ref[pl.ds(dr * 4 + a, 16, stride=8), :]
            step = steps_ref[0, a]
            noised.append(table_ref[0, step] * view + table_ref[1, step] * noise)
            noises.append(noise)

    def patched(pieces):
        turned = jnp.concatenate(pieces, axis=0).T
        first, last = [], []
        for m in range(8):
            even = turned[16 * m : 16 * m + 8]
            odd = turned[16 * m + 8 : 16 * m + 16]
            first.append(jnp.where(lane < 64, even, pltpu.roll(odd, 64, 1)))
            last.append(jnp.where(lane < 64, pltpu.roll(even, 64, 1), odd))
        return jnp.concatenate(
            [jnp.concatenate(first, axis=1), jnp.concatenate(last, axis=1)], axis=0
        )

    patches = patched(noised).astype(BF16)
    target_ref[...] = patched(noises)

    which = lax.broadcasted_iota(jnp.int32, (96, TOK), 0)
    token = lax.broadcasted_iota(jnp.int32, (96, TOK), 1)
    cell = jnp.where(which < 48, token % 16, token // 64)
    marks = jnp.where(which % 16 == cell, 1.0, 0.0).astype(BF16)
    tok_ref[...] = lax.dot_general(
        jnp.concatenate([wp_ref[...], pos_ref[...]], axis=0),
        jnp.concatenate([patches, marks], axis=0),
        (((0,), (0,)), ((), ())),
        preferred_element_type=F32,
    )

    @pl.loop(0, TOK // WIDE)
    def _(m):
        at = pl.ds(pl.multiple_of(m * WIDE, WIDE), WIDE)
        value = tok_ref[:, at]
        center = value - jnp.sum(value, axis=0, keepdims=True) * (1.0 / D)
        variance = jnp.sum(center * center, axis=0, keepdims=True) * (1.0 / D)
        normed = center * lax.rsqrt(variance + norm_epsilon)
        out = normed * widened(scale_ref) + widened(shift_ref)
        modt_ref[:, at] = out.astype(BF16)
        mod_ref[at, :] = out.T.astype(BF16)

    def weights(w, k):
        near = all_ref[w, y_at(NY - k), :, 0].reshape(CHUNK // 2, D)
        other = all_ref[w, :, x_at(NX - k), 1].reshape(CHUNK // 2, D)
        return jnp.concatenate([near, other], axis=0)

    root = math.sqrt(2.0 / math.pi)

    def forward(k):
        for h in range(2):
            crossed[h, k].wait_recv()
        at = pl.ds(k * CHUNK, CHUNK)
        pre = jnp.dot(weights(0, k), modt_ref[...], preferred_element_type=F32)
        squared = pre * pre
        inner = pre * (squared * (root * 0.044715) + root)
        share = 0.5 * jnp.tanh(inner) + 0.5
        hidden = pre * share
        hid_ref[at, :] = hidden.astype(BF16)
        slope = (1.0 - share) * hidden * (squared * (6.0 * root * 0.044715) + 2.0 * root)
        slope_ref[at, :] = slope + share
        w2_ref[:, at] = weights(1, k).astype(F32).T.astype(BF16)

    def pass_on(k):
        for h in range(2):
            late[h, k].wait_recv()
            crossed[h, k].start()

    forward(0)
    pass_on(1)
    pass_on(3)
    forward(1)
    pass_on(2)
    forward(3)
    forward(2)

    own_ref[1] = jnp.zeros((8, 128), F32)

    @pl.loop(0, TOK // WIDE)
    def _(m):
        at = pl.ds(pl.multiple_of(m * WIDE, WIDE), WIDE)
        branch = jnp.dot(w2_ref[...], hid_ref[:, at], preferred_element_type=F32)
        gate = widened(gate_ref)
        mixed = tok_ref[:, at] + gate * branch
        center = mixed - jnp.sum(mixed, axis=0, keepdims=True) * (1.0 / D)
        variance = jnp.sum(center * center, axis=0, keepdims=True) * (1.0 / D)
        inverse = lax.rsqrt(variance + norm_epsilon)
        normed = center * inverse
        predicted = jnp.dot(wf_ref[...], normed.astype(BF16), preferred_element_type=F32)
        residue = predicted - target_ref[:, at]
        own_ref[1] += jnp.sum(residue * residue) * (1.0 / (TOK * 16))
        grad_pred = (residue * (2.0 / (TOK * 16))).astype(BF16)
        grad_normed = lax.dot_general(
            wf_ref[...], grad_pred, (((0,), (0,)), ((), ())), preferred_element_type=F32
        )
        mean = jnp.sum(grad_normed, axis=0, keepdims=True) * (1.0 / D)
        along = jnp.sum(grad_normed * normed, axis=0, keepdims=True) * (1.0 / D)
        grad_mixed = inverse * (grad_normed - mean - normed * along)
        grad_branch = gate * grad_mixed
        gbt_ref[:, at] = grad_branch.astype(BF16)
        gb_ref[at, :] = grad_branch.T.astype(BF16)

    square_ref[...] = jnp.zeros_like(square_ref)
    chosen = selected_ref[0, 0] == 1
    l0[0] = jnp.where(chosen, own_ref[1], 0.0)
    losses = [remote(l0.at[0], l0.at[1], l_send.at[0], l_recv.at[0], partner)]
    losses[0].start()

    def swap(half, k):
        if half == 0:
            at = (y_at(NY - k), slice(None), 0)
        else:
            at = (slice(None), x_at(NX - k), 1)
        return remote(
            send_ref.at[at], r0.at[at], q_send.at[half, k], q_recv.at[half, k], partner
        )

    for k in range(4):
        at = pl.ds(k * CHUNK, CHUNK)
        grad_hidden = jnp.dot(weights(1, k), gbt_ref[...], preferred_element_type=F32)
        grad_pre = (slope_ref[at, :] * grad_hidden).astype(BF16)
        grad_1 = jnp.dot(grad_pre, mod_ref[...], preferred_element_type=F32)
        grad_2 = jnp.dot(hid_ref[at, :], gb_ref[...], preferred_element_type=F32)
        grad_1 = jnp.where(chosen, grad_1, 0.0)
        grad_2 = jnp.where(chosen, grad_2, 0.0)
        kept = jnp.where(c == 0, grad_1, grad_2)
        sent = jnp.where(c == 0, grad_2, grad_1).astype(BF16)
        for h in range(2):
            rows = slice(h * CHUNK // 2, (h + 1) * CHUNK // 2)
            kept_half = kept[rows].reshape(4, HALF, D)
            sent_half = sent[rows].reshape(4, HALF, D)
            if h == 0:
                keep_ref[y_at(NY - k), :, 0] = kept_half
                send_ref[y_at(NY - k), :, 0] = sent_half
            else:
                keep_ref[:, x_at(NX - k), 1] = kept_half
                send_ref[:, x_at(NX - k), 1] = sent_half
            swap(h, k).start()
        square_ref[...] += jnp.sum(
            grad_1 * grad_1 + grad_2 * grad_2, axis=0, keepdims=True
        )

    total = jnp.sum(square_ref[...], axis=1, keepdims=True)
    factor = 1.0 / (jnp.sqrt(total * (1.0 / (2 * D * FF))) + clip_offset)
    own_ref[0] = jnp.broadcast_to(factor, (8, 128))
    factors = remote(own_ref.at[0], own_ref.at[2], l_send.at[7], l_recv.at[7], partner)
    factors.start()
    losses[0].wait_recv()
    l1[x] = l0[0] + l0[1]
    for k in range(1, NX):
        copy = remote(l1.at[x], l1.at[x], l_send.at[k], l_recv.at[k], {"fsdp_1": x_at(k)})
        copy.start()
        losses.append(copy)
    for k in range(4):
        for h in range(2):
            swap(h, k).wait_recv()
    factors.wait_recv()
    mine = own_ref[0, 0:1, 0:1]
    other = own_ref[2, 0:1, 0:1]

    def part(half, k, j):
        if half == 0:
            return (j, x_at(k), 0)
        return (y_at(k), j, 1)

    def chip(half, k, j):
        at = part(half, k, j)
        return keep_ref[at] * mine + r0[at].astype(F32) * other

    offsets = (2, 1, 3, 0)
    firsts = {}
    for group in range(2):
        for k in (2, 1, 3):
            for h in range(2):
                for q in (2 * group, 2 * group + 1):
                    value = chip(h, k, second_at(h, offsets[q]))
                    s1[h, k - 1, q] = value.astype(BF16)
                firsts[h, k, group] = remote(
                    s1.at[h, k - 1, pl.ds(2 * group, 2)],
                    r1.at[h, k - 1, pl.ds(2 * group, 2)],
                    s1_send.at[h, 2 * k + group],
                    s1_recv.at[h, 2 * k + group],
                    first_to(h, k),
                )
                firsts[h, k, group].start()
    for h in range(2):
        for q in range(4):
            acc[h, q] = chip(h, 0, second_at(h, offsets[q]))
    for copy in losses[1:]:
        copy.wait_recv()
    l2[y] = (l1[0] + l1[1]) + (l1[2] + l1[3])
    for k in range(1, NY):
        copy = remote(
            l2.at[y], l2.at[y], l_send.at[3 + k], l_recv.at[3 + k], {"fsdp_0": y_at(k)}
        )
        copy.start()
        losses.append(copy)
    seconds = {}
    for group in range(2):
        for h in range(2):
            for k in (1, 3, 2):
                firsts[h, k, group].wait_recv()
            for q in (2 * group, 2 * group + 1):
                k = offsets[q]
                value = (acc[h, q] + r1[h, 0, q].astype(F32)) + (
                    r1[h, 1, q].astype(F32) + r1[h, 2, q].astype(F32)
                )
                if k == 0:
                    acc[h, q] = value
                else:
                    c2[h, k - 1] = value.astype(BF16)
                    seconds[h, k] = remote(
                        c2.at[h, k - 1],
                        r2.at[h, k - 1],
                        s2_send.at[h, k],
                        s2_recv.at[h, k],
                        second_to(h, k),
                    )
                    seconds[h, k].start()
    for copy in losses[4:]:
        copy.wait_recv()
    plane = (l2[0] + l2[1]) + (l2[2] + l2[3])
    coarse = plane.astype(BF16).astype(F32)
    at = USED_TILES
    tiles[at // PIECE, at % PIECE] = coarse
    tiles[at // PIECE, at % PIECE + 1] = plane - coarse
    for t in range(USED_TILES + 2, TILES):
        tiles[t // PIECE, t % PIECE] = jnp.zeros((8, 128), F32)
    for h in range(2):
        for k in (1, 3, 2):
            seconds[h, k].wait_recv()
        value = (acc[h, 3] + r2[h, 0].astype(F32)) + (
            r2[h, 1].astype(F32) + r2[h, 2].astype(F32)
        )
        for i in range(HALF // 8):
            for n in range(D // 128):
                t = (h * (HALF // 8) + i) * (D // 128) + n
                tiles[t // PIECE, t % PIECE] = value[8 * i : 8 * i + 8, 128 * n : 128 * n + 128]

    order = (4, 3, 5, 2, 6, 1, 7)
    thirds = []
    for k in order:
        if k in FAR:
            slot = k - FAR[0]
            far_ref[slot] = tiles[z_at(k)].reshape(PIECE * 8, 128).astype(BF16)
            src, dst = far_ref.at[slot], r3_far.at[slot]
        else:
            src, dst = tiles.at[z_at(k)], r3.at[k]
        copy = remote(src, dst, z_send.at[k], z_recv.at[k], {"dp_0": z_at(k)})
        copy.start()
        thirds.append(copy)
    for copy in thirds:
        copy.wait_recv()
    value = tiles[z]
    for k in range(1, NZ):
        if k in FAR:
            value = value + r3_far[k - FAR[0]].astype(F32).reshape(PIECE, 8, 128)
        else:
            value = value + r3[k]
    whole[c, z] = value
    spreads = {}
    for k in order:
        spreads[k] = remote(
            whole.at[c, z], whole.at[c, z], a_send.at[k], a_recv.at[k], {"dp_0": z_at(k)}
        )
        spreads[k].start()
    crossings = []
    for k in (0, 7, 1, 6, 2, 5, 3, 4):
        if k > 0:
            spreads[k].wait_recv()
        at = z_at(NZ - k) if k > 0 else z
        copy = remote(whole.at[c, at], whole.at[c, at], f_send.at[k], f_recv.at[k], partner)
        copy.start()
        crossings.append(copy)
    for copy in crossings:
        copy.wait_recv()
    for w in range(2):
        for t in range(USED_TILES):
            i, n = t // (D // 128), t % (D // 128)
            sum_ref[w, 8 * i : 8 * i + 8, 128 * n : 128 * n + 128] = whole[
                w, t // PIECE, t % PIECE
            ]
    at = USED_TILES
    total_ref[...] = whole[0, at // PIECE, at % PIECE] + whole[0, at // PIECE, at % PIECE + 1]
    for k in range(4):
        for h in range(2):
            swap(h, k).wait_send()
    for group in (early, late, crossed, firsts, seconds, spreads):
        for copy in group.values():
            copy.wait_send()
    for group in (messages, losses, thirds, crossings, [factors]):
        for copy in group:
            copy.wait_send()


def finish_kernel(sum_ref, total_ref, moved_ref, n1_ref, n2_ref, *outs):
    u1_ref, u2_ref, mean_ref, moments_ref = outs
    u1_ref[...] = (sum_ref[0] + noise_weight * n1_ref[...]) * (1.0 / SELECTED)
    u2_ref[...] = (sum_ref[1] + noise_weight * n2_ref[...]) * (1.0 / SELECTED)
    mean_ref[...] = total_ref[0:1, 0:1] * (1.0 / SELECTED)
    moments_ref[...] = moved_ref[...]


def per_device(
    features,
    conv_weight,
    vae_noise,
    flips,
    crops,
    tsteps,
    diffusion_noise,
    selected,
    w_patch,
    w_time,
    w_ada,
    w_fc1,
    w_fc2,
    w_final,
    noise_fc1,
    noise_fc2,
):
    dma = pltpu.SemaphoreType.DMA
    pixels = features.reshape(TOK, FCH)
    taps = conv_weight.transpose(0, 1, 3, 2).reshape(72, FCH)
    views = diffusion_noise.reshape(AUG, SIDE, SIDE * LC).transpose(1, 0, 2)
    grid = (NY, NX, 2, HALF, D)
    tile = (8, 128)
    vmem = pltpu.VMEM
    sums, total, moved = pl.pallas_call(
        step_kernel,
        out_shape=(
            jax.ShapeDtypeStruct((2, SHARD, D), F32),
            jax.ShapeDtypeStruct(tile, F32),
            jax.ShapeDtypeStruct((2 * SIDE, 128), F32),
        ),
        in_specs=[HBM_SPEC] * 17,
        out_specs=(VMEM_SPEC,) * 3,
        scratch_shapes=[
            pltpu.SMEM((1, AUG), jnp.int32),
            pltpu.SMEM((2, AUG), jnp.int32),
            pltpu.SMEM((1, AUG), jnp.int32),
            pltpu.SMEM((1, 1), jnp.int32),
            pltpu.SMEM((2, TSTEPS), F32),
            vmem((TOK, FCH), BF16),
            vmem((72, FCH), BF16),
            vmem((SHARD, D), BF16),
            vmem((SHARD, D), BF16),
            vmem((SIDE, 128), F32),
            vmem((SIDE * AUG, 128), F32),
            vmem((16, D), BF16),
            vmem((96, D), BF16),
            vmem((1, 128), F32),
            vmem((256, D), BF16),
            vmem((D, 3 * D), BF16),
            vmem((16, D), BF16),
            vmem((2,) + grid, BF16),
            vmem((NDP,) + tile, F32),
            vmem((NDP,) + tile, F32),
            vmem((256, 128), F32),
            vmem((AUG, 40, 128), F32),
            vmem((D, 128), F32),
            vmem((D, 128), F32),
            vmem((D, 128), F32),
            vmem((D, TOK), F32),
            vmem((D, TOK), BF16),
            vmem((TOK, D), BF16),
            vmem((D, FF), BF16),
            vmem((FF, TOK), BF16),
            vmem((FF, TOK), F32),
            vmem((16, TOK), F32),
            vmem((D, TOK), BF16),
            vmem((TOK, D), BF16),
            vmem((1, D), F32),
            vmem((4,) + tile, F32),
            vmem(grid, F32),
            vmem(grid, BF16),
            vmem(grid, BF16),
            vmem((2, 3, 4, HALF, D), BF16),
            vmem((2, 3, 4, HALF, D), BF16),
            vmem((2, 4, HALF, D), F32),
            vmem((2, 3, HALF, D), BF16),
            vmem((2, 3, HALF, D), BF16),
            vmem((NZ, PIECE) + tile, F32),
            vmem((NZ, PIECE) + tile, F32),
            vmem((2, NZ, PIECE) + tile, F32),
            vmem((2,) + tile, F32),
            vmem((NX,) + tile, F32),
            vmem((NY,) + tile, F32),
            vmem((3, PIECE * 8, 128), BF16),
            vmem((3, PIECE * 8, 128), BF16),
        ]
        + [dma((2, 4))] * 10
        + [dma((2, 8))] * 2
        + [dma((NDP,))] * 2
        + [dma((NZ,))] * 8
        + [dma((17,))],
        compiler_params=pltpu.CompilerParams(
            collective_id=0, has_side_effects=True, vmem_limit_bytes=56 << 20
        ),
        name="step",
    )(
        flips.reshape(1, AUG),
        crops.reshape(AUG, 2).T,
        tsteps.reshape(1, AUG),
        selected,
        jnp.asarray(blend_tables()),
        pixels,
        taps,
        w_fc1.T,
        w_fc2.T,
        vae_noise.reshape(SIDE, SIDE * LC),
        views.reshape(SIDE * AUG, SIDE * LC),
        w_patch,
        jnp.asarray(position_rows()),
        jnp.asarray(time_rates()),
        w_time,
        w_ada,
        w_final.T,
    )
    update_1, update_2, mean_loss, moments = pl.pallas_call(
        finish_kernel,
        out_shape=(
            jax.ShapeDtypeStruct((SHARD, D), F32),
            jax.ShapeDtypeStruct((SHARD, D), F32),
            jax.ShapeDtypeStruct((1, 1), F32),
            jax.ShapeDtypeStruct((2 * SIDE, 128), F32),
        ),
        in_specs=[VMEM_SPEC] * 5,
        out_specs=(VMEM_SPEC,) * 4,
        name="finish",
    )(sums, total, moved, noise_fc1.T, noise_fc2.T)
    return (update_1.T, update_2.T, mean_loss.reshape(()), moments.reshape(1, 1, -1))


def solution(mesh):
    split = Mesh(mesh.devices.reshape(NZ, NC, NY, NX), DP + FSDP)
    return jax.shard_map(
        per_device,
        mesh=split,
        in_specs=(
            P(FSDP, None, DP, None, None),
            P(),
            P(DP, FSDP, None),
            P(DP, FSDP, None),
            P(DP, FSDP, None, None),
            P(DP, FSDP, None),
            P(DP, FSDP, None, None),
            P(DP, FSDP),
            P(),
            P(),
            P(),
            P(None, FSDP),
            P(None, FSDP),
            P(),
            P(None, FSDP),
            P(None, FSDP),
        ),
        out_specs=(P(None, FSDP), P(None, FSDP), P(), P(DP, FSDP, None)),
        check_vma=False,
    )
```

```python
import math

import jax
import jax.numpy as jnp
import ml_dtypes
import numpy as np
from jax import lax
from jax.experimental import pallas as pl
from jax.experimental.pallas import tpu as pltpu
from jax.sharding import Mesh
from jax.sharding import PartitionSpec as P

MESH = pl.DeviceIdType.MESH
DP = ("dp_0", "dp_1")
FSDP = ("fsdp_0", "fsdp_1")
NZ, NC, NY, NX = 8, 2, 4, 4
NDP = NZ * NC
D, FF, TOK, FCH = 384, 1536, 1024, 512
SHARD = FF // (NY * NX)
HALF = SHARD // 2
SIDE, LC, AUG, TSTEPS = 32, 4, 4, 1000
SELECTED = 128
CHUNK = 384
WIDE = 1024
PIECE = 5
FAR = (3, 4, 5)
GROUPS = ((0, 3), (3, 4))
TILES = NZ * PIECE
USED_TILES = (SHARD // 8) * (D // 128)
clip_offset = 1e-05
noise_weight = 16.0
norm_epsilon = 1e-06
VMEM_SPEC = pl.BlockSpec(memory_space=pltpu.VMEM)
HBM_SPEC = pl.BlockSpec(memory_space=pltpu.HBM)
SMEM_SPEC = pl.BlockSpec(memory_space=pltpu.SMEM)
F32, BF16 = jnp.float32, jnp.bfloat16


def three_parts(table):
    high = table.astype(np.float32).astype(ml_dtypes.bfloat16)
    rest = table.astype(np.float32) - high.astype(np.float32)
    middle = rest.astype(ml_dtypes.bfloat16)
    low = (rest - middle.astype(np.float32)).astype(ml_dtypes.bfloat16)
    return high, middle, low


def position_rows():
    side, quarter = SIDE // 2, D // 4
    frequency = 1.0 / 10000.0 ** (np.arange(quarter) / quarter)
    angles = np.arange(side)[:, None] * frequency[None, :]
    line = np.concatenate([np.sin(angles), np.cos(angles)], axis=1)
    parts = three_parts(line)
    zero = np.zeros_like(parts[0])
    rows = [np.concatenate([p, zero], axis=1) for p in parts]
    cols = [np.concatenate([zero, p], axis=1) for p in parts]
    return np.concatenate(rows + cols, axis=0)


def blend_tables():
    beta = 0.0001 + np.arange(TSTEPS) * (0.02 - 0.0001) / (TSTEPS - 1)
    alpha_bar = np.cumprod(1.0 - beta)
    return np.stack([np.sqrt(alpha_bar), np.sqrt(1.0 - alpha_bar)]).astype(np.float32)


def time_rates():
    steps = np.arange(128, dtype=np.float32)
    scaled = np.float32(-math.log(10000.0)) * steps / np.float32(128)
    return np.exp(scaled).astype(np.float32).reshape(1, 128)


def place():
    return tuple(lax.axis_index(a) for a in ("dp_0", "dp_1", "fsdp_0", "fsdp_1"))


def widened(ref):
    return jnp.concatenate([ref[...]] * (WIDE // 128), axis=1)


def split_three(value):
    high = value.astype(BF16)
    rest = value - high.astype(F32)
    middle = rest.astype(BF16)
    low = (rest - middle.astype(F32)).astype(BF16)
    return jnp.concatenate([high, middle, low], axis=0)


def joined_three(value, rows):
    return (value[2 * rows :] + value[rows : 2 * rows]) + value[:rows]


def step_kernel(*refs):
    inputs, (sum_ref, total_ref, moments_ref) = refs[:17], refs[17:20]
    buffers, scratch = refs[20:37], refs[37:]
    (flips_ref, crops_ref, steps_ref, selected_ref, table_ref) = buffers[:5]
    (x_buf, taps_ref, w1_ref, w2s_ref, vae_ref, noise_ref, wp_ref) = buffers[5:12]
    (pos_ref, rates_ref, wt_buf, wa_buf, wf_ref) = buffers[12:]
    (all_ref, msg_ref, got_ref) = scratch[:3]
    (rows_ref, pads_ref, shift_ref, scale_ref, gate_ref, tok_ref, modt_ref) = scratch[3:10]
    (mod_ref, w2_ref, hid_ref, slope_ref, target_ref, gbt_ref, gb_ref) = scratch[10:17]
    (square_ref, own_ref, keep_ref, send_ref, r0, s1, r1, acc, c2, r2) = scratch[17:27]
    (tiles, r3, whole, l0, l1, l2, far_ref, r3_far) = scratch[27:35]
    (g1_send, g1_recv, g2_send, g2_recv, p_send, p_recv) = scratch[35:41]
    (s2_send, s2_recv, q_send, q_recv, s1_send, s1_recv) = scratch[41:47]
    (m_send, m_recv, z_send, z_recv) = scratch[47:51]
    (a_send, a_recv, f_send, f_recv, l_send, l_recv, c_sem) = scratch[51:]
    z, c, y, x = place()
    me = z * NC + c
    partner = {"dp_1": 1 - c}
    lane = lax.broadcasted_iota(jnp.int32, (8, 128), 1)
    zero = jnp.zeros((8, 128), F32)

    def x_at(k):
        return lax.rem(x + k, NX)

    def y_at(k):
        return lax.rem(y + k, NY)

    def z_at(k):
        return lax.rem(z + k, NZ)

    def dp_at(k):
        return lax.rem(me + k, NDP)

    def dp_device(k):
        other = dp_at(k)
        return {"dp_0": other // NC, "dp_1": lax.rem(other, NC)}

    def remote(src, dst, send, recv, device):
        return pltpu.make_async_remote_copy(
            src_ref=src,
            dst_ref=dst,
            send_sem=send,
            recv_sem=recv,
            device_id=device,
            device_id_type=MESH,
        )

    def first_to(half, k):
        return {"fsdp_1": x_at(k)} if half == 0 else {"fsdp_0": y_at(k)}

    def second_to(half, k):
        return {"fsdp_0": y_at(k)} if half == 0 else {"fsdp_1": x_at(k)}

    def second_at(half, k):
        return y_at(k) if half == 0 else x_at(k)

    barrier = pltpu.get_barrier_semaphore()
    for k in range(1, NX):
        pl.semaphore_signal(barrier, 1, device_id={"fsdp_1": x_at(k)}, device_id_type=MESH)
        pl.semaphore_signal(barrier, 1, device_id={"fsdp_0": y_at(k)}, device_id_type=MESH)
    for k in range(1, NDP):
        pl.semaphore_signal(barrier, 1, device_id=dp_device(k), device_id_type=MESH)
    loads = [
        pltpu.make_async_copy(inputs[i], buffers[i], c_sem.at[i]) for i in range(len(inputs))
    ]
    shards, pictures = (7, 8), (5, 6)
    for i in shards + pictures:
        loads[i].start()
    for i in range(len(inputs)):
        if i not in shards + pictures:
            loads[i].start()
    for i in shards:
        loads[i].wait()
    own_shard = jnp.where(c == 0, w1_ref[...], w2s_ref[...])
    all_ref[c, y, x, 0] = own_shard[:HALF]
    all_ref[c, y, x, 1] = own_shard[HALF:]
    pl.semaphore_wait(barrier, NX - 1 + NY - 1 + NDP - 1)

    def message(k):
        return remote(
            msg_ref.at[dp_at(k)], got_ref.at[me], m_send.at[k], m_recv.at[k], dp_device(k)
        )

    def gather_first(half, k):
        at = all_ref.at[c, y, x, half]
        return remote(at, at, g1_send.at[half, k], g1_recv.at[half, k], first_to(half, k))

    def line(half, k):
        if half == 0:
            return all_ref.at[c, y_at(NY - k), :, 0]
        return all_ref.at[c, :, x_at(NX - k), 1]

    def gather_second(half, k):
        at = line(half, 0)
        return remote(at, at, g2_send.at[half, k], g2_recv.at[half, k], second_to(half, k))

    def across(half, k):
        at = line(half, k)
        return remote(at, at, p_send.at[half, k], p_recv.at[half, k], partner)

    messages = [message(k) for k in range(1, NDP)]
    early = {(h, k): gather_first(h, k) for k in (1, 3, 2) for h in range(2)}
    late = {(h, k): gather_second(h, k) for k in (1, 3, 2) for h in range(2)}
    crossed = {(h, k): across(h, k) for k in (0, 1, 3, 2) for h in range(2)}
    for copy in early.values():
        copy.start()
    for i in pictures:
        loads[i].wait()
    taps = lax.dot_general(
        taps_ref[...], x_buf[...], (((1,), (1,)), ((), ())), preferred_element_type=F32
    )
    col = lane % SIDE

    def tap(dy, dx, v):
        at = (dy * 3 + dx) * 8
        return taps[at : at + 8, 128 * v : 128 * v + 128]

    for v in range(8):
        rows = []
        for dy in range(3):
            left = jnp.where(col == 0, zero, pltpu.roll(tap(dy, 0, v), 1, 1))
            right = jnp.where(col == SIDE - 1, zero, pltpu.roll(tap(dy, 2, v), 127, 1))
            rows.append(left + tap(dy, 1, v) + right)
        for odd in range(2):
            parts = [pltpu.roll(r, 64, 1) if odd else r for r in rows]
            parts = [jnp.where(lane < 64, r, zero) for r in parts]
            msg_ref[2 * v + odd] = (
                parts[2] + pltpu.roll(parts[1], 32, 1) + pltpu.roll(parts[0], 64, 1)
            )
    got_ref[me] = msg_ref[me]
    for m in messages:
        m.start()
    for copy in early.values():
        copy.wait_recv()
    for copy in late.values():
        copy.start()
    for h in range(2):
        crossed[h, 0].start()
    for i in range(len(inputs)):
        if i not in shards + pictures:
            loads[i].wait()

    row = lax.broadcasted_iota(jnp.int32, (8, 128), 0)
    steps = jnp.zeros((8, 128), F32)
    for a in range(AUG):
        steps = jnp.where(row == a, steps_ref[0, a].astype(F32), steps)
    phases = steps * rates_ref[...]
    stamp = jnp.concatenate([jnp.cos(phases), jnp.sin(phases)], axis=1).astype(BF16)
    raw = jnp.dot(stamp, wt_buf[...], preferred_element_type=F32)
    conditioning = (raw * (1.0 / (1.0 + jnp.exp(-raw)))).astype(BF16)
    modulation = jnp.dot(conditioning, wa_buf[...], preferred_element_type=F32)
    views = [jnp.broadcast_to(modulation[a : a + 1], (16, 3 * D)) for a in range(AUG)]
    turned = jnp.concatenate(views + views, axis=0).T
    shift_ref[...] = turned[:D]
    scale_ref[...] = 1.0 + turned[D : 2 * D]
    gate_ref[...] = turned[2 * D :]

    for m in messages:
        m.wait_recv()
    for k in range(8):
        low = pltpu.roll(got_ref[2 * k], 96, 1)
        above = pltpu.roll(got_ref[2 * k + 2], 96, 1) if k < 7 else zero
        high = pltpu.roll(got_ref[2 * k + 1], 32, 1)
        below = pltpu.roll(got_ref[2 * k - 1], 32, 1) if k > 0 else zero
        four = jnp.where(lane < 96, low, above) + jnp.where(lane >= 32, high, below)
        for r in range(4):
            at = (4 * k + r) * 8
            rows_ref[at : at + 8, :] = pltpu.roll(four, 128 - 32 * r, 1) if r else four
    wide = lax.broadcasted_iota(jnp.int32, (SIDE, 128), 1) // SIDE
    halves = []
    for h in range(2):
        value = rows_ref[pl.ds(4 * h, SIDE, stride=8), :]
        for ch in range(1, 4):
            part = rows_ref[pl.ds(4 * h + ch, SIDE, stride=8), :]
            value = jnp.where(wide == ch, pltpu.roll(part, 32 * ch, 1), value)
        halves.append(value)
    by_channel = jnp.concatenate(halves, axis=1)
    source = lax.broadcasted_iota(jnp.int32, (256, 512), 0)
    goal = lax.broadcasted_iota(jnp.int32, (256, 512), 1)
    channel, column = source // SIDE, source % SIDE
    natural = column * 8 + channel
    apart = 256 + (channel // 4) * 128 + column * 4 + channel % 4
    spread = jnp.where((goal == natural) | (goal == apart), 1.0, 0.0).astype(BF16)
    placed = joined_three(
        jnp.dot(split_three(by_channel), spread, preferred_element_type=F32), SIDE
    )
    moments_ref[pl.ds(0, SIDE, stride=2), :] = placed[:, 0:128]
    moments_ref[pl.ds(1, SIDE, stride=2), :] = placed[:, 128:256]

    latent = placed[:, 256:384] + jnp.exp(0.5 * placed[:, 384:512]) * vae_ref[...]
    source = lax.broadcasted_iota(jnp.int32, (128, 128), 0)
    goal = lax.broadcasted_iota(jnp.int32, (128, 128), 1)
    maps = []
    for a in range(AUG):
        cell = goal // LC + crops_ref[1, a] - 2
        inside = (cell >= 0) & (cell < SIDE)
        mirror = (flips_ref[0, a] == 1).astype(jnp.int32)
        cell = cell + mirror * (SIDE - 1 - 2 * cell)
        match = inside & (source == cell * LC + goal % LC)
        maps.append(jnp.where(match, 1.0, 0.0).astype(BF16))
    columns = jnp.dot(
        split_three(latent), jnp.concatenate(maps, axis=1), preferred_element_type=F32
    )
    columns = joined_three(columns, SIDE)
    noised, noises = [], []
    for a in range(AUG):
        pads_ref[a] = jnp.zeros((40, 128), F32)
        pads_ref[a, 2 : 2 + SIDE, :] = columns[:, 128 * a : 128 * a + 128]
    for dr in range(2):
        for a in range(AUG):
            view = pads_ref[a, pl.ds(crops_ref[0, a] + dr, 16, stride=2), :]
            noise = noise_ref[pl.ds(dr * 4 + a, 16, stride=8), :]
            step = steps_ref[0, a]
            noised.append(table_ref[0, step] * view + table_ref[1, step] * noise)
            noises.append(noise)

    def patched(pieces):
        turned = jnp.concatenate(pieces, axis=0).T
        first, last = [], []
        for m in range(8):
            even = turned[16 * m : 16 * m + 8]
            odd = turned[16 * m + 8 : 16 * m + 16]
            first.append(jnp.where(lane < 64, even, pltpu.roll(odd, 64, 1)))
            last.append(jnp.where(lane < 64, pltpu.roll(even, 64, 1), odd))
        return jnp.concatenate(
            [jnp.concatenate(first, axis=1), jnp.concatenate(last, axis=1)], axis=0
        )

    patches = patched(noised).astype(BF16)
    target_ref[...] = patched(noises)

    which = lax.broadcasted_iota(jnp.int32, (96, TOK), 0)
    token = lax.broadcasted_iota(jnp.int32, (96, TOK), 1)
    cell = jnp.where(which < 48, token % 16, token // 64)
    marks = jnp.where(which % 16 == cell, 1.0, 0.0).astype(BF16)
    tok_ref[...] = lax.dot_general(
        jnp.concatenate([wp_ref[...], pos_ref[...]], axis=0),
        jnp.concatenate([patches, marks], axis=0),
        (((0,), (0,)), ((), ())),
        preferred_element_type=F32,
    )

    @pl.loop(0, TOK // WIDE)
    def _(m):
        at = pl.ds(pl.multiple_of(m * WIDE, WIDE), WIDE)
        value = tok_ref[:, at]
        center = value - jnp.sum(value, axis=0, keepdims=True) * (1.0 / D)
        variance = jnp.sum(center * center, axis=0, keepdims=True) * (1.0 / D)
        normed = center * lax.rsqrt(variance + norm_epsilon)
        out = normed * widened(scale_ref) + widened(shift_ref)
        modt_ref[:, at] = out.astype(BF16)
        mod_ref[at, :] = out.T.astype(BF16)

    def weights(w, k):
        near = all_ref[w, y_at(NY - k), :, 0].reshape(CHUNK // 2, D)
        other = all_ref[w, :, x_at(NX - k), 1].reshape(CHUNK // 2, D)
        return jnp.concatenate([near, other], axis=0)

    root = math.sqrt(2.0 / math.pi)

    def forward(k):
        for h in range(2):
            crossed[h, k].wait_recv()
        at = pl.ds(k * CHUNK, CHUNK)
        pre = jnp.dot(weights(0, k), modt_ref[...], preferred_element_type=F32)
        squared = pre * pre
        inner = pre * (squared * (root * 0.044715) + root)
        share = 0.5 * jnp.tanh(inner) + 0.5
        hidden = pre * share
        hid_ref[at, :] = hidden.astype(BF16)
        slope = (1.0 - share) * hidden * (squared * (6.0 * root * 0.044715) + 2.0 * root)
        slope_ref[at, :] = slope + share
        w2_ref[:, at] = weights(1, k).astype(F32).T.astype(BF16)

    def pass_on(k):
        for h in range(2):
            late[h, k].wait_recv()
            crossed[h, k].start()

    forward(0)
    pass_on(1)
    pass_on(3)
    forward(1)
    pass_on(2)
    forward(3)
    forward(2)

    own_ref[1] = jnp.zeros((8, 128), F32)

    @pl.loop(0, TOK // WIDE)
    def _(m):
        at = pl.ds(pl.multiple_of(m * WIDE, WIDE), WIDE)
        branch = jnp.dot(w2_ref[...], hid_ref[:, at], preferred_element_type=F32)
        gate = widened(gate_ref)
        mixed = tok_ref[:, at] + gate * branch
        center = mixed - jnp.sum(mixed, axis=0, keepdims=True) * (1.0 / D)
        variance = jnp.sum(center * center, axis=0, keepdims=True) * (1.0 / D)
        inverse = lax.rsqrt(variance + norm_epsilon)
        normed = center * inverse
        predicted = jnp.dot(wf_ref[...], normed.astype(BF16), preferred_element_type=F32)
        residue = predicted - target_ref[:, at]
        own_ref[1] += jnp.sum(residue * residue) * (1.0 / (TOK * 16))
        grad_pred = (residue * (2.0 / (TOK * 16))).astype(BF16)
        grad_normed = lax.dot_general(
            wf_ref[...], grad_pred, (((0,), (0,)), ((), ())), preferred_element_type=F32
        )
        mean = jnp.sum(grad_normed, axis=0, keepdims=True) * (1.0 / D)
        along = jnp.sum(grad_normed * normed, axis=0, keepdims=True) * (1.0 / D)
        grad_mixed = inverse * (grad_normed - mean - normed * along)
        grad_branch = gate * grad_mixed
        gbt_ref[:, at] = grad_branch.astype(BF16)
        gb_ref[at, :] = grad_branch.T.astype(BF16)

    square_ref[...] = jnp.zeros_like(square_ref)
    chosen = selected_ref[0, 0] == 1
    l0[0] = jnp.where(chosen, own_ref[1], 0.0)
    losses = [remote(l0.at[0], l0.at[1], l_send.at[0], l_recv.at[0], partner)]
    losses[0].start()

    def swap(half, k):
        if half == 0:
            at = (y_at(NY - k), slice(None), 0)
        else:
            at = (slice(None), x_at(NX - k), 1)
        return remote(
            send_ref.at[at], r0.at[at], q_send.at[half, k], q_recv.at[half, k], partner
        )

    for k in range(4):
        at = pl.ds(k * CHUNK, CHUNK)
        grad_hidden = jnp.dot(weights(1, k), gbt_ref[...], preferred_element_type=F32)
        grad_pre = (slope_ref[at, :] * grad_hidden).astype(BF16)
        grad_1 = jnp.dot(grad_pre, mod_ref[...], preferred_element_type=F32)
        grad_2 = jnp.dot(hid_ref[at, :], gb_ref[...], preferred_element_type=F32)
        grad_1 = jnp.where(chosen, grad_1, 0.0)
        grad_2 = jnp.where(chosen, grad_2, 0.0)
        kept = jnp.where(c == 0, grad_1, grad_2)
        sent = jnp.where(c == 0, grad_2, grad_1).astype(BF16)
        for h in range(2):
            rows = slice(h * CHUNK // 2, (h + 1) * CHUNK // 2)
            kept_half = kept[rows].reshape(4, HALF, D)
            sent_half = sent[rows].reshape(4, HALF, D)
            if h == 0:
                keep_ref[y_at(NY - k), :, 0] = kept_half
                send_ref[y_at(NY - k), :, 0] = sent_half
            else:
                keep_ref[:, x_at(NX - k), 1] = kept_half
                send_ref[:, x_at(NX - k), 1] = sent_half
            swap(h, k).start()
        square_ref[...] += jnp.sum(
            grad_1 * grad_1 + grad_2 * grad_2, axis=0, keepdims=True
        )

    total = jnp.sum(square_ref[...], axis=1, keepdims=True)
    factor = 1.0 / (jnp.sqrt(total * (1.0 / (2 * D * FF))) + clip_offset)
    own_ref[0] = jnp.broadcast_to(factor, (8, 128))
    factors = remote(own_ref.at[0], own_ref.at[2], l_send.at[7], l_recv.at[7], partner)
    factors.start()
    losses[0].wait_recv()
    l1[x] = l0[0] + l0[1]
    for k in range(1, NX):
        copy = remote(l1.at[x], l1.at[x], l_send.at[k], l_recv.at[k], {"fsdp_1": x_at(k)})
        copy.start()
        losses.append(copy)
    for k in range(4):
        for h in range(2):
            swap(h, k).wait_recv()
    factors.wait_recv()
    mine = own_ref[0, 0:1, 0:1]
    other = own_ref[2, 0:1, 0:1]

    def part(half, k, j):
        if half == 0:
            return (j, x_at(k), 0)
        return (y_at(k), j, 1)

    def chip(half, k, j):
        at = part(half, k, j)
        return keep_ref[at] * mine + r0[at].astype(F32) * other

    offsets = (2, 1, 3, 0)
    firsts = {}
    for group in range(2):
        span = slice(*GROUPS[group])
        for k in (2, 1, 3):
            for h in range(2):
                for q in range(*GROUPS[group]):
                    value = chip(h, k, second_at(h, offsets[q]))
                    s1[h, k - 1, q] = value.astype(BF16)
                firsts[h, k, group] = remote(
                    s1.at[h, k - 1, span],
                    r1.at[h, k - 1, span],
                    s1_send.at[h, 2 * k + group],
                    s1_recv.at[h, 2 * k + group],
                    first_to(h, k),
                )
                firsts[h, k, group].start()
    for h in range(2):
        for q in range(4):
            acc[h, q] = chip(h, 0, second_at(h, offsets[q]))
    for copy in losses[1:]:
        copy.wait_recv()
    l2[y] = (l1[0] + l1[1]) + (l1[2] + l1[3])
    for k in range(1, NY):
        copy = remote(
            l2.at[y], l2.at[y], l_send.at[3 + k], l_recv.at[3 + k], {"fsdp_0": y_at(k)}
        )
        copy.start()
        losses.append(copy)
    seconds = {}
    for group in range(2):
        for h in range(2):
            for k in (1, 3, 2):
                firsts[h, k, group].wait_recv()
            for q in range(*GROUPS[group]):
                k = offsets[q]
                value = (acc[h, q] + r1[h, 0, q].astype(F32)) + (
                    r1[h, 1, q].astype(F32) + r1[h, 2, q].astype(F32)
                )
                if k == 0:
                    acc[h, q] = value
                else:
                    c2[h, k - 1] = value.astype(BF16)
                    seconds[h, k] = remote(
                        c2.at[h, k - 1],
                        r2.at[h, k - 1],
                        s2_send.at[h, k],
                        s2_recv.at[h, k],
                        second_to(h, k),
                    )
                    seconds[h, k].start()
    for copy in losses[4:]:
        copy.wait_recv()
    plane = (l2[0] + l2[1]) + (l2[2] + l2[3])
    coarse = plane.astype(BF16).astype(F32)
    at = USED_TILES
    tiles[at // PIECE, at % PIECE] = coarse
    tiles[at // PIECE, at % PIECE + 1] = plane - coarse
    for t in range(USED_TILES + 2, TILES):
        tiles[t // PIECE, t % PIECE] = jnp.zeros((8, 128), F32)
    for h in range(2):
        for k in (1, 3, 2):
            seconds[h, k].wait_recv()
        value = (acc[h, 3] + r2[h, 0].astype(F32)) + (
            r2[h, 1].astype(F32) + r2[h, 2].astype(F32)
        )
        for i in range(HALF // 8):
            for n in range(D // 128):
                t = (h * (HALF // 8) + i) * (D // 128) + n
                tiles[t // PIECE, t % PIECE] = value[8 * i : 8 * i + 8, 128 * n : 128 * n + 128]

    order = (4, 3, 5, 2, 6, 1, 7)
    thirds = []
    for k in order:
        if k in FAR:
            slot = k - FAR[0]
            far_ref[slot] = tiles[z_at(k)].reshape(PIECE * 8, 128).astype(BF16)
            src, dst = far_ref.at[slot], r3_far.at[slot]
        else:
            src, dst = tiles.at[z_at(k)], r3.at[k]
        copy = remote(src, dst, z_send.at[k], z_recv.at[k], {"dp_0": z_at(k)})
        copy.start()
        thirds.append(copy)
    for copy in thirds:
        copy.wait_recv()
    value = tiles[z]
    for k in range(1, NZ):
        if k in FAR:
            value = value + r3_far[k - FAR[0]].astype(F32).reshape(PIECE, 8, 128)
        else:
            value = value + r3[k]
    whole[c, z] = value
    spreads = {}
    for k in order:
        spreads[k] = remote(
            whole.at[c, z], whole.at[c, z], a_send.at[k], a_recv.at[k], {"dp_0": z_at(k)}
        )
        spreads[k].start()
    crossings = []
    for k in (0, 7, 1, 6, 2, 5, 3, 4):
        if k > 0:
            spreads[k].wait_recv()
        at = z_at(NZ - k) if k > 0 else z
        copy = remote(whole.at[c, at], whole.at[c, at], f_send.at[k], f_recv.at[k], partner)
        copy.start()
        crossings.append(copy)
    for copy in crossings:
        copy.wait_recv()
    for w in range(2):
        for t in range(USED_TILES):
            i, n = t // (D // 128), t % (D // 128)
            sum_ref[w, 8 * i : 8 * i + 8, 128 * n : 128 * n + 128] = whole[
                w, t // PIECE, t % PIECE
            ]
    at = USED_TILES
    total_ref[...] = whole[0, at // PIECE, at % PIECE] + whole[0, at // PIECE, at % PIECE + 1]
    for k in range(4):
        for h in range(2):
            swap(h, k).wait_send()
    for group in (early, late, crossed, firsts, seconds, spreads):
        for copy in group.values():
            copy.wait_send()
    for group in (messages, losses, thirds, crossings, [factors]):
        for copy in group:
            copy.wait_send()


def finish_kernel(sum_ref, total_ref, moved_ref, n1_ref, n2_ref, *outs):
    u1_ref, u2_ref, mean_ref, moments_ref = outs
    u1_ref[...] = (sum_ref[0] + noise_weight * n1_ref[...]) * (1.0 / SELECTED)
    u2_ref[...] = (sum_ref[1] + noise_weight * n2_ref[...]) * (1.0 / SELECTED)
    mean_ref[...] = total_ref[0:1, 0:1] * (1.0 / SELECTED)
    moments_ref[...] = moved_ref[...]


def per_device(
    features,
    conv_weight,
    vae_noise,
    flips,
    crops,
    tsteps,
    diffusion_noise,
    selected,
    w_patch,
    w_time,
    w_ada,
    w_fc1,
    w_fc2,
    w_final,
    noise_fc1,
    noise_fc2,
):
    dma = pltpu.SemaphoreType.DMA
    pixels = features.reshape(TOK, FCH)
    taps = conv_weight.transpose(0, 1, 3, 2).reshape(72, FCH)
    views = diffusion_noise.reshape(AUG, SIDE, SIDE * LC).transpose(1, 0, 2)
    grid = (NY, NX, 2, HALF, D)
    tile = (8, 128)
    vmem = pltpu.VMEM
    sums, total, moved = pl.pallas_call(
        step_kernel,
        out_shape=(
            jax.ShapeDtypeStruct((2, SHARD, D), F32),
            jax.ShapeDtypeStruct(tile, F32),
            jax.ShapeDtypeStruct((2 * SIDE, 128), F32),
        ),
        in_specs=[HBM_SPEC] * 17,
        out_specs=(VMEM_SPEC,) * 3,
        scratch_shapes=[
            pltpu.SMEM((1, AUG), jnp.int32),
            pltpu.SMEM((2, AUG), jnp.int32),
            pltpu.SMEM((1, AUG), jnp.int32),
            pltpu.SMEM((1, 1), jnp.int32),
            pltpu.SMEM((2, TSTEPS), F32),
            vmem((TOK, FCH), BF16),
            vmem((72, FCH), BF16),
            vmem((SHARD, D), BF16),
            vmem((SHARD, D), BF16),
            vmem((SIDE, 128), F32),
            vmem((SIDE * AUG, 128), F32),
            vmem((16, D), BF16),
            vmem((96, D), BF16),
            vmem((1, 128), F32),
            vmem((256, D), BF16),
            vmem((D, 3 * D), BF16),
            vmem((16, D), BF16),
            vmem((2,) + grid, BF16),
            vmem((NDP,) + tile, F32),
            vmem((NDP,) + tile, F32),
            vmem((256, 128), F32),
            vmem((AUG, 40, 128), F32),
            vmem((D, 128), F32),
            vmem((D, 128), F32),
            vmem((D, 128), F32),
            vmem((D, TOK), F32),
            vmem((D, TOK), BF16),
            vmem((TOK, D), BF16),
            vmem((D, FF), BF16),
            vmem((FF, TOK), BF16),
            vmem((FF, TOK), F32),
            vmem((16, TOK), F32),
            vmem((D, TOK), BF16),
            vmem((TOK, D), BF16),
            vmem((1, D), F32),
            vmem((4,) + tile, F32),
            vmem(grid, F32),
            vmem(grid, BF16),
            vmem(grid, BF16),
            vmem((2, 3, 4, HALF, D), BF16),
            vmem((2, 3, 4, HALF, D), BF16),
            vmem((2, 4, HALF, D), F32),
            vmem((2, 3, HALF, D), BF16),
            vmem((2, 3, HALF, D), BF16),
            vmem((NZ, PIECE) + tile, F32),
            vmem((NZ, PIECE) + tile, F32),
            vmem((2, NZ, PIECE) + tile, F32),
            vmem((2,) + tile, F32),
            vmem((NX,) + tile, F32),
            vmem((NY,) + tile, F32),
            vmem((3, PIECE * 8, 128), BF16),
            vmem((3, PIECE * 8, 128), BF16),
        ]
        + [dma((2, 4))] * 10
        + [dma((2, 8))] * 2
        + [dma((NDP,))] * 2
        + [dma((NZ,))] * 8
        + [dma((17,))],
        compiler_params=pltpu.CompilerParams(
            collective_id=0, has_side_effects=True, vmem_limit_bytes=56 << 20
        ),
        name="step",
    )(
        flips.reshape(1, AUG),
        crops.reshape(AUG, 2).T,
        tsteps.reshape(1, AUG),
        selected,
        jnp.asarray(blend_tables()),
        pixels,
        taps,
        w_fc1.T,
        w_fc2.T,
        vae_noise.reshape(SIDE, SIDE * LC),
        views.reshape(SIDE * AUG, SIDE * LC),
        w_patch,
        jnp.asarray(position_rows()),
        jnp.asarray(time_rates()),
        w_time,
        w_ada,
        w_final.T,
    )
    update_1, update_2, mean_loss, moments = pl.pallas_call(
        finish_kernel,
        out_shape=(
            jax.ShapeDtypeStruct((SHARD, D), F32),
            jax.ShapeDtypeStruct((SHARD, D), F32),
            jax.ShapeDtypeStruct((1, 1), F32),
            jax.ShapeDtypeStruct((2 * SIDE, 128), F32),
        ),
        in_specs=[VMEM_SPEC] * 5,
        out_specs=(VMEM_SPEC,) * 4,
        name="finish",
    )(sums, total, moved, noise_fc1.T, noise_fc2.T)
    return (update_1.T, update_2.T, mean_loss.reshape(()), moments.reshape(1, 1, -1))


def solution(mesh):
    split = Mesh(mesh.devices.reshape(NZ, NC, NY, NX), DP + FSDP)
    return jax.shard_map(
        per_device,
        mesh=split,
        in_specs=(
            P(FSDP, None, DP, None, None),
            P(),
            P(DP, FSDP, None),
            P(DP, FSDP, None),
            P(DP, FSDP, None, None),
            P(DP, FSDP, None),
            P(DP, FSDP, None, None),
            P(DP, FSDP),
            P(),
            P(),
            P(),
            P(None, FSDP),
            P(None, FSDP),
            P(),
            P(None, FSDP),
            P(None, FSDP),
        ),
        out_specs=(P(None, FSDP), P(None, FSDP), P(), P(DP, FSDP, None)),
        check_vma=False,
    )
```
